32 devices in a mesh: dp: 8 (over y, x, core), stream: 4 (over z).
Axes of the slice: x: 2, y: 2, z: 4, core: 2. Of those that a mesh axis runs over, the one named last changes fastest.
Arguments:
- text_input: bfloat16 [64, 512, 768], P('dp', 'stream'), may hold values from -6 to 6
- visual_features: bfloat16 [64, 49, 256], P(('dp', 'stream')), may hold values from -6 to 6
- receipt_text: int32 [64, 512], P('dp'), may hold values from 0 to 7, never falling along the last dimension, each value on 1 to 128 neighbouring positions
- receipt_visual: int32 [64, 49], P('dp'), may hold values from 0 to 7
- boxes: int32 [2, 64, 561], P(None, 'dp'), may hold values from 0 to 1023
- w_query: bfloat16 [768, 768], replicated, may hold values from -0.21875 to 0.21875
- b_query: bfloat16 [768], replicated, may hold values from -3 to 3
- w_key: bfloat16 [768, 768], replicated, may hold values from -0.21875 to 0.21875
- w_value: bfloat16 [768, 768], replicated, may hold values from -0.21875 to 0.21875
- b_value: bfloat16 [768], replicated, may hold values from -3 to 3
- w_out: bfloat16 [768, 768], replicated, may hold values from -1.75 to 1.75
- b_out: bfloat16 [768], replicated, may hold values from -3 to 3
- gain_attn: bfloat16 [768], replicated, may hold values from 0.099609375 to 1.8984375
- shift_attn: bfloat16 [768], replicated, may hold values from -2 to 2
- w_up: bfloat16 [768, 3072], replicated, may hold values from -0.21875 to 0.21875
- b_up: bfloat16 [3072], replicated, may hold values from -3 to 3
- w_down: bfloat16 [3072, 768], replicated, may hold values from -0.109375 to 0.109375
- b_down: bfloat16 [768], replicated, may hold values from -3 to 3
- gain_ffn: bfloat16 [768], replicated, may hold values from 0.099609375 to 1.8984375
- shift_ffn: bfloat16 [768], replicated, may hold values from -2 to 2
- w_visual: bfloat16 [256, 768], replicated, may hold values from -0.375 to 0.375
- b_visual: bfloat16 [768], replicated, may hold values from -3 to 3
- table_line: bfloat16 [12, 32], replicated, may hold values from -4 to 4
- table_x: bfloat16 [12, 64], replicated, may hold values from -4 to 4
- table_y: bfloat16 [12, 64], replicated, may hold values from -4 to 4
- cotangent_text: bfloat16 [64, 512, 768], P('dp', 'stream'), may hold values from -6 to 6
- cotangent_visual: bfloat16 [64, 49, 768], P(('dp', 'stream')), may hold values from -6 to 6
Outputs:
- out_text: bfloat16 [64, 512, 768], P('dp', 'stream')
- out_visual: bfloat16 [64, 49, 768], P(('dp', 'stream'))
- grad_text: float32 [64, 512, 768], P('dp', 'stream')
- grad_features: float32 [64, 49, 256], P(('dp', 'stream'))
- grad_w_query: float32 [768, 768], P(('dp', 'stream'))
- grad_b_query: float32 [768], P(('dp', 'stream'))
- grad_w_key: float32 [768, 768], P(('dp', 'stream'))
- grad_w_value: float32 [768, 768], P(('dp', 'stream'))
- grad_b_value: float32 [768], P(('dp', 'stream'))
- grad_w_out: float32 [768, 768], P(('dp', 'stream'))
- grad_b_out: float32 [768], P(('dp', 'stream'))
- grad_gain_attn: float32 [768], P(('dp', 'stream'))
- grad_shift_attn: float32 [768], P(('dp', 'stream'))
- grad_w_up: float32 [768, 3072], P(('dp', 'stream'))
- grad_b_up: float32 [3072], P(('dp', 'stream'))
- grad_w_down: float32 [3072, 768], P(('dp', 'stream'))
- grad_b_down: float32 [768], P(('dp', 'stream'))
- grad_gain_ffn: float32 [768], P(('dp', 'stream'))
- grad_shift_ffn: float32 [768], P(('dp', 'stream'))
- grad_w_visual: float32 [256, 768], P(('dp', 'stream'))
- grad_b_visual: float32 [768], P(('dp', 'stream'))
- grad_table_line: float32 [12, 32], replicated
- grad_table_x: float32 [12, 64], replicated
- grad_table_y: float32 [12, 64], replicated
The draws below stay inside these ranges and needn't reach their ends.
Inputs may be any that keep to these rules, and one draw needn't show every extreme that they name: `receipt_text`: receipt ids never fall along a row's text; each of the 8 receipts holds 1 to 128 text slots of the row, and one holds exactly 128.
All inputs are finite; a program needn't handle non-finite values.
Results may differ from the reference program's by a relative error of at most 0.015.
Values may be sent and summed in bfloat16 or wider, within the bound.
No kernel may reach another device: no remote copies, remote signals or barrier semaphores. Data moves between devices by JAX's collectives and lax.ppermute only.
A program may use at most 320 MiB of HBM per device.

```python
import math
import jax
import jax.numpy as jnp
import numpy as np
from jax import lax

D = 768
H = 12
DH = 64
FF = 3072
CV = 256
VIS = 49
NB1 = 32
NB2 = 64
NSEG = 8
ROWS = 64
TEXT = 512
SLOTS = 561


def touch_ends(drawn, stream_key, least, high):
    longest = drawn.shape.index(max(drawn.shape))
    spots = []
    for shift in (0, 1):
        where = [jax.random.randint(jax.random.fold_in(stream_key, axis), (), 0, length) for axis, length in enumerate(drawn.shape)]
        where[longest] = (where[longest] + shift) % drawn.shape[longest]
        spots.append(tuple(where))
    return drawn.at[spots[0]].set(least).at[spots[1]].set(high)


def raised(result, own_key, source, target, blocks, factor):
    owner, partner = [(jnp.arange(result.shape[position]) // (result.shape[position] // blocks)).reshape([-1 if axis == position else 1 for axis in range(result.ndim)]) for position in (source, target)]
    chosen = jax.random.permutation(own_key, blocks)[partner]
    strong = (owner == chosen) | (owner == (partner + blocks // 2) % blocks)
    return jnp.where(strong, factor * result, result)


def levels(key, extent, shards, smallest, largest):
    level = 1.0
    for position, parts in shards:
        heights = jax.random.uniform(jax.random.fold_in(jax.random.fold_in(key, 6), position), (parts,), jnp.float32, smallest / len(shards), largest / len(shards))
        level = level * jnp.repeat(jnp.exp(heights), extent[position] // parts).reshape((-1,) + (1,) * (len(extent) - 1 - position))
    return level


def length_profile(count, total, bound, slope):
    loads = [(1 << 20) // math.isqrt(rank ** slope) + 1 for rank in range(2, count + 1)]
    spare, counts = total - bound - (count - 1), [1] * (count - 1)
    while spare > 0:
        movable = [i for i in range(count - 1) if counts[i] < bound]
        whole, left = sum([loads[i] for i in movable]), spare
        for i in movable:
            extra = min(bound - counts[i], max(1, left * loads[i] // whole), spare)
            counts[i] = counts[i] + extra
            spare = spare - extra
    return np.array([bound] + counts)


def uneven_parts(own_key, number_of, total, most, skew):
    if number_of == 2:
        one = jax.random.randint(own_key, (), max(1, total - most), min(most, total - 1) + 1)
        return jnp.stack([one, total - one])
    tallies = jnp.asarray(length_profile(number_of, total, most, skew), jnp.int32)
    couples = (number_of - 1) // 2
    giver, taker = tallies[1:1 + 2 * couples:2], tallies[2:2 + 2 * couples:2]
    room = jnp.minimum(giver - 1, most - taker)
    moved = jax.random.randint(jax.random.fold_in(own_key, 1), (couples,), 0, 1 << 20) % (room + 1)
    tallies = tallies.at[1:1 + 2 * couples:2].set(giver - moved).at[2:2 + 2 * couples:2].set(taker + moved)
    return tallies[jax.random.permutation(jax.random.fold_in(own_key, 2), number_of)]


def gaussian(key, shape, deviation, most, cuts=(), held_as=jnp.bfloat16):
    factor_of = levels(key, shape, cuts, -0.22, 0.18) if cuts else 1.0
    drawn = jax.random.normal(key, shape, jnp.float32) * deviation * factor_of
    return jnp.minimum(jnp.maximum(drawn, -most), most).astype(held_as)


def noise_with(rng, shape, deviation, most, cuts, heavy, kind=jnp.bfloat16):
    entries = deviation * jax.random.normal(rng, shape, jnp.float32)
    if cuts:
        entries = entries * levels(rng, shape, cuts, -0.22, 0.18)
    return jnp.clip(raised(entries, jax.random.fold_in(rng, 3), *heavy), -most, most).astype(kind)


def setup_inputs(seed: int = 0) -> dict:
    arg_keys = jax.random.split(jax.random.key(seed), 28)
    return {
        "text_input": noise_with(arg_keys[0], (ROWS, TEXT, D), 1.0, 6.0, ((0, 8), (1, 4)), (0, 2, 8, 2.0)),
        "visual_features": gaussian(arg_keys[1], (ROWS, VIS, CV), 1.0, 6.0, ((0, 32),)),
        "receipt_text": jax.vmap(lambda own: jnp.searchsorted(jnp.cumsum(uneven_parts(own, NSEG, TEXT, TEXT // 4, 1)), jnp.arange(TEXT), side="right"))(jax.random.split(arg_keys[2], ROWS)).reshape((ROWS, TEXT)).astype(jnp.int32),
        "receipt_visual": touch_ends(jax.random.randint(arg_keys[3], (ROWS, VIS), 0, NSEG), jax.random.fold_in(arg_keys[3], 1), 0, NSEG - 1).astype(jnp.int32),
        "boxes": touch_ends(jax.random.randint(arg_keys[4], (2, ROWS, SLOTS), 0, 1024), jax.random.fold_in(arg_keys[4], 1), 0, 1023).astype(jnp.int32),
        "w_query": gaussian(arg_keys[5], (D, D), D ** -0.5, 0.21875),
        "b_query": gaussian(arg_keys[6], (D,), 0.5, 3.0),
        "w_key": gaussian(arg_keys[7], (D, D), D ** -0.5, 0.21875),
        "w_value": gaussian(arg_keys[8], (D, D), D ** -0.5, 0.21875),
        "b_value": gaussian(arg_keys[9], (D,), 0.5, 3.0),
        "w_out": gaussian(arg_keys[10], (D, D), (D // 64) ** -0.5, 1.75),
        "b_out": gaussian(arg_keys[11], (D,), 0.5, 3.0),
        "gain_attn": jnp.clip(1.0 + 0.18 * jax.random.normal(arg_keys[12], (D,), jnp.float32), 0.099609375, 1.8984375).astype(jnp.bfloat16),
        "shift_attn": gaussian(arg_keys[13], (D,), 0.3, 2.0),
        "w_up": gaussian(arg_keys[14], (D, FF), D ** -0.5, 0.21875),
        "b_up": gaussian(arg_keys[15], (FF,), 0.5, 3.0),
        "w_down": gaussian(arg_keys[16], (FF, D), FF ** -0.5, 0.109375),
        "b_down": gaussian(arg_keys[17], (D,), 0.5, 3.0),
        "gain_ffn": jnp.clip(1.0 + 0.18 * jax.random.normal(arg_keys[18], (D,), jnp.float32), 0.099609375, 1.8984375).astype(jnp.bfloat16),
        "shift_ffn": gaussian(arg_keys[19], (D,), 0.3, 2.0),
        "w_visual": gaussian(arg_keys[20], (CV, D), CV ** -0.5, 0.375),
        "b_visual": gaussian(arg_keys[21], (D,), 0.5, 3.0),
        "table_line": gaussian(arg_keys[22], (H, NB1), 1.0, 4.0),
        "table_x": gaussian(arg_keys[23], (H, NB2), 1.0, 4.0),
        "table_y": gaussian(arg_keys[24], (H, NB2), 1.0, 4.0),
        "cotangent_text": gaussian(arg_keys[25], (ROWS, TEXT, D), 1.0, 6.0, ((0, 8), (1, 4))),
        "cotangent_visual": gaussian(arg_keys[26], (ROWS, VIS, D), 1.0, 6.0, ((0, 32),)),
    }


reach_line = 128
reach_plane = 256

@jax.custom_vjp
def low(v):
    return lax.optimization_barrier(v.astype(jnp.bfloat16)).astype(jnp.float32)

@jax.custom_vjp
def low_back(v):
    return v

def low_keep(v):
    return (low(v), None)

def low_pass(kept, grad):
    return (grad,)

def back_keep(v):
    return (v, None)

def back_low(kept, grad):
    return (low(grad),)
low.defvjp(low_keep, low_pass)
low_back.defvjp(back_keep, back_low)

def thresholds(half, reach):
    exact = half // 2
    steps = half - exact
    return [int(math.floor(exact * (reach / exact) ** (power / steps) + 0.5)) for power in range(1, steps)]

def bucket(diff, count, reach):
    half = count // 2
    exact = half // 2
    dist = jnp.abs(diff)
    passed = jnp.zeros_like(dist)
    for limit in thresholds(half, reach):
        passed = passed + (dist >= limit).astype(jnp.int32)
    inner = jnp.where(dist < exact, dist, exact + passed)
    return inner + half * (diff > 0).astype(jnp.int32)

def highest(left, right):
    return jnp.einsum('...i,ij->...j', left, right, precision=lax.Precision.HIGHEST)

def layer_norm(values, gain, shift):
    centred = values - lax.optimization_barrier(jnp.mean(values, axis=-1, keepdims=True))
    spread = lax.optimization_barrier(jnp.mean(centred * centred, axis=-1, keepdims=True))
    return centred * lax.rsqrt(spread + 1e-05) * gain + shift

def run_block(params, text_rows, feature_rows, receipt_rows, receipt_visual_rows, box_rows):
    w_query, b_query, w_key, w_value, b_value, w_out, b_out, gain_attn, shift_attn, w_up, b_up, w_down, b_down, gain_ffn, shift_ffn, w_visual, b_visual, table_line, table_x, table_y = params
    visual = low_back(highest(feature_rows, w_visual) + b_visual)
    stream_in = jnp.concatenate([text_rows, visual], axis=1)
    entered = low(stream_in)
    query = low(low_back(highest(entered, w_query) + b_query))
    keys = low(low_back(highest(entered, w_key)))
    values = low(low_back(highest(entered, w_value) + b_value))
    batch = stream_in.shape[0]
    slots = stream_in.shape[1]

    def split_heads(array):
        return array.reshape(batch, slots, H, DH)
    scale = 1.0 / math.sqrt(DH)
    raw = jnp.einsum('bqhd,bkhd->bhqk', split_heads(query), split_heads(keys), precision=lax.Precision.HIGHEST) * scale
    positions = jnp.concatenate([jnp.arange(TEXT, dtype=jnp.int32), jnp.arange(VIS, dtype=jnp.int32)])
    line = bucket(positions[None, :] - positions[:, None], NB1, reach_line)
    across = bucket(box_rows[0][:, None, :] - box_rows[0][:, :, None], NB2, reach_plane)
    down = bucket(box_rows[1][:, None, :] - box_rows[1][:, :, None], NB2, reach_plane)
    bias = jnp.take(table_line, line, axis=1)[None]
    bias = bias + jnp.moveaxis(jnp.take(table_x, across, axis=1), 0, 1)
    bias = bias + jnp.moveaxis(jnp.take(table_y, down, axis=1), 0, 1)
    scores = low_back(raw + bias)
    receipts = jnp.concatenate([receipt_rows, receipt_visual_rows], axis=1)
    same = (receipts[:, :, None] == receipts[:, None, :])[:, None]
    probs = jax.nn.softmax(jnp.where(same, scores, -1e+30), axis=-1)
    shares = low(probs)
    context = jnp.einsum('bhqk,bkhd->bqhd', shares, split_heads(values), precision=lax.Precision.HIGHEST).reshape(batch, slots, D)
    context = low(low_back(context))
    attended = low_back(highest(context, w_out) + b_out)
    norm_one = layer_norm(stream_in + attended, gain_attn, shift_attn)
    inner_up = low_back(highest(low(norm_one), w_up) + b_up)
    active = low(jax.nn.gelu(inner_up, approximate=False))
    branch = low_back(highest(active, w_down) + b_down)
    outcome = layer_norm(norm_one + branch, gain_ffn, shift_ffn)
    return (outcome[:, :TEXT], outcome[:, TEXT:])

def reference(text_input, visual_features, receipt_text, receipt_visual, boxes, w_query, b_query, w_key, w_value, b_value, w_out, b_out, gain_attn, shift_attn, w_up, b_up, w_down, b_down, gain_ffn, shift_ffn, w_visual, b_visual, table_line, table_x, table_y, cotangent_text, cotangent_visual):
    params = tuple((item.astype(jnp.float32) for item in (w_query, b_query, w_key, w_value, b_value, w_out, b_out, gain_attn, shift_attn, w_up, b_up, w_down, b_down, gain_ffn, shift_ffn, w_visual, b_visual, table_line, table_x, table_y)))
    checked = jax.checkpoint(run_block)
    receipt_blocks = receipt_text.reshape(-1, 4, TEXT)
    visual_receipt_blocks = receipt_visual.reshape(-1, 4, VIS)
    box_blocks = jnp.moveaxis(boxes.reshape(2, -1, 4, SLOTS), 1, 0)

    def forward(weights, text_all, features_all):
        blocks = (text_all.reshape(-1, 4, TEXT, D), features_all.reshape(-1, 4, VIS, CV), receipt_blocks, visual_receipt_blocks, box_blocks)
        text_out, visual_out = lax.map(lambda block: checked(weights, *block), blocks)
        return (text_out.reshape(ROWS, TEXT, D), visual_out.reshape(ROWS, VIS, D))
    outputs, pullback = jax.vjp(forward, params, text_input.astype(jnp.float32), visual_features.astype(jnp.float32))
    grads, grad_text, grad_features = pullback((cotangent_text.astype(jnp.float32), cotangent_visual.astype(jnp.float32)))
    grad_w_query, grad_b_query, grad_w_key, grad_w_value, grad_b_value, grad_w_out, grad_b_out, grad_gain_attn, grad_shift_attn, grad_w_up, grad_b_up, grad_w_down, grad_b_down, grad_gain_ffn, grad_shift_ffn, grad_w_visual, grad_b_visual, grad_table_line, grad_table_x, grad_table_y = grads
    return (outputs[0].astype(jnp.bfloat16), outputs[1].astype(jnp.bfloat16), grad_text, grad_features, grad_w_query, grad_b_query, grad_w_key, grad_w_value, grad_b_value, grad_w_out, grad_b_out, grad_gain_attn, grad_shift_attn, grad_w_up, grad_b_up, grad_w_down, grad_b_down, grad_gain_ffn, grad_shift_ffn, grad_w_visual, grad_b_visual, grad_table_line, grad_table_x, grad_table_y)
```

```python
import math

import jax, jax.numpy as jnp
from jax import lax
from jax.experimental import pallas as pl
from jax.experimental.pallas import tpu as pltpu
from jax.sharding import PartitionSpec as P

HEADS = 12
RECEIPTS = 8
SPAN = 576
BINS = 160
NONE = -1e30


def thresholds(half, reach):
    exact = half // 2
    steps = half - exact
    return [
        int(math.floor(exact * (reach / exact) ** (power / steps) + 0.5))
        for power in range(1, steps)
    ]


def bucket(diff, count, reach):
    half = count // 2
    exact = half // 2
    dist = jnp.abs(diff)
    passed = jnp.where(diff > 0, half, 0)
    for limit in thresholds(half, reach):
        passed = passed + jnp.where(dist >= limit, 1, 0)
    return passed + jnp.minimum(dist, exact)


def dot(a, b, ca, cb):
    return lax.dot_general(a, b, (((ca,), (cb,)), ((), ())), preferred_element_type=jnp.float32)


def window(bounds_ref, receipt):
    base = pl.program_id(0) * 16
    first = bounds_ref[base + receipt]
    last = bounds_ref[base + receipt + 1]
    return first, last, (first // 16) * 16


def marks(receipt, first, rows, lanes, col_ref, row_ref, line_s, x_s, y_s):
    at_q = pl.multiple_of(jnp.minimum(first, SPAN - rows), 16)
    at_k = pl.multiple_of(jnp.minimum(first, SPAN - lanes), 16)
    col = col_ref[0, pl.ds(at_q, rows), :]
    row = pltpu.roll(row_ref[0], lax.rem(640 - at_k, 640), 1)[:, :lanes]
    mine = col[:, 3:4] == receipt
    shape = (rows, lanes)

    def gap(n):
        return jnp.broadcast_to(row[n : n + 1, :], shape) - jnp.broadcast_to(col[:, n : n + 1], shape)

    same = jnp.logical_and(
        jnp.broadcast_to(row[3:4, :], shape) == receipt,
        jnp.broadcast_to(col[:, 3:4], shape) == receipt,
    )
    line = jnp.where(same, bucket(gap(0), 32, 128), 32)
    across = bucket(gap(1), 64, 256)
    down = bucket(gap(2), 64, 256) + 64
    for c in range(lanes // 128):
        piece = slice(128 * c, 128 * (c + 1))
        line_s[c, :rows] = line[:, piece]
        x_s[c, :rows] = across[:, piece]
        y_s[c, :rows] = down[:, piece]
    return at_q, at_k, mine


def bias_of(pair, rows, lanes, plane_ref, lines_ref, line_s, x_s, y_s):
    halves = []
    for h in range(2):
        plane = jnp.broadcast_to(plane_ref[pl.ds(2 * pair + h, 1), :], (rows, 128))
        lines = jnp.broadcast_to(lines_ref[pl.ds(2 * pair + h, 1), :], (rows, 128))
        cols = []
        for c in range(lanes // 128):
            def look(table, index):
                return jnp.take_along_axis(table, index[c, :rows], axis=1, mode="promise_in_bounds")
            cols.append(look(plane, x_s) + look(plane, y_s) + look(lines, line_s))
        halves.append(cols[0] if len(cols) == 1 else jnp.concatenate(cols, axis=1))
    return jnp.concatenate(halves, axis=0)


def split_pair(value, scale=1.0):
    lane = lax.broadcasted_iota(jnp.int32, value.shape, 1)
    full = value.astype(jnp.float32) * scale
    low = jnp.where(lane < 64, full, 0.0).astype(value.dtype)
    high = jnp.where(lane < 64, 0.0, full).astype(value.dtype)
    return jnp.concatenate([low, high], axis=0)


def softmax(scores):
    expo = jnp.exp(scores - jnp.max(scores, axis=1, keepdims=True))
    return expo * (1.0 / jnp.sum(expo, axis=1, keepdims=True))


def by_size(bounds_ref, run):
    def step(receipt, carry):
        first, last, start = window(bounds_ref, receipt)
        span = last - start
        for low, rows, lanes in ((0, 64, 128), (64, 128, 128), (128, 192, 256)):
            inside = span > low
            if rows < 192:
                inside = jnp.logical_and(inside, span <= rows)

            @pl.when(inside)
            def _(rows=rows, lanes=lanes):
                run(receipt, first, last, start, rows, lanes)

        return carry

    lax.fori_loop(0, RECEIPTS, step, 0)


def forward_kernel(bounds_ref, q_ref, k_ref, v_ref, col_ref, row_ref, plane_ref, lines_ref, out_ref, line_s, x_s, y_s):
    out_ref[...] = jnp.zeros_like(out_ref)

    def run(receipt, first, last, start, rows, lanes):
        at_q, at_k, mine = marks(receipt, start, rows, lanes, col_ref, row_ref, line_s, x_s, y_s)

        def pair_step(pair, carry):
            at = pl.multiple_of(pair * 128, 128)
            q = split_pair(q_ref[0, pl.ds(at_q, rows), pl.ds(at, 128)], 0.125)
            k = k_ref[0, pl.ds(at_k, lanes), pl.ds(at, 128)]
            v = split_pair(v_ref[0, pl.ds(at_k, lanes), pl.ds(at, 128)])
            scores = dot(q, k, 1, 1) + bias_of(pair, rows, lanes, plane_ref, lines_ref, line_s, x_s, y_s)
            shares = softmax(scores).astype(jnp.bfloat16)
            shares = jnp.concatenate([shares[:rows], shares[rows:]], axis=1)
            context = dot(shares, v, 1, 0)
            here = (0, pl.ds(at_q, rows), pl.ds(at, 128))
            out_ref[here] = jnp.where(mine, context, out_ref[here].astype(jnp.float32)).astype(jnp.bfloat16)
            return carry

        lax.fori_loop(0, HEADS // 2, pair_step, 0)

    by_size(bounds_ref, run)


def backward_kernel(
    bounds_ref, q_ref, k_ref, v_ref, g_ref, col_ref, row_ref, plane_ref, lines_ref,
    dq_ref, dk_ref, dv_ref, bins_ref, line_s, x_s, y_s, ds_s,
):
    dq_ref[...] = jnp.zeros_like(dq_ref)
    dk_ref[...] = jnp.zeros_like(dk_ref)
    dv_ref[...] = jnp.zeros_like(dv_ref)

    @pl.when(pl.program_id(0) == 0)
    def _():
        bins_ref[...] = jnp.zeros_like(bins_ref)
        ds_s[...] = jnp.zeros_like(ds_s)

    def run(receipt, first, last, start, rows, lanes):
        at_q, at_k, mine = marks(receipt, start, rows, lanes, col_ref, row_ref, line_s, x_s, y_s)
        mine_k = col_ref[0, pl.ds(at_k, lanes), :][:, 3:4] == receipt

        def pair_step(pair, carry):
            at = pl.multiple_of(pair * 128, 128)
            rows_at = (0, pl.ds(at_q, rows), pl.ds(at, 128))
            keys_at = (0, pl.ds(at_k, lanes), pl.ds(at, 128))
            q = split_pair(q_ref[rows_at], 0.125)
            k = k_ref[keys_at]
            v = v_ref[keys_at]
            g = jnp.where(mine, g_ref[rows_at].astype(jnp.float32), 0.0).astype(jnp.bfloat16)
            g = split_pair(g)
            scores = dot(q, k, 1, 1) + bias_of(pair, rows, lanes, plane_ref, lines_ref, line_s, x_s, y_s)
            probs = softmax(scores)
            shares = probs.astype(jnp.bfloat16)
            gp = dot(g, v, 1, 1)
            inner = jnp.sum(probs * gp, axis=1, keepdims=True)
            gs = (probs * (gp - inner)).astype(jnp.bfloat16)
            wide = gs.astype(jnp.float32)
            for h in range(2):
                for c in range(0, lanes, 128):
                    ds_s[c // 128, pl.ds(2 * pair + h, rows, stride=16), :] = wide[h * rows : (h + 1) * rows, c : c + 128]
            dv = dot(shares, g, 0, 0)
            dk = dot(gs, q, 0, 0)
            dq = dot(jnp.concatenate([gs[:rows], gs[rows:]], axis=1), split_pair(k, 0.125), 1, 0)

            def put(ref, where, mask, value):
                ref[where] = jnp.where(mask, value, ref[where].astype(jnp.float32)).astype(jnp.bfloat16)

            put(dq_ref, rows_at, mine, dq)
            put(dk_ref, keys_at, mine_k, dk)
            put(dv_ref, keys_at, mine_k, dv)
            return carry

        lax.fori_loop(0, HEADS // 2, pair_step, 0)
        group = 2
        level = lax.broadcasted_iota(jnp.int32, (BINS, 128), 0)

        def bin_step(step, total):
            hots, terms = [], []
            for n in range(group):
                i = step * group + n
                for c in range(lanes // 128):
                    def spread(s, count):
                        return jnp.broadcast_to(s[c, pl.ds(i, 1), :], (count, 128))
                    index = jnp.concatenate([spread(x_s, 64), spread(y_s, 64), spread(line_s, 32) + 128], axis=0)
                    hots.append(jnp.where(level == index, 1.0, 0.0).astype(jnp.bfloat16))
                    terms.append(ds_s[c, pl.ds(pl.multiple_of(i * 16, 16), 16), :].astype(jnp.bfloat16))
            return total + dot(jnp.concatenate(hots, axis=1), jnp.concatenate(terms, axis=1), 1, 1)

        total = lax.fori_loop(
            (first - at_q) // group, pl.cdiv(last - at_q, group), bin_step, jnp.zeros((BINS, 16), jnp.float32)
        )
        bins_ref[:, :16] += total

    by_size(bounds_ref, run)


def attend(bounds, q, k, v, col, row, plane, lines):
    rows, span, width = q.shape
    wide = pl.BlockSpec((1, span, width), lambda i, *_: (i, 0, 0))
    spec = pltpu.PrefetchScalarGridSpec(
        num_scalar_prefetch=1,
        grid=(rows,),
        in_specs=[wide, wide, wide,
            pl.BlockSpec((1, span, 128), lambda i, *_: (i, 0, 0)),
            pl.BlockSpec((1, 8, 640), lambda i, *_: (i, 0, 0)),
            pl.BlockSpec((HEADS, 128), lambda i, *_: (0, 0)),
            pl.BlockSpec((HEADS, 128), lambda i, *_: (0, 0)),
        ],
        out_specs=wide,
        scratch_shapes=[pltpu.VMEM((2, 192, 128), jnp.int32)] * 3,
    )
    return pl.pallas_call(
        forward_kernel,
        grid_spec=spec,
        out_shape=jax.ShapeDtypeStruct(q.shape, q.dtype),
        compiler_params=pltpu.CompilerParams(vmem_limit_bytes=40 * 1024 * 1024),
        name="attend",
    )(bounds, q, k, v, col, row, plane, lines)


def attend_back(bounds, q, k, v, g, col, row, plane, lines):
    rows, span, width = q.shape
    wide = pl.BlockSpec((1, span, width), lambda i, *_: (i, 0, 0))
    spec = pltpu.PrefetchScalarGridSpec(
        num_scalar_prefetch=1,
        grid=(rows,),
        in_specs=[wide, wide, wide, wide,
            pl.BlockSpec((1, span, 128), lambda i, *_: (i, 0, 0)),
            pl.BlockSpec((1, 8, 640), lambda i, *_: (i, 0, 0)),
            pl.BlockSpec((HEADS, 128), lambda i, *_: (0, 0)),
            pl.BlockSpec((HEADS, 128), lambda i, *_: (0, 0)),
        ],
        out_specs=[wide, wide, wide, pl.BlockSpec((BINS, 128), lambda i, *_: (0, 0))],
        scratch_shapes=[pltpu.VMEM((2, 192, 128), jnp.int32)] * 3 + [pltpu.VMEM((2, 192 * 16, 128), jnp.float32)],
    )
    same = jax.ShapeDtypeStruct(q.shape, q.dtype)
    return pl.pallas_call(
        backward_kernel,
        grid_spec=spec,
        out_shape=[same, same, same, jax.ShapeDtypeStruct((BINS, 128), jnp.float32)],
        compiler_params=pltpu.CompilerParams(vmem_limit_bytes=48 * 1024 * 1024),
        name="attend_back",
    )(bounds, q, k, v, g, col, row, plane, lines)


DP = "dp"
STREAM = "stream"


def layer_norm(values, gain, shift):
    centred = values - jnp.mean(values, axis=-1, keepdims=True)
    spread = jnp.mean(centred * centred, axis=-1, keepdims=True)
    return centred * lax.rsqrt(spread + 1e-05) * gain + shift


def gelu_exact(values):
    return jax.nn.gelu(values, approximate=False)


def swap(value, axis, bit):
    count = lax.axis_size(axis)
    return lax.ppermute(value, axis, [(i, i ^ bit) for i in range(count)])


def bits_of(axis):
    count = lax.axis_size(axis)
    return [1 << n for n in range(count.bit_length() - 1)]


def stages(flip):
    core, *chips = bits_of(DP)
    if flip:
        chips = chips[::-1]
    return [(DP, core)] + [(DP, bit) for bit in chips] + [(STREAM, bit) for bit in bits_of(STREAM)]


def scatter_sum(value, flip):
    names = [(axis, bit) for axis in (DP, STREAM) for bit in bits_of(axis)[::-1]]
    value = value.reshape((2,) * len(names) + value.shape[1:])
    for stage in stages(flip):
        axis, bit = stage
        dim = names.index(stage)
        side = (lax.axis_index(axis) // bit) % 2
        given = lax.dynamic_index_in_dim(value, 1 - side, dim, keepdims=False)
        kept = lax.dynamic_index_in_dim(value, side, dim, keepdims=False)
        value = kept.astype(jnp.float32) + swap(given.astype(jnp.bfloat16), axis, bit).astype(jnp.float32)
        names.pop(dim)
    return value


def sum_all(value):
    for axis, bit in stages(False):
        value = value + swap(value, axis, bit)
    return value


def by_rows(value):
    count = lax.axis_size(STREAM)
    place = lax.axis_index(STREAM)
    block = value.shape[0] // count
    parts = [lax.dynamic_slice_in_dim(value, place * block, block, 0)]
    for shift in range(1, count):
        sent = lax.dynamic_slice_in_dim(value, (place + shift) % count * block, block, 0)
        parts.append(lax.ppermute(sent, STREAM, [(i, (i + shift) % count) for i in range(count)]))
    stacked = jnp.stack(parts)
    order = (place - jnp.arange(count)) % count
    ordered = [lax.dynamic_index_in_dim(stacked, order[n], 0, keepdims=False) for n in range(count)]
    return jnp.concatenate(ordered, axis=1)


def by_slots(value):
    return lax.all_to_all(value, STREAM, 1, 0, tiled=True)


def per_device(
    text_input,
    visual_features,
    receipt_text,
    receipt_visual,
    boxes,
    w_query,
    b_query,
    w_key,
    w_value,
    b_value,
    w_out,
    b_out,
    gain_attn,
    shift_attn,
    w_up,
    b_up,
    w_down,
    b_down,
    gain_ffn,
    shift_ffn,
    w_visual,
    b_visual,
    table_line,
    table_x,
    table_y,
    cotangent_text,
    cotangent_visual,
):
    floating = jnp.float32
    narrow = jnp.bfloat16
    width = text_input.shape[-1]
    rows, visual, channels = visual_features.shape
    text = receipt_text.shape[1]
    slots = text + visual
    world = lax.axis_size(DP) * lax.axis_size(STREAM)
    place = lax.axis_index(STREAM)
    first_row = place * rows

    text_rows = lax.all_to_all(text_input, STREAM, 0, 1, tiled=True)
    kept = lax.optimization_barrier((text_rows, cotangent_text))
    text_rows = kept[0]
    cotangent_rows = lax.all_to_all(kept[1], STREAM, 0, 1, tiled=True)

    def pad(value, fill=0):
        extra = SPAN - value.shape[1]
        return jnp.pad(value, ((0, 0), (0, extra)) + ((0, 0),) * (value.ndim - 2), constant_values=fill)

    seg_text = lax.dynamic_slice_in_dim(receipt_text, first_row, rows, 0)
    seg_visual = lax.dynamic_slice_in_dim(receipt_visual, first_row, rows, 0)
    box = lax.dynamic_slice_in_dim(boxes, first_row, rows, 1)
    seg = pad(jnp.concatenate([seg_text, seg_visual], axis=1), RECEIPTS)
    index = jnp.arange(SPAN, dtype=jnp.int32)
    ahead = (seg[:, None, :] < seg[:, :, None]) | (
        (seg[:, None, :] == seg[:, :, None]) & (index[None, :] < index[:, None])[None]
    )
    target = jnp.sum(ahead.astype(jnp.int32), axis=2)
    moved = target[:, None, :] == index[None, :, None]
    position = jnp.where(index < text, index, index - text)
    facts = jnp.stack(
        [jnp.broadcast_to(position, seg.shape), pad(box[0]), pad(box[1]), seg], axis=1
    )
    facts = jnp.sum(jnp.where(moved[:, None], facts[:, :, None, :], 0), axis=3)
    col = jnp.pad(jnp.swapaxes(facts, 1, 2), ((0, 0), (0, 0), (0, 124)))
    row = jnp.pad(facts, ((0, 0), (0, 4), (0, 640 - SPAN)), constant_values=RECEIPTS)
    bounds = jnp.sum(
        (seg[:, None, :] < jnp.arange(16, dtype=jnp.int32)[None, :, None]).astype(jnp.int32), axis=2
    ).reshape(-1)
    plane = jnp.concatenate([table_x, table_y], axis=1).astype(floating)
    lines = jnp.pad(table_line.astype(floating), ((0, 0), (0, 96)), constant_values=NONE)

    moving = moved.astype(narrow)

    def sort(value):
        return jnp.einsum("rps,rsd->rpd", moving[:, :, : value.shape[1]], value, preferred_element_type=floating)

    def unsort(value):
        return jnp.einsum("rps,rpd->rsd", moving, value, preferred_element_type=floating)

    features = jnp.einsum(
        "rpv,rvc->rpc", moving[:, :, text:slots], visual_features, preferred_element_type=floating
    ).astype(narrow)
    is_visual = jnp.sum(moving[:, :, text:slots].astype(floating), axis=2)[:, :, None]
    features_flat = features.reshape(-1, channels)
    visual_pre = jnp.einsum("rpc,cd->rpd", features, w_visual, preferred_element_type=floating)
    visual_pre = (visual_pre + b_visual.astype(floating)) * is_visual
    stream_in = (sort(text_rows) + visual_pre).reshape(-1, width)
    entered = stream_in.astype(narrow)
    query = (
        jnp.dot(entered, w_query, preferred_element_type=floating) + b_query.astype(floating)
    ).astype(narrow)
    key = jnp.dot(entered, w_key, preferred_element_type=floating).astype(narrow)
    value = (
        jnp.dot(entered, w_value, preferred_element_type=floating) + b_value.astype(floating)
    ).astype(narrow)

    def rowwise(array):
        return array.reshape(rows, SPAN, width)

    context = attend(bounds, rowwise(query), rowwise(key), rowwise(value), col, row, plane, lines)
    context = context.reshape(-1, width)
    grad_outcome = sort(jnp.concatenate([cotangent_rows, cotangent_visual], axis=1)).reshape(-1, width)

    attended = jnp.dot(context, w_out, preferred_element_type=floating) + b_out.astype(floating)
    norm_one, back_one = jax.vjp(
        layer_norm, stream_in + attended, gain_attn.astype(floating), shift_attn.astype(floating)
    )
    hidden = norm_one.astype(narrow)
    inner_up = jnp.dot(hidden, w_up, preferred_element_type=floating) + b_up.astype(floating)
    active, back_gelu = jax.vjp(gelu_exact, inner_up)
    active_low = active.astype(narrow)
    branch = jnp.dot(active_low, w_down, preferred_element_type=floating) + b_down.astype(floating)
    outcome, back_two = jax.vjp(
        layer_norm, norm_one + branch, gain_ffn.astype(floating), shift_ffn.astype(floating)
    )
    out_rows = unsort(rowwise(outcome.astype(narrow))).astype(narrow)
    out_text = by_slots(out_rows[:, :text])
    out_visual = out_rows[:, text:slots]

    grad_top, grad_gain_ffn, grad_shift_ffn = back_two(grad_outcome)
    grad_branch = grad_top.astype(narrow)
    grad_b_down = jnp.sum(grad_branch, axis=0, dtype=floating)
    grad_w_down = jnp.einsum("tf,td->fd", active_low, grad_branch, preferred_element_type=floating)
    down_sum = scatter_sum(grad_w_down.reshape(world, -1, width), False)
    grad_active = jnp.einsum("td,fd->tf", grad_branch, w_down, preferred_element_type=floating)
    grad_inner = back_gelu(grad_active)[0].astype(narrow)
    grad_b_up = jnp.sum(grad_inner, axis=0, dtype=floating)
    grad_w_up = jnp.einsum("td,tf->df", hidden, grad_inner, preferred_element_type=floating)
    up_sum = scatter_sum(grad_w_up.reshape(world, -1, w_up.shape[1]), True)
    grad_norm = grad_top + jnp.einsum("tf,df->td", grad_inner, w_up, preferred_element_type=floating)
    grad_mid, grad_gain_attn, grad_shift_attn = back_one(grad_norm)
    grad_attended = grad_mid.astype(narrow)
    grad_b_out = jnp.sum(grad_attended, axis=0, dtype=floating)
    grad_w_out = jnp.einsum("td,te->de", context, grad_attended, preferred_element_type=floating)
    out_sum = scatter_sum(grad_w_out.reshape(world, -1, width), False)
    grad_context = jnp.einsum("te,de->td", grad_attended, w_out, preferred_element_type=floating).astype(narrow)

    grad_query, grad_key, grad_value, bins = attend_back(
        bounds, rowwise(query), rowwise(key), rowwise(value), rowwise(grad_context), col, row, plane, lines
    )
    grad_query, grad_key, grad_value = (part.reshape(-1, width) for part in (grad_query, grad_key, grad_value))
    grad_stream = grad_mid + jnp.einsum("te,de->td", grad_query, w_query, preferred_element_type=floating)
    grad_stream = grad_stream + jnp.einsum("te,de->td", grad_key, w_key, preferred_element_type=floating)
    grad_stream = grad_stream + jnp.einsum("te,de->td", grad_value, w_value, preferred_element_type=floating)
    grad_low = grad_stream.astype(narrow)
    back_rows = unsort(rowwise(grad_low)).astype(narrow)
    grad_text = by_slots(back_rows[:, :text]).astype(floating)
    grad_visual = back_rows[:, text:slots]
    grad_w_query = jnp.einsum("td,te->de", entered, grad_query, preferred_element_type=floating)
    grad_b_query = jnp.sum(grad_query, axis=0, dtype=floating)
    grad_w_key = jnp.einsum("td,te->de", entered, grad_key, preferred_element_type=floating)
    grad_w_value = jnp.einsum("td,te->de", entered, grad_value, preferred_element_type=floating)
    grad_b_value = jnp.sum(grad_value, axis=0, dtype=floating)
    grad_w_visual = jnp.einsum("rvc,rvd->cd", visual_features, grad_visual, preferred_element_type=floating)
    grad_b_visual = jnp.sum(grad_visual, axis=(0, 1), dtype=floating)
    grad_features = jnp.einsum("rvd,cd->rvc", grad_visual, w_visual, preferred_element_type=floating)
    first = scatter_sum(
        jnp.concatenate([part.reshape(world, -1, width) for part in (grad_w_query, grad_w_visual)], axis=1), False
    )
    second = scatter_sum(
        jnp.concatenate([part.reshape(world, -1, width) for part in (grad_w_key, grad_w_value)], axis=1), True
    )
    step = width // world
    small = sum_all(
        jnp.concatenate(
            [
                jnp.stack(
                    [
                        grad_b_query, grad_b_value, grad_b_out, grad_gain_attn, grad_shift_attn,
                        grad_b_down, grad_gain_ffn, grad_shift_ffn, grad_b_visual,
                    ]
                ),
                grad_b_up.reshape(-1, width),
                jnp.pad(bins.reshape(-1), (0, -bins.size % width)).reshape(-1, width),
            ],
            axis=0,
        )
    )
    device = lax.axis_index(DP) * lax.axis_size(STREAM) + place
    mine = lax.dynamic_slice_in_dim(small[:9], device * step, step, 1)
    up_step = w_up.shape[1] // world
    ups = small[9 : 9 + w_up.shape[1] // width].reshape(-1)
    bins = small[9 + w_up.shape[1] // width :].reshape(-1)[: bins.size].reshape(bins.shape)[:, :HEADS].T
    return (
        out_text,
        out_visual,
        grad_text,
        grad_features,
        first[:step],
        mine[0],
        second[:step],
        second[step:],
        mine[1],
        out_sum,
        mine[2],
        mine[3],
        mine[4],
        up_sum,
        lax.dynamic_slice_in_dim(ups, device * up_step, up_step, 0),
        down_sum,
        mine[5],
        mine[6],
        mine[7],
        first[step:],
        mine[8],
        bins[:, 128:160],
        bins[:, :64],
        bins[:, 64:128],
    )


def solution(mesh):
    placed = (
        P("dp", "stream", None),
        P(("dp", "stream"), None, None),
        P("dp", None),
        P("dp", None),
        P(None, "dp", None),
        P(),
        P(),
        P(),
        P(),
        P(),
        P(),
        P(),
        P(),
        P(),
        P(),
        P(),
        P(),
        P(),
        P(),
        P(),
        P(),
        P(),
        P(),
        P(),
        P(),
        P("dp", "stream", None),
        P(("dp", "stream"), None, None),
    )
    return jax.shard_map(
        per_device,
        mesh=mesh,
        in_specs=placed,
        out_specs=(
            P("dp", "stream", None),
            P(("dp", "stream"), None, None),
            P("dp", "stream", None),
            P(("dp", "stream"), None, None),
            P(("dp", "stream"), None),
            P(("dp", "stream")),
            P(("dp", "stream"), None),
            P(("dp", "stream"), None),
            P(("dp", "stream")),
            P(("dp", "stream"), None),
            P(("dp", "stream")),
            P(("dp", "stream")),
            P(("dp", "stream")),
            P(("dp", "stream"), None),
            P(("dp", "stream")),
            P(("dp", "stream"), None),
            P(("dp", "stream")),
            P(("dp", "stream")),
            P(("dp", "stream")),
            P(("dp", "stream"), None),
            P(("dp", "stream")),
            P(),
            P(),
            P(),
        ),
        check_vma=False,
    )
```

```python
import functools
import math

import jax, jax.numpy as jnp
from jax import lax
from jax.experimental import pallas as pl
from jax.experimental.pallas import tpu as pltpu
from jax.sharding import PartitionSpec as P

HEADS = 12
RECEIPTS = 8
SPAN = 576
BINS = 160
NONE = -1e30
TALL = 192
WIDE = 256


def thresholds(half, reach):
    exact = half // 2
    steps = half - exact
    return [
        int(math.floor(exact * (reach / exact) ** (power / steps) + 0.5))
        for power in range(1, steps)
    ]


def bucket(diff, count, reach):
    half = count // 2
    exact = half // 2
    dist = jnp.abs(diff)
    passed = jnp.where(diff > 0, half, 0)
    for limit in thresholds(half, reach):
        passed = passed + jnp.where(dist >= limit, 1, 0)
    return passed + jnp.minimum(dist, exact)


def dot(a, b, ca, cb):
    return lax.dot_general(a, b, (((ca,), (cb,)), ((), ())), preferred_element_type=jnp.float32)


def by_size(bounds_ref, run, offset=0):
    step = pl.program_id(0) + offset * RECEIPTS
    receipt = lax.rem(step, RECEIPTS)
    base = step // RECEIPTS * 16 + receipt
    first = bounds_ref[base]
    last = bounds_ref[base + 1]
    start = first // 16 * 16
    for low, tall, wide in ((0, 64, 128), (64, 128, 128), (128, 192, 256)):
        inside = last - start > low
        if tall < TALL:
            inside = jnp.logical_and(inside, last - start <= tall)

        @pl.when(inside)
        def _(tall=tall, wide=wide):
            at_k = pl.multiple_of(jnp.minimum(start, SPAN - tall), 16)
            at_q = pl.multiple_of(jnp.minimum(start, SPAN - wide), 16)
            run(receipt, first - at_k, last - at_k, at_k, at_q, tall, wide)


def bias_kernel(bounds_ref, col_ref, row_ref, plane_ref, lines_ref, bias_ref, index_ref):
    def run(receipt, low, high, at_k, at_q, tall, wide):
        row = pltpu.roll(row_ref[0], lax.rem(640 - at_q, 640), 1)[:, :wide]
        height = 16

        def step(n, carry):
            at = pl.multiple_of(n * height, height)
            col = col_ref[0, pl.ds(pl.multiple_of(at_k + at, 16), height), :]
            shape = (height, 128)
            for c in range(wide // 128):
                lanes = slice(128 * c, 128 * (c + 1))

                def spread(r):
                    return (jnp.broadcast_to(col[:, r : r + 1], shape), jnp.broadcast_to(row[r : r + 1, lanes], shape))

                def gap(r):
                    key, query = spread(r)
                    return key - query

                key, query = spread(3)
                same = jnp.logical_and(key == receipt, query == receipt)
                line = jnp.where(same, bucket(gap(0), 32, 128), 32)
                across = bucket(gap(1), 64, 256)
                down = bucket(gap(2), 64, 256) + 64
                index_ref[0, pl.ds(at, height), lanes] = across + down * 256 + line * 65536
                for h in range(HEADS):
                    def look(ref, index):
                        table = jnp.broadcast_to(ref[h : h + 1, :], shape)
                        return jnp.take_along_axis(table, index, axis=1, mode="promise_in_bounds")

                    bias_ref[0, h, pl.ds(at, height), lanes] = (
                        look(plane_ref, across) + look(plane_ref, down) + look(lines_ref, line)
                    )
            return carry

        lax.fori_loop(0, tall // height, step, 0)

    by_size(bounds_ref, run)


def split_pair(value, scale=1.0):
    lane = lax.broadcasted_iota(jnp.int32, value.shape, 1)
    full = value.astype(jnp.float32) * scale
    low = jnp.where(lane < 64, full, 0.0).astype(value.dtype)
    high = jnp.where(lane < 64, 0.0, full).astype(value.dtype)
    return jnp.concatenate([low, high], axis=0)


def parts(pair, at_k, at_q, tall, wide):
    width = HEADS * 64
    return (
        (0, pl.ds(at_q, wide), pl.ds(128 * pair, 128)),
        (0, pl.ds(at_k, tall), pl.ds(width + 128 * pair, 128)),
        (0, pl.ds(at_k, tall), pl.ds(2 * width + 128 * pair, 128)),
    )


def gather_into(ref, where, value):
    ref[where] = (ref[where].astype(jnp.float32) + value).astype(ref.dtype)


def forward_kernel(bounds_ref, qkv_ref, row_ref, bias_ref, out_ref, shares_ref):
    @pl.when(lax.rem(pl.program_id(0), RECEIPTS) == 0)
    def _():
        out_ref[...] = jnp.zeros_like(out_ref)

    def run(receipt, low, high, at_k, at_q, tall, wide):
        owner = pltpu.roll(row_ref[0], lax.rem(640 - at_q, 640), 1)[3:4, :wide]
        mine = jnp.where(owner == receipt, 1.0, 0.0)
        for pair in range(HEADS // 2):
            queries, keys, values = parts(pair, at_k, at_q, tall, wide)
            scores = dot(split_pair(qkv_ref[keys], 0.125), qkv_ref[queries], 1, 1)
            halves = []
            for h in range(2):
                part = scores[h * tall : (h + 1) * tall] + bias_ref[0, 2 * pair + h, :tall, :wide]
                expo = jnp.exp(part - jnp.max(part, axis=0, keepdims=True))
                share = expo * (mine / jnp.sum(expo, axis=0, keepdims=True))
                halves.append(share.astype(jnp.bfloat16))
                shares_ref[0, 2 * pair + h, :tall, :wide] = halves[h]
            shares = jnp.concatenate(halves, axis=0)
            gather_into(out_ref, queries, dot(shares, split_pair(qkv_ref[values]), 0, 0))

    by_size(bounds_ref, run)


def backward_kernel(offset, bounds_ref, qkv_ref, g_ref, shares_ref, dqkv_ref, ds_ref):
    @pl.when(lax.rem(pl.program_id(0), RECEIPTS) == 0)
    def _():
        dqkv_ref[...] = jnp.zeros_like(dqkv_ref)

    def run(receipt, low, high, at_k, at_q, tall, wide):
        for pair in range(HEADS // 2):
            queries, keys, values = parts(pair, at_k, at_q, tall, wide)
            grad = g_ref[queries]
            grad_probs = dot(split_pair(qkv_ref[values]), grad, 1, 1)
            shares, steps = [], []
            for h in range(2):
                share = shares_ref[0, 2 * pair + h, :tall, :wide]
                part = grad_probs[h * tall : (h + 1) * tall]
                probs = share.astype(jnp.float32)
                inner = jnp.sum(probs * part, axis=0, keepdims=True)
                step = (probs * (part - inner)).astype(jnp.bfloat16)
                ds_ref[0, 2 * pair + h, :tall, :wide] = step
                shares.append(share)
                steps.append(step)
            gather_into(dqkv_ref, values, dot(jnp.concatenate(shares, axis=1), split_pair(grad), 1, 0))
            gather_into(dqkv_ref, keys, dot(jnp.concatenate(steps, axis=1), split_pair(qkv_ref[queries], 0.125), 1, 0))
            gather_into(dqkv_ref, queries, dot(jnp.concatenate(steps, axis=0), split_pair(qkv_ref[keys], 0.125), 0, 0))

    by_size(bounds_ref, run, offset)


def bins_kernel(offset, bounds_ref, index_ref, ds_ref, bins_ref, terms_s):
    @pl.when(pl.program_id(0) == 0)
    def _():
        bins_ref[...] = jnp.zeros_like(bins_ref)
        terms_s[...] = jnp.zeros_like(terms_s)

    group = 16

    def run(receipt, low, high, at_k, at_q, tall, wide):
        for h in range(HEADS):
            for c in range(wide // 128):
                terms_s[c, pl.ds(h, tall, stride=16), :] = ds_ref[0, h, :tall, 128 * c : 128 * c + 128].astype(jnp.float32)
        level = lax.broadcasted_iota(jnp.int32, (BINS, 128), 0)

        def step(n, total):
            hots, terms = [], []
            at = pl.multiple_of(n * group, group)
            for c in range(wide // 128):
                packed = index_ref[0, pl.ds(at, group), 128 * c : 128 * c + 128]
                x, y, line = packed & 255, (packed >> 8) & 255, (packed >> 16) + 128
                for i in range(group):
                    def spread(value, count):
                        return jnp.broadcast_to(value[i : i + 1, :], (count, 128))

                    index = jnp.concatenate([spread(x, 64), spread(y, 64), spread(line, 32)], axis=0)
                    hots.append(jnp.where(level == index, 1.0, 0.0).astype(jnp.bfloat16))
                    terms.append(terms_s[c, pl.ds(pl.multiple_of((at + i) * 16, 16), 16), :].astype(jnp.bfloat16))
            return total + dot(jnp.concatenate(hots, axis=1), jnp.concatenate(terms, axis=1), 1, 1)

        total = lax.fori_loop(low // group, pl.cdiv(high, group), step, jnp.zeros((BINS, 16), jnp.float32))
        bins_ref[:, :BINS] += total.T

    by_size(bounds_ref, run, offset)


def of_row(shape, offset=0):
    return pl.BlockSpec((1,) + shape, lambda n, *_: (n // RECEIPTS + offset,) + (0,) * len(shape))


def of_step(shape, offset=0):
    return pl.BlockSpec((1,) + shape, lambda n, *_: (n + offset * RECEIPTS,) + (0,) * len(shape))


def fixed(shape):
    return pl.BlockSpec(shape, lambda n, *_: (0,) * len(shape))


def call(kernel, name, bounds, args, in_specs, out_specs, out_shape, steps, cost, scratch=(), vmem=48):
    return pl.pallas_call(
        kernel,
        grid_spec=pltpu.PrefetchScalarGridSpec(
            num_scalar_prefetch=1, grid=(steps,), in_specs=in_specs, out_specs=out_specs, scratch_shapes=scratch
        ),
        out_shape=out_shape,
        compiler_params=pltpu.CompilerParams(vmem_limit_bytes=vmem * 1024 * 1024),
        cost_estimate=pl.CostEstimate(flops=cost, bytes_accessed=cost // 1000, transcendentals=0),
        name=name,
    )(bounds, *args)


def make_bias(bounds, col, row, plane, lines):
    steps = col.shape[0] * RECEIPTS
    return call(
        bias_kernel, "make_bias", bounds, (col, row, plane, lines),
        [of_row((SPAN, 128)), of_row((8, 640)), fixed((HEADS, 128)), fixed((HEADS, 128))],
        [of_step((HEADS, TALL, WIDE)), of_step((TALL, WIDE))],
        [jax.ShapeDtypeStruct((steps, HEADS, TALL, WIDE), jnp.float32), jax.ShapeDtypeStruct((steps, TALL, WIDE), jnp.int32)],
        steps, 30_000_000_000,
    )


def attend(bounds, qkv, row, bias):
    rows, span, width = qkv.shape
    steps = rows * RECEIPTS
    return call(
        forward_kernel, "attend", bounds, (qkv, row, bias),
        [of_row((span, width)), of_row((8, 640)), of_step((HEADS, TALL, WIDE))],
        [of_row((span, width // 3)), of_step((HEADS, TALL, WIDE))],
        [
            jax.ShapeDtypeStruct((rows, span, width // 3), qkv.dtype),
            jax.ShapeDtypeStruct((steps, HEADS, TALL, WIDE), jnp.bfloat16),
        ],
        steps, 20_000_000_000,
    )


def attend_back(bounds, qkv, g, shares, first):
    rows, span, width = qkv.shape
    return call(
        functools.partial(backward_kernel, first), "attend_back", bounds, (qkv, g, shares),
        [of_row((span, width), first), of_row((span, width // 3), first), of_step((HEADS, TALL, WIDE), first)],
        [of_row((span, width)), of_step((HEADS, TALL, WIDE))],
        [
            jax.ShapeDtypeStruct((1, span, width), qkv.dtype),
            jax.ShapeDtypeStruct((RECEIPTS, HEADS, TALL, WIDE), jnp.bfloat16),
        ],
        RECEIPTS, 12_000_000_000,
    )


def make_bins(bounds, index, grads, first):
    out = (16, HEADS * 64)
    return call(
        functools.partial(bins_kernel, first), "make_bins", bounds, (index, grads),
        [of_step((TALL, WIDE), first), of_step((HEADS, TALL, WIDE))],
        fixed(out),
        jax.ShapeDtypeStruct(out, jnp.float32),
        RECEIPTS, 12_000_000_000, [pltpu.VMEM((2, TALL * 16, 128), jnp.float32)],
    )


EPSILON = 1e-05


def gelu_parts(u):
    expo = jnp.exp(u * u * -0.5)
    share = 0.5 + 0.5 * lax.erf(u * (1.0 / math.sqrt(2.0)))
    return u * share, share + u * expo * (1.0 / math.sqrt(2.0 * math.pi))


def standard(values):
    centred = values - jnp.mean(values, axis=1, keepdims=True)
    scale = lax.rsqrt(jnp.mean(centred * centred, axis=1, keepdims=True) + EPSILON)
    return centred * scale, scale


def standard_back(normed, scale, grad):
    return (
        grad - jnp.mean(grad, axis=1, keepdims=True) - normed * jnp.mean(grad * normed, axis=1, keepdims=True)
    ) * scale


def total(value):
    return jnp.sum(value, axis=0, keepdims=True)


def up_kernel(
    context_ref, stream_ref, cot_ref, w_out_ref, w_up_ref, w_down_ref, rows_ref, b_up_ref,
    mid_ref, hidden_ref, active_ref, slope_ref, out_ref, top_ref, branch_ref, sums_ref, *, chunk,
):
    b_out, gain_1, shift_1, b_down, gain_2, shift_2 = (rows_ref[n : n + 1, :] for n in range(6))
    mid = stream_ref[...] + dot(context_ref[...], w_out_ref[...], 1, 0) + b_out
    mid_ref[...] = mid
    norm_one = standard(mid)[0] * gain_1 + shift_1
    hidden = norm_one.astype(jnp.bfloat16)
    hidden_ref[...] = hidden
    branch = norm_one + b_down
    for at in range(0, w_up_ref.shape[1], chunk):
        piece = slice(at, at + chunk)
        inner = dot(hidden, w_up_ref[:, piece], 1, 0) + b_up_ref[:, piece]
        active, slope = gelu_parts(inner)
        active = active.astype(jnp.bfloat16)
        active_ref[:, piece] = active
        slope_ref[:, piece] = slope.astype(jnp.bfloat16)
        branch = branch + dot(active, w_down_ref[piece, :], 1, 0)
    normed, scale = standard(branch)
    out_ref[...] = (normed * gain_2 + shift_2).astype(jnp.bfloat16)
    cot = cot_ref[...].astype(jnp.float32)
    top = standard_back(normed, scale, cot * gain_2)
    top_ref[...] = top
    low = top.astype(jnp.bfloat16)
    branch_ref[...] = low

    @pl.when(pl.program_id(0) == 0)
    def _():
        sums_ref[...] = jnp.zeros_like(sums_ref)

    sums_ref[0:1, :] += total(cot * normed)
    sums_ref[1:2, :] += total(cot)
    sums_ref[2:3, :] += total(low.astype(jnp.float32))


def down_kernel(
    branch_ref, slope_ref, top_ref, mid_ref, w_out_ref, w_up_ref, w_down_ref, rows_ref,
    inner_ref, mid_grad_ref, attended_ref, context_ref, sums_ref, ups_ref, *, chunk,
):
    @pl.when(pl.program_id(0) == 0)
    def _():
        sums_ref[...] = jnp.zeros_like(sums_ref)
        ups_ref[...] = jnp.zeros_like(ups_ref)

    gain_1 = rows_ref[1:2, :]
    branch = branch_ref[...]
    grad = top_ref[...]
    for at in range(0, w_up_ref.shape[1], chunk):
        piece = slice(at, at + chunk)
        inner = dot(branch, w_down_ref[piece, :], 1, 1) * slope_ref[:, piece].astype(jnp.float32)
        low = inner.astype(jnp.bfloat16)
        inner_ref[:, piece] = low
        ups_ref[0:1, piece] += total(low.astype(jnp.float32))
        grad = grad + dot(low, w_up_ref[:, piece], 1, 1)
    normed, scale = standard(mid_ref[...])
    back = standard_back(normed, scale, grad * gain_1)
    mid_grad_ref[...] = back
    low = back.astype(jnp.bfloat16)
    attended_ref[...] = low
    context_ref[...] = dot(low, w_out_ref[...], 1, 1).astype(jnp.bfloat16)
    sums_ref[0:1, :] += total(grad * normed)
    sums_ref[1:2, :] += total(grad)
    sums_ref[2:3, :] += total(low.astype(jnp.float32))


def tiled(tile, width):
    return pl.BlockSpec((tile, width), lambda n: (n, 0))


def whole(shape):
    return pl.BlockSpec(shape, lambda n: (0, 0))


def feed_forward(context, stream_in, cot, w_out, w_up, w_down, vectors, b_up, tile=384, chunk=512):
    tokens, width = context.shape
    deep = w_up.shape[1]
    low, full = jnp.bfloat16, jnp.float32
    shapes = [(width, full), (width, low), (deep, low), (deep, low), (width, low), (width, full), (width, low)]
    return pl.pallas_call(
        functools.partial(up_kernel, chunk=chunk),
        grid=(tokens // tile,),
        in_specs=[tiled(tile, width)] * 3
        + [whole(w_out.shape), whole(w_up.shape), whole(w_down.shape), whole(vectors.shape), whole(b_up.shape)],
        out_specs=[tiled(tile, n) for n, _ in shapes] + [whole((8, width))],
        out_shape=[jax.ShapeDtypeStruct((tokens, n), kind) for n, kind in shapes]
        + [jax.ShapeDtypeStruct((8, width), full)],
        compiler_params=pltpu.CompilerParams(vmem_limit_bytes=60 * 1024 * 1024),
        cost_estimate=pl.CostEstimate(flops=20_000_000_000, bytes_accessed=60_000_000, transcendentals=0),
        name="feed_forward",
    )(context, stream_in, cot, w_out, w_up, w_down, vectors, b_up)


def feed_back(branch, slope, top, mid, w_out, w_up, w_down, vectors, tile=384, chunk=512):
    tokens, width = branch.shape
    deep = w_up.shape[1]
    low, full = jnp.bfloat16, jnp.float32
    shapes = [(deep, low), (width, full), (width, low), (width, low)]
    return pl.pallas_call(
        functools.partial(down_kernel, chunk=chunk),
        grid=(tokens // tile,),
        in_specs=[tiled(tile, width), tiled(tile, deep), tiled(tile, width), tiled(tile, width)]
        + [whole(w_out.shape), whole(w_up.shape), whole(w_down.shape), whole(vectors.shape)],
        out_specs=[tiled(tile, n) for n, _ in shapes] + [whole((8, width)), whole((8, deep))],
        out_shape=[jax.ShapeDtypeStruct((tokens, n), kind) for n, kind in shapes]
        + [jax.ShapeDtypeStruct((8, width), full), jax.ShapeDtypeStruct((8, deep), full)],
        compiler_params=pltpu.CompilerParams(vmem_limit_bytes=60 * 1024 * 1024),
        cost_estimate=pl.CostEstimate(flops=20_000_000_000, bytes_accessed=60_000_000, transcendentals=0),
        name="feed_back",
    )(branch, slope, top, mid, w_out, w_up, w_down, vectors)


DP = "dp"
STREAM = "stream"


def swap(value, axis, bit):
    count = lax.axis_size(axis)
    return lax.ppermute(value, axis, [(i, i ^ bit) for i in range(count)])


def bits_of(axis):
    count = lax.axis_size(axis)
    return [1 << n for n in range(count.bit_length() - 1)]


def stages(flip):
    core, *chips = bits_of(DP)
    if flip:
        chips = chips[::-1]
    return [(DP, core)] + [(DP, bit) for bit in chips] + [(STREAM, bit) for bit in bits_of(STREAM)]


class Scatter:
    def __init__(self, values, flip):
        self.names = [(axis, bit) for axis in (DP, STREAM) for bit in bits_of(axis)[::-1]]
        self.values = [value.reshape((2,) * len(self.names) + value.shape[1:]) for value in values]
        self.left = stages(flip)

    def send(self):
        stage = self.left.pop(0)
        axis, bit = stage
        dim = self.names.index(stage)
        self.names.pop(dim)
        side = (lax.axis_index(axis) // bit) % 2

        def pick(value, n):
            return lax.dynamic_index_in_dim(value, n, dim, keepdims=False)

        given = jnp.concatenate([pick(value, 1 - side).astype(jnp.bfloat16) for value in self.values], axis=-1)
        self.kept = [pick(value, side) for value in self.values]
        self.got = swap(given, axis, bit)

    def add(self):
        if self.got is None:
            return
        self.values, at = [], 0
        for kept in self.kept:
            got = self.got[..., at : at + kept.shape[-1]]
            at += kept.shape[-1]
            self.values.append(kept + got.astype(jnp.float32))
        self.got = None

    def next(self):
        self.add()
        if self.left:
            self.send()

    def after(self, other):
        if self.got is None:
            return other
        other, self.got = lax.optimization_barrier((other, self.got))
        return other

    def finish(self):
        while self.left:
            self.next()
        self.add()
        return self.values


def together(*values):
    return lax.optimization_barrier(values)


def sum_all(value):
    for axis, bit in stages(False):
        value = value + swap(value, axis, bit)
    return value


def turned(shift):
    count = lax.axis_size(STREAM)
    return [(i, (i + shift) % count) for i in range(count)]


def to_rows(value):
    count = lax.axis_size(STREAM)
    place = lax.axis_index(STREAM)
    block = value.shape[0] // count
    parts = []
    for shift in range(count):
        part = lax.dynamic_slice_in_dim(value, (place - shift) % count * block, block, 0)
        parts.append(lax.ppermute(part, STREAM, turned(-shift)) if shift else part)
    return jnp.concatenate(parts, axis=1)


def slot_sends(value):
    count = lax.axis_size(STREAM)
    block = value.shape[0] // count
    parts = [value[shift * block : (shift + 1) * block] for shift in range(count)]
    return parts[:1] + [lax.ppermute(parts[shift], STREAM, turned(shift)) for shift in range(1, count)]


def from_sends(rows, dtype):
    count = lax.axis_size(STREAM)
    place = lax.axis_index(STREAM)
    whole = jnp.zeros((len(rows) * count,) + rows[0][0].shape, dtype)
    for at, parts in enumerate(rows):
        for shift, part in enumerate(parts):
            whole = lax.dynamic_update_slice_in_dim(
                whole, part[None].astype(dtype), (place - shift) % count * len(rows) + at, 0
            )
    return whole


def per_device(
    text_input,
    visual_features,
    receipt_text,
    receipt_visual,
    boxes,
    w_query,
    b_query,
    w_key,
    w_value,
    b_value,
    w_out,
    b_out,
    gain_attn,
    shift_attn,
    w_up,
    b_up,
    w_down,
    b_down,
    gain_ffn,
    shift_ffn,
    w_visual,
    b_visual,
    table_line,
    table_x,
    table_y,
    cotangent_text,
    cotangent_visual,
):
    floating = jnp.float32
    narrow = jnp.bfloat16
    width = text_input.shape[-1]
    rows, visual, channels = visual_features.shape
    text = receipt_text.shape[1]
    slots = text + visual
    world = lax.axis_size(DP) * lax.axis_size(STREAM)
    place = lax.axis_index(STREAM)
    first_row = place * rows

    text_rows = to_rows(text_input)
    text_rows, cotangent_text = lax.optimization_barrier((text_rows, cotangent_text))
    cotangent_rows = to_rows(cotangent_text)

    def pad(value, fill=0):
        extra = SPAN - value.shape[1]
        return jnp.pad(value, ((0, 0), (0, extra)) + ((0, 0),) * (value.ndim - 2), constant_values=fill)

    seg_text = lax.dynamic_slice_in_dim(receipt_text, first_row, rows, 0)
    seg_visual = lax.dynamic_slice_in_dim(receipt_visual, first_row, rows, 0)
    box = lax.dynamic_slice_in_dim(boxes, first_row, rows, 1)
    index = jnp.arange(SPAN, dtype=jnp.int32)
    position = jnp.where(index < text, index, index - text)
    facts = jnp.stack(
        [
            jnp.broadcast_to(position, (rows, SPAN)),
            pad(box[0]),
            pad(box[1]),
            pad(jnp.concatenate([seg_text, seg_visual], axis=1), RECEIPTS),
            jnp.broadcast_to(index, (rows, SPAN)),
        ],
        axis=1,
    )
    own = lax.dynamic_slice_in_dim(
        jnp.concatenate([facts[:, :, :text], facts[:, :, :text]], axis=2), place * text_input.shape[1], text, 2
    )
    facts = jnp.concatenate([own, facts[:, :, text:]], axis=2)
    rank = facts[:, 3] * SPAN + facts[:, 4]
    seg = facts[:, 3]
    target = jnp.sum((rank[:, None, :] < rank[:, :, None]).astype(jnp.int32), axis=2)
    moved = target[:, None, :] == index[None, :, None]
    facts = facts[:, :4]
    facts = jnp.sum(jnp.where(moved[:, None], facts[:, :, None, :], 0), axis=3)
    col = jnp.pad(jnp.swapaxes(facts, 1, 2), ((0, 0), (0, 0), (0, 124)))
    row = jnp.pad(facts, ((0, 0), (0, 4), (0, 640 - SPAN)), constant_values=RECEIPTS)
    bounds = jnp.sum(
        (seg[:, None, :] < jnp.arange(16, dtype=jnp.int32)[None, :, None]).astype(jnp.int32), axis=2
    ).reshape(-1)
    plane = jnp.concatenate([table_x, table_y], axis=1).astype(floating)
    lines = jnp.pad(table_line.astype(floating), ((0, 0), (0, 96)), constant_values=NONE)

    bias, places = make_bias(bounds, col, row, plane, lines)
    moving = moved.astype(narrow)

    def sort(value):
        return jnp.einsum("rps,rsd->rpd", moving[:, :, : value.shape[1]], value, preferred_element_type=floating)

    def unsort(value):
        return jnp.einsum("rps,rpd->rsd", moving, value, preferred_element_type=floating)

    def rowwise(array):
        return array.reshape(rows, SPAN, -1)

    w_qkv = jnp.concatenate([w_query, w_key, w_value], axis=1)
    b_qkv = jnp.concatenate([b_query, jnp.zeros_like(b_query), b_value]).astype(floating)
    features = jnp.einsum(
        "rpv,rvc->rpc", moving[:, :, text:slots], visual_features, preferred_element_type=floating
    ).astype(narrow)
    is_visual = jnp.sum(moving[:, :, text:slots].astype(floating), axis=2)[:, :, None]
    features_flat = features.reshape(-1, channels)
    visual_pre = jnp.einsum("rpc,cd->rpd", features, w_visual, preferred_element_type=floating)
    visual_pre = (visual_pre + b_visual.astype(floating)) * is_visual
    stream_in = (sort(text_rows) + visual_pre).reshape(-1, width)
    entered = stream_in.astype(narrow)
    qkv = rowwise((jnp.dot(entered, w_qkv, preferred_element_type=floating) + b_qkv).astype(narrow))
    context, shares = attend(bounds, qkv, row, bias)
    context, cotangent_rows = together(context, cotangent_rows)
    context = context.reshape(-1, width)
    cotangent = sort(jnp.concatenate([cotangent_rows, cotangent_visual], axis=1)).astype(narrow).reshape(-1, width)
    vectors = jnp.stack([b_out, gain_attn, shift_attn, b_down, gain_ffn, shift_ffn, b_out, b_out]).astype(floating)
    mid, hidden, active, slope, outcome, grad_top, grad_branch, ffn_sums = feed_forward(
        context, stream_in, cotangent, w_out, w_up, w_down, vectors, b_up.astype(floating)[None]
    )
    grad_w_down = jnp.einsum("tf,td->fd", active, grad_branch, preferred_element_type=floating)
    grad_w_down, grad_branch, outcome = together(grad_w_down, grad_branch, outcome)
    downs = Scatter([grad_w_down.reshape(world, -1, width)], False)
    downs.send()
    out_rows = unsort(rowwise(outcome)).astype(narrow)
    out_visual = out_rows[:, text:slots]
    grad_branch, out_rows = together(grad_branch, out_rows)
    grad_branch = downs.after(grad_branch)
    downs.next()
    out_sends = [slot_sends(out[:text]) for out in out_rows]
    grad_inner, grad_mid, grad_attended, grad_context, attn_sums, up_sums = feed_back(
        grad_branch, slope, grad_top, mid, w_out, w_up, w_down, vectors
    )
    grad_w_up = jnp.einsum("td,tf->df", hidden, grad_inner, preferred_element_type=floating)
    grad_w_out = jnp.einsum("td,te->de", context, grad_attended, preferred_element_type=floating)
    grad_context, grad_w_out, grad_w_up = together(grad_context, grad_w_out, grad_w_up)
    flat, tree = jax.tree.flatten(out_sends)
    grad_context, *flat = together(grad_context, *flat)
    out_text = from_sends(jax.tree.unflatten(tree, flat), narrow)
    ups = Scatter([part.reshape(world, width // world, -1) for part in (grad_w_up, grad_w_out)], True)
    ups.send()

    grad_context = rowwise(grad_context)
    entered_rows, grad_mid_rows = rowwise(entered), rowwise(grad_mid)

    def advance(value, groups, extra=()):
        tied = together(value, *extra, *(group.got for group in groups))
        for group, got in zip(groups, tied[1 + len(extra) :]):
            group.got = got
            group.next()
        return tied[0], list(tied[1 : 1 + len(extra)])

    def project(r, grad_qkv):
        grad_stream = grad_mid_rows[r] + jnp.einsum("te,de->td", grad_qkv, w_qkv, preferred_element_type=floating)
        (grad_low,) = together(grad_stream.astype(narrow))
        back = jnp.einsum("ps,pd->sd", moving[r], grad_low, preferred_element_type=floating).astype(narrow)
        grad_w = jnp.einsum("td,te->de", entered_rows[r], grad_qkv, preferred_element_type=floating)
        return back, grad_w, jnp.sum(grad_qkv, axis=0, dtype=floating)

    grad_qkv, step_0 = attend_back(bounds, qkv, grad_context, shares, 0)
    grad_qkv, _ = advance(grad_qkv[0], [downs, ups])
    back_0, grad_w_qkv, grad_b_qkv = project(0, grad_qkv)
    got_0 = slot_sends(back_0[:text])
    grad_context, back_0, grad_w_qkv = together(grad_context, back_0, grad_w_qkv)
    grad_qkv, step_1 = attend_back(bounds, qkv, grad_context, shares, 1)
    grad_qkv, got_0 = advance(grad_qkv[0], [downs, ups], got_0)
    back_1, more_w, more_b = project(1, grad_qkv)
    got_1 = slot_sends(back_1[:text])
    grad_w_qkv, grad_b_qkv = grad_w_qkv + more_w, grad_b_qkv + more_b
    grad_visual = jnp.stack([back_0[text:slots], back_1[text:slots]])
    grad_w_visual = jnp.einsum("rvc,rvd->cd", visual_features, grad_visual, preferred_element_type=floating)
    grad_b_visual = jnp.sum(grad_visual, axis=(0, 1), dtype=floating)
    grad_features = jnp.einsum("rvd,cd->rvc", grad_visual, w_visual, preferred_element_type=floating)
    lasts = Scatter([part.reshape(world, width // world, -1) for part in (grad_w_qkv, grad_w_visual)], False)
    lasts.send()
    step_0, back_1, *lasts.kept = together(step_0, back_1, *lasts.kept)
    bins = make_bins(bounds, places, step_0, 0)
    bins, got_1 = advance(bins, [downs, ups, lasts], got_1)
    step_1, bins = together(step_1, bins)
    more = make_bins(bounds, places, step_1, 1)
    more, _ = advance(more, [group for group in (downs, ups, lasts) if group.got is not None])
    bins = bins + more
    grad_text = from_sends([got_0, got_1], floating)
    (down_sum,) = downs.finish()
    up_sum, out_sum = ups.finish()
    qkv_sum, visual_sum = lasts.finish()
    query_sum, key_sum, value_sum = (qkv_sum[:, n * width : (n + 1) * width] for n in range(3))
    visual_sum = visual_sum.reshape(-1, width)
    step = width // world
    def lines_of(value):
        return [value[:, n : n + width] for n in range(0, value.shape[1], width)]

    small = sum_all(
        jnp.concatenate(
            [ffn_sums, attn_sums, bins]
            + lines_of(grad_b_qkv[None]) + [grad_b_visual[None]] + lines_of(up_sums[:1]),
            axis=0,
        )
    )
    device = lax.axis_index(DP) * lax.axis_size(STREAM) + place
    mine = lax.dynamic_slice_in_dim(small, device * step, step, 1)
    up_step = w_up.shape[1] // world
    bins = small[16 : 16 + HEADS]
    return (
        out_text,
        out_visual,
        grad_text,
        grad_features,
        query_sum,
        mine[32],
        key_sum,
        value_sum,
        mine[34],
        out_sum,
        mine[10],
        mine[8],
        mine[9],
        up_sum,
        lax.dynamic_slice_in_dim(small[36:].reshape(-1), device * up_step, up_step, 0),
        down_sum,
        mine[2],
        mine[0],
        mine[1],
        visual_sum,
        mine[35],
        bins[:, 128:160],
        bins[:, :64],
        bins[:, 64:128],
    )


def solution(mesh):
    placed = (
        P("dp", "stream", None),
        P(("dp", "stream"), None, None),
        P("dp", None),
        P("dp", None),
        P(None, "dp", None),
        P(),
        P(),
        P(),
        P(),
        P(),
        P(),
        P(),
        P(),
        P(),
        P(),
        P(),
        P(),
        P(),
        P(),
        P(),
        P(),
        P(),
        P(),
        P(),
        P(),
        P("dp", "stream", None),
        P(("dp", "stream"), None, None),
    )
    return jax.shard_map(
        per_device,
        mesh=mesh,
        in_specs=placed,
        out_specs=(
            P("dp", "stream", None),
            P(("dp", "stream"), None, None),
            P("dp", "stream", None),
            P(("dp", "stream"), None, None),
            P(("dp", "stream"), None),
            P(("dp", "stream")),
            P(("dp", "stream"), None),
            P(("dp", "stream"), None),
            P(("dp", "stream")),
            P(("dp", "stream"), None),
            P(("dp", "stream")),
            P(("dp", "stream")),
            P(("dp", "stream")),
            P(("dp", "stream"), None),
            P(("dp", "stream")),
            P(("dp", "stream"), None),
            P(("dp", "stream")),
            P(("dp", "stream")),
            P(("dp", "stream")),
            P(("dp", "stream"), None),
            P(("dp", "stream")),
            P(),
            P(),
            P(),
        ),
        check_vma=False,
    )
```

```python
import functools
import math

import jax, jax.numpy as jnp
from jax import lax
from jax.experimental import pallas as pl
from jax.experimental.pallas import tpu as pltpu
from jax.sharding import PartitionSpec as P

HEADS = 12
RECEIPTS = 8
VISUAL = 49
PLAN = 32
SPAN = 576
BINS = 160
NONE = -1e30
TALL = 192
WIDE = 256
FORWARD_PAIRS = 6
BACKWARD_PAIRS = 6


def thresholds(half, reach):
    exact = half // 2
    steps = half - exact
    return [
        int(math.floor(exact * (reach / exact) ** (power / steps) + 0.5))
        for power in range(1, steps)
    ]


def bucket(diff, count, reach):
    half = count // 2
    exact = half // 2
    dist = jnp.abs(diff)
    passed = jnp.where(diff > 0, half, 0)
    for limit in thresholds(half, reach):
        passed = passed + jnp.where(dist >= limit, 1, 0)
    return passed + jnp.minimum(dist, exact)


def dot(a, b, ca, cb):
    return lax.dot_general(a, b, (((ca,), (cb,)), ((), ())), preferred_element_type=jnp.float32)


def by_size(plan_ref, run, offset=0):
    step = pl.program_id(0)
    receipt = lax.rem(step, RECEIPTS)
    base = (step // RECEIPTS + offset) * PLAN + receipt
    first = plan_ref[base]
    last = plan_ref[base + 1]
    start = first // 16 * 16
    low = 0
    for tall in (64, 96, 128, 160, 192):
        wide = 128 if tall <= 128 else 256
        inside = last - start > low
        if tall < TALL:
            inside = jnp.logical_and(inside, last - start <= tall)
        low = tall

        @pl.when(inside)
        def _(tall=tall, wide=wide):
            at_k = pl.multiple_of(jnp.minimum(start, SPAN - tall), 16)
            at_q = pl.multiple_of(jnp.minimum(start, SPAN - wide), 16)
            run(receipt, first - at_k, last - at_k, at_k, at_q, tall, wide)


def blocks(refs, head, tile, tall):
    found = []
    for n, (which, lead) in enumerate((((0, ()), (1, ()), (2, (0,))), ((2, (1,)), (2, (2,)), (2, (3,))))[tile]):
        size = min(64, tall - 64 * n)
        if size > 0:
            found.append((refs[which], (0,) + lead + (head, pl.ds(0, size)), 64 * n, size))
    return found


def load(refs, head, tall, wide):
    return joined(
        [joined([ref[at] for ref, at, _, _ in blocks(refs, head, tile, tall)], 0) for tile in range(wide // 128)], 1
    )


def store(refs, head, value):
    tall, wide = value.shape
    for tile in range(wide // 128):
        for ref, at, row, size in blocks(refs, head, tile, tall):
            ref[at] = value[row : row + size, 128 * tile : 128 * tile + 128]


def joined(pieces, axis):
    return pieces[0] if len(pieces) == 1 else jnp.concatenate(pieces, axis=axis)


def bias_kernel(plan_ref, col_ref, row_ref, plane_ref, lines_ref, near_ref, mid_ref, far_ref, index_ref):
    refs = (near_ref, mid_ref, far_ref)
    height = 32

    def run(receipt, low, high, at_k, at_q, tall, wide):
        row = pltpu.roll(row_ref[0], lax.rem(640 - at_q, 640), 1)[:, :wide]
        shape = (height, 128)

        def fill(tile, n, at):
            _, lead = (((0, ()), (1, ()), (2, (0,))), ((2, (1,)), (2, (2,)), (2, (3,))))[tile][n]
            ref = refs[(((0, 1, 2), (2, 2, 2))[tile])[n]]
            lanes = slice(128 * tile, 128 * (tile + 1))
            here = pl.multiple_of(64 * n + at, height)
            used = jnp.logical_and(here < high, here + height > low)

            @pl.when(jnp.logical_not(used))
            def _():
                for h in range(HEADS):
                    ref[(0,) + lead + (h, pl.ds(at, height))] = jnp.full(shape, NONE, jnp.float32)

            @pl.when(used)
            def _():
                col = col_ref[0, pl.ds(pl.multiple_of(at_k + here, 16), height), :]

                def spread(r):
                    return (jnp.broadcast_to(col[:, r : r + 1], shape), jnp.broadcast_to(row[r : r + 1, lanes], shape))

                def gap(r):
                    key, query = spread(r)
                    return key - query

                key, query = spread(3)
                same = jnp.logical_and(key == receipt, query == receipt)
                line = jnp.where(same, bucket(gap(0), 32, 128), 32)
                across = bucket(gap(1), 64, 256)
                down = bucket(gap(2), 64, 256) + 64
                index_ref[0, pl.ds(here, height), lanes] = across + down * 256 + line * 65536
                def look(table_ref, h, index):
                    table = jnp.broadcast_to(table_ref[h : h + 1, :], (8, 128))
                    return jnp.take_along_axis(table, index, axis=1, mode="promise_in_bounds")
                for r in range(height // 8):
                    a8, d8, l8 = (v[8 * r : 8 * r + 8] for v in (across, down, line))

                    xs = [look(plane_ref, h, a8) for h in range(HEADS)]
                    ys = [look(plane_ref, h, d8) for h in range(HEADS)]
                    ls = [look(lines_ref, h, l8) for h in range(HEADS)]
                    for h in range(HEADS):
                        ref[(0,) + lead + (h, pl.ds(at + 8 * r, 8))] = xs[h] + ys[h] + ls[h]

        for tile in range(wide // 128):
            for n in range(pl.cdiv(tall, 64)):
                def step(m, carry, tile=tile, n=n):
                    fill(tile, n, pl.multiple_of(m * height, height))
                    return carry

                lax.fori_loop(0, 2, step, 0)

    by_size(plan_ref, run)


def split_pair(value, scale=1.0):
    lane = lax.broadcasted_iota(jnp.int32, value.shape, 1)
    full = value.astype(jnp.float32) * scale
    low = jnp.where(lane < 64, full, 0.0).astype(value.dtype)
    high = jnp.where(lane < 64, 0.0, full).astype(value.dtype)
    return jnp.concatenate([low, high], axis=0)


def grouped(size):
    return [range(n, n + size) for n in range(0, HEADS // 2, size)]


def parts(pair, at_k, at_q, tall, wide):
    width = HEADS * 64
    return (
        (0, pl.ds(at_q, wide), pl.ds(128 * pair, 128)),
        (0, pl.ds(at_k, tall), pl.ds(width + 128 * pair, 128)),
        (0, pl.ds(at_k, tall), pl.ds(2 * width + 128 * pair, 128)),
    )


def gather_into(ref, where, value):
    ref[where] = (ref[where].astype(jnp.float32) + value).astype(ref.dtype)


def forward_kernel(plan_ref, qkv_ref, row_ref, *refs):
    bias_refs, out_ref, shares_refs = refs[:3], refs[3], refs[4:]

    @pl.when(lax.rem(pl.program_id(0), RECEIPTS) == 0)
    def _():
        out_ref[...] = jnp.zeros_like(out_ref)

    def run(receipt, low, high, at_k, at_q, tall, wide):
        owner = pltpu.roll(row_ref[0], lax.rem(640 - at_q, 640), 1)[3:4, :wide]
        mine = jnp.where(owner == receipt, 1.0, 0.0)
        for group in grouped(FORWARD_PAIRS):
            spots = [parts(pair, at_k, at_q, tall, wide) for pair in group]
            scores = [
                dot(split_pair(qkv_ref[keys], 0.125), qkv_ref[queries], 1, 1) for queries, keys, _ in spots
            ]
            shares = []
            for pair, score in zip(group, scores):
                halves = []
                for h in range(2):
                    part = score[h * tall : (h + 1) * tall] + load(bias_refs, 2 * pair + h, tall, wide)
                    expo = jnp.exp(part - jnp.max(part, axis=0, keepdims=True))
                    share = expo * (mine / jnp.sum(expo, axis=0, keepdims=True))
                    halves.append(share.astype(jnp.bfloat16))
                    store(shares_refs, 2 * pair + h, halves[h])
                shares.append(jnp.concatenate(halves, axis=0))
            results = [dot(share, split_pair(qkv_ref[values]), 0, 0) for share, (_, _, values) in zip(shares, spots)]
            for result, (queries, _, _) in zip(results, spots):
                gather_into(out_ref, queries, result)

    by_size(plan_ref, run)


def backward_kernel(offset, plan_ref, qkv_ref, g_ref, *refs):
    shares_refs, dqkv_ref, ds_refs = refs[:3], refs[3], refs[4:]

    @pl.when(lax.rem(pl.program_id(0), RECEIPTS) == 0)
    def _():
        dqkv_ref[...] = jnp.zeros_like(dqkv_ref)

    def run(receipt, low, high, at_k, at_q, tall, wide):
        for group in grouped(BACKWARD_PAIRS):
            spots = [parts(pair, at_k, at_q, tall, wide) for pair in group]
            grads = [g_ref[queries] for queries, _, _ in spots]
            parts_of = [
                dot(split_pair(qkv_ref[values]), grad, 1, 1) for grad, (_, _, values) in zip(grads, spots)
            ]
            shares, steps = [], []
            for pair, grad_probs in zip(group, parts_of):
                for h in range(2):
                    share = load(shares_refs, 2 * pair + h, tall, wide)
                    part = grad_probs[h * tall : (h + 1) * tall]
                    probs = share.astype(jnp.float32)
                    inner = jnp.sum(probs * part, axis=0, keepdims=True)
                    step = (probs * (part - inner)).astype(jnp.bfloat16)
                    store(ds_refs, 2 * pair + h, step)
                    shares.append(share)
                    steps.append(step)
            results = []
            for n, (queries, keys, values) in enumerate(spots):
                pair = slice(2 * n, 2 * n + 2)
                results.append((values, dot(jnp.concatenate(shares[pair], axis=1), split_pair(grads[n]), 1, 0)))
                query = split_pair(qkv_ref[queries], 0.125)
                results.append((keys, dot(jnp.concatenate(steps[pair], axis=1), query, 1, 0)))
                key = split_pair(qkv_ref[keys], 0.125)
                results.append((queries, dot(jnp.concatenate(steps[pair], axis=0), key, 0, 0)))
            for where, result in results:
                gather_into(dqkv_ref, where, result)

    by_size(plan_ref, run, offset)


def bins_kernel(offset, plan_ref, index_ref, near_ref, mid_ref, far_ref, bins_ref, terms_s):
    refs = (near_ref, mid_ref, far_ref)

    @pl.when(pl.program_id(0) == 0)
    def _():
        bins_ref[...] = jnp.zeros_like(bins_ref)
        terms_s[...] = jnp.zeros_like(terms_s)

    group = 32

    def run(receipt, low, high, at_k, at_q, tall, wide):
        for h in range(HEADS):
            for c in range(wide // 128):
                for ref, at, row, size in blocks(refs, h, c, tall):
                    terms_s[c, pl.ds(row * 16 + h, size, stride=16), :] = ref[at].astype(jnp.float32)
        level = lax.broadcasted_iota(jnp.int32, (BINS, 128), 0)

        def step(n, total):
            hots, terms = [], []
            at = pl.multiple_of(n * group, group)
            for c in range(wide // 128):
                packed = index_ref[0, pl.ds(at, group), 128 * c : 128 * c + 128]
                x, y, line = packed & 255, (packed >> 8) & 255, (packed >> 16) + 128
                for i in range(group):
                    def spread(value, count):
                        return jnp.broadcast_to(value[i : i + 1, :], (count, 128))

                    index = jnp.concatenate([spread(x, 64), spread(y, 64), spread(line, 32)], axis=0)
                    hots.append(jnp.where(level == index, 1.0, 0.0).astype(jnp.bfloat16))
                    terms.append(terms_s[c, pl.ds(pl.multiple_of((at + i) * 16, 16), 16), :].astype(jnp.bfloat16))
            return total + dot(jnp.concatenate(terms, axis=1), jnp.concatenate(hots, axis=1), 1, 1)

        total = lax.fori_loop(low // group, pl.cdiv(high, group), step, jnp.zeros((16, BINS), jnp.float32))
        bins_ref[:, :BINS] += total

    by_size(plan_ref, run, offset)


def of_row(shape, offset=0):
    return pl.BlockSpec((1,) + shape, lambda n, *_: (n // RECEIPTS + offset,) + (0,) * len(shape))


def of_step(shape, offset=0):
    return pl.BlockSpec((1,) + shape, lambda n, *_: (n + offset * RECEIPTS,) + (0,) * len(shape))


def of_plan(shape, offset, base, at):
    def place(n, plan_ref):
        row = n // RECEIPTS
        step = plan_ref[(row + offset) * PLAN + at + lax.rem(n, RECEIPTS)]
        return ((row + base) * RECEIPTS + step,) + (0,) * len(shape)

    return pl.BlockSpec((1,) + shape, place)


def tile_specs(offset=0, base=0):
    near, far = (HEADS, 64, 128), (4, HEADS, 64, 128)
    return [of_step(near, base), of_plan(near, offset, base, 16), of_plan(far, offset, base, 24)]


def tile_shapes(steps, kind):
    shapes = ((HEADS, 64, 128), (HEADS, 64, 128), (4, HEADS, 64, 128))
    return [jax.ShapeDtypeStruct((steps,) + shape, kind) for shape in shapes]


def fixed(shape):
    return pl.BlockSpec(shape, lambda n, *_: (0,) * len(shape))


def call(kernel, name, plan, args, in_specs, out_specs, out_shape, steps, cost, scratch=(), vmem=48):
    return pl.pallas_call(
        kernel,
        grid_spec=pltpu.PrefetchScalarGridSpec(
            num_scalar_prefetch=1, grid=(steps,), in_specs=in_specs, out_specs=out_specs, scratch_shapes=scratch
        ),
        out_shape=out_shape,
        compiler_params=pltpu.CompilerParams(vmem_limit_bytes=vmem * 1024 * 1024),
        cost_estimate=pl.CostEstimate(flops=cost, bytes_accessed=cost // 1000, transcendentals=0),
        name=name,
    )(plan, *args)


def make_bias(plan, col, row, plane, lines):
    steps = col.shape[0] * RECEIPTS
    *bias, index = call(
        bias_kernel, "make_bias", plan, (col, row, plane, lines),
        [of_row((SPAN, 128)), of_row((8, 640)), fixed((HEADS, 128)), fixed((HEADS, 128))],
        tile_specs() + [of_step((TALL, WIDE))],
        tile_shapes(steps, jnp.float32) + [jax.ShapeDtypeStruct((steps, TALL, WIDE), jnp.int32)],
        steps, 30_000_000_000,
    )
    return bias, index


def attend(plan, qkv, row, bias):
    rows, span, width = qkv.shape
    steps = rows * RECEIPTS
    out, *shares = call(
        forward_kernel, "attend", plan, (qkv, row, *bias),
        [of_row((span, width)), of_row((8, 640))] + tile_specs(),
        [of_row((span, width // 3))] + tile_specs(),
        [jax.ShapeDtypeStruct((rows, span, width // 3), qkv.dtype)] + tile_shapes(steps, jnp.bfloat16),
        steps, 20_000_000_000,
    )
    return out, shares


def attend_back(plan, qkv, g, shares, first):
    rows, span, width = qkv.shape
    out, *grads = call(
        functools.partial(backward_kernel, first), "attend_back", plan, (qkv, g, *shares),
        [of_row((span, width), first), of_row((span, width // 3), first)] + tile_specs(first, first),
        [of_row((span, width))] + tile_specs(first),
        [jax.ShapeDtypeStruct((1, span, width), qkv.dtype)] + tile_shapes(RECEIPTS, jnp.bfloat16),
        RECEIPTS, 12_000_000_000,
    )
    return out, grads


def make_bins(plan, index, grads, first):
    out = (16, HEADS * 64)
    return call(
        functools.partial(bins_kernel, first), "make_bins", plan, (index, *grads),
        [of_step((TALL, WIDE), first)] + tile_specs(first),
        fixed(out),
        jax.ShapeDtypeStruct(out, jnp.float32),
        RECEIPTS, 12_000_000_000, [pltpu.VMEM((2, TALL * 16, 128), jnp.float32)],
    )


def make_plan(starts):
    first, last = starts[:, :-1], starts[:, 1:]
    span = last - first // 16 * 16
    order = jnp.arange(RECEIPTS, dtype=jnp.int32)

    def latest(need):
        passed = need[:, None, :] & (order[None, :] <= order[:, None])[None]
        behind = jnp.max(jnp.where(passed, order, -1), axis=2)
        ahead = jnp.min(jnp.where(need, order, RECEIPTS - 1), axis=1, keepdims=True)
        return jnp.where(behind < 0, ahead, behind)

    bounds = jnp.pad(starts, ((0, 0), (0, 15 - RECEIPTS)))
    return jnp.concatenate([bounds, latest(span > 64), latest(span > 128)], axis=1).reshape(-1)


EPSILON = 1e-05


def gelu_parts(u):
    expo = jnp.exp(u * u * -0.5)
    share = 0.5 + 0.5 * lax.erf(u * (1.0 / math.sqrt(2.0)))
    return u * share, share + u * expo * (1.0 / math.sqrt(2.0 * math.pi))


def standard(values):
    centred = values - jnp.mean(values, axis=1, keepdims=True)
    scale = lax.rsqrt(jnp.mean(centred * centred, axis=1, keepdims=True) + EPSILON)
    return centred * scale, scale


def standard_back(normed, scale, grad):
    return (
        grad - jnp.mean(grad, axis=1, keepdims=True) - normed * jnp.mean(grad * normed, axis=1, keepdims=True)
    ) * scale


def total(value):
    return jnp.sum(value, axis=0, keepdims=True)


def sorted_sum(moving, parts):
    value, at = 0.0, 0
    for part in parts:
        count = part.shape[1]
        value = value + dot(moving[:, at : at + count], part[0], 1, 0)
        at += count
    return value


def enter_kernel(*refs):
    count = len(refs) - 9
    moving_ref, *part_refs = refs[: count + 1]
    features_ref, w_visual_ref, b_visual_ref, w_qkv_ref, b_qkv_ref, stream_ref, low_ref, qkv_ref = refs[count + 1 :]
    moving = moving_ref[0]
    text = sum(ref.shape[1] for ref in part_refs)
    at_visual = moving[:, text:]
    features = dot(at_visual, features_ref[0], 1, 0).astype(jnp.bfloat16)
    lane = lax.broadcasted_iota(jnp.int32, at_visual.shape, 1)
    is_visual = jnp.sum(jnp.where(lane < VISUAL, at_visual.astype(jnp.float32), 0.0), axis=1, keepdims=True)
    visual = dot(features, w_visual_ref[...], 1, 0) + b_visual_ref[...]
    stream = sorted_sum(moving, part_refs) + visual * is_visual
    stream_ref[...] = stream
    low = stream.astype(jnp.bfloat16)
    low_ref[...] = low
    qkv_ref[...] = (dot(low, w_qkv_ref[...], 1, 0) + b_qkv_ref[...]).astype(jnp.bfloat16)


def by_half(shape):
    return pl.BlockSpec((1,) + shape, lambda n: (n // 2, 0, 0))


def enter(moving, parts, features, w_visual, b_visual, w_qkv, b_qkv):
    rows = moving.shape[0]
    width = w_visual.shape[1]
    tile = SPAN // 2
    tokens = rows * SPAN
    return pl.pallas_call(
        enter_kernel,
        grid=(2 * rows,),
        in_specs=[pl.BlockSpec((1, tile, SPAN), lambda n: (n // 2, n % 2, 0))]
        + [by_half(part.shape[1:]) for part in (*parts, features)]
        + [whole(value.shape) for value in (w_visual, b_visual, w_qkv, b_qkv)],
        out_specs=[tiled(tile, width), tiled(tile, width), tiled(tile, 3 * width)],
        out_shape=[
            jax.ShapeDtypeStruct((tokens, width), jnp.float32),
            jax.ShapeDtypeStruct((tokens, width), jnp.bfloat16),
            jax.ShapeDtypeStruct((tokens, 3 * width), jnp.bfloat16),
        ],
        compiler_params=pltpu.CompilerParams(vmem_limit_bytes=48 * 1024 * 1024),
        cost_estimate=pl.CostEstimate(flops=8_000_000_000, bytes_accessed=20_000_000, transcendentals=0),
        name="enter",
    )(moving, *parts, features, w_visual, b_visual, w_qkv, b_qkv)


def up_kernel(context_ref, stream_ref, w_out_ref, w_up_ref, w_down_ref, rows_ref, b_up_ref, moving_ref, *refs, chunk):
    part_refs = refs[:-8]
    mid_ref, hidden_ref, active_ref, slope_ref, out_ref, top_ref, branch_ref, sums_ref = refs[-8:]
    b_out, gain_1, shift_1, b_down, gain_2, shift_2 = (rows_ref[n : n + 1, :] for n in range(6))
    mid = stream_ref[...] + dot(context_ref[...], w_out_ref[...], 1, 0) + b_out
    mid_ref[...] = mid
    norm_one = standard(mid)[0] * gain_1 + shift_1
    hidden = norm_one.astype(jnp.bfloat16)
    hidden_ref[...] = hidden
    branch = norm_one + b_down
    for at in range(0, w_up_ref.shape[1], chunk):
        piece = slice(at, at + chunk)
        inner = dot(hidden, w_up_ref[:, piece], 1, 0) + b_up_ref[:, piece]
        active, slope = gelu_parts(inner)
        active = active.astype(jnp.bfloat16)
        active_ref[:, piece] = active
        slope_ref[:, piece] = slope.astype(jnp.bfloat16)
        branch = branch + dot(active, w_down_ref[piece, :], 1, 0)
    normed, scale = standard(branch)
    out_ref[...] = (normed * gain_2 + shift_2).astype(jnp.bfloat16)
    cot = sorted_sum(moving_ref[0], part_refs)
    top = standard_back(normed, scale, cot * gain_2)
    top_ref[...] = top
    low = top.astype(jnp.bfloat16)
    branch_ref[...] = low

    @pl.when(pl.program_id(0) == 0)
    def _():
        sums_ref[...] = jnp.zeros_like(sums_ref)

    sums_ref[0:1, :] += total(cot * normed)
    sums_ref[1:2, :] += total(cot)
    sums_ref[2:3, :] += total(low.astype(jnp.float32))


def down_kernel(
    branch_ref, slope_ref, top_ref, mid_ref, w_out_ref, w_up_ref, w_down_ref, rows_ref,
    inner_ref, mid_grad_ref, attended_ref, context_ref, sums_ref, ups_ref, *, chunk,
):
    @pl.when(pl.program_id(0) == 0)
    def _():
        sums_ref[...] = jnp.zeros_like(sums_ref)
        ups_ref[...] = jnp.zeros_like(ups_ref)

    gain_1 = rows_ref[1:2, :]
    branch = branch_ref[...]
    grad = top_ref[...]
    for at in range(0, w_up_ref.shape[1], chunk):
        piece = slice(at, at + chunk)
        inner = dot(branch, w_down_ref[piece, :], 1, 1) * slope_ref[:, piece].astype(jnp.float32)
        low = inner.astype(jnp.bfloat16)
        inner_ref[:, piece] = low
        ups_ref[0:1, piece] += total(low.astype(jnp.float32))
        grad = grad + dot(low, w_up_ref[:, piece], 1, 1)
    normed, scale = standard(mid_ref[...])
    back = standard_back(normed, scale, grad * gain_1)
    mid_grad_ref[...] = back
    low = back.astype(jnp.bfloat16)
    attended_ref[...] = low
    context_ref[...] = dot(low, w_out_ref[...], 1, 1).astype(jnp.bfloat16)
    sums_ref[0:1, :] += total(grad * normed)
    sums_ref[1:2, :] += total(grad)
    sums_ref[2:3, :] += total(low.astype(jnp.float32))


def tiled(tile, width):
    return pl.BlockSpec((tile, width), lambda n: (n, 0))


def whole(shape):
    return pl.BlockSpec(shape, lambda n: (0, 0))


def feed_forward(context, stream_in, moving, cots, w_out, w_up, w_down, vectors, b_up, chunk=768):
    tokens, width = context.shape
    tile = SPAN // 2
    deep = w_up.shape[1]
    low, full = jnp.bfloat16, jnp.float32
    shapes = [(width, full), (width, low), (deep, low), (deep, low), (width, low), (width, full), (width, low)]
    return pl.pallas_call(
        functools.partial(up_kernel, chunk=chunk),
        grid=(tokens // tile,),
        in_specs=[tiled(tile, width)] * 2
        + [whole(w_out.shape), whole(w_up.shape), whole(w_down.shape), whole(vectors.shape), whole(b_up.shape)]
        + [pl.BlockSpec((1, tile, SPAN), lambda n: (n // 2, n % 2, 0))]
        + [by_half(part.shape[1:]) for part in cots],
        out_specs=[tiled(tile, n) for n, _ in shapes] + [whole((8, width))],
        out_shape=[jax.ShapeDtypeStruct((tokens, n), kind) for n, kind in shapes]
        + [jax.ShapeDtypeStruct((8, width), full)],
        compiler_params=pltpu.CompilerParams(vmem_limit_bytes=60 * 1024 * 1024),
        cost_estimate=pl.CostEstimate(flops=20_000_000_000, bytes_accessed=60_000_000, transcendentals=0),
        name="feed_forward",
    )(context, stream_in, w_out, w_up, w_down, vectors, b_up, moving, *cots)


def feed_back(branch, slope, top, mid, w_out, w_up, w_down, vectors, tile=SPAN // 2, chunk=768):
    tokens, width = branch.shape
    deep = w_up.shape[1]
    low, full = jnp.bfloat16, jnp.float32
    shapes = [(deep, low), (width, full), (width, low), (width, low)]
    return pl.pallas_call(
        functools.partial(down_kernel, chunk=chunk),
        grid=(tokens // tile,),
        in_specs=[tiled(tile, width), tiled(tile, deep), tiled(tile, width), tiled(tile, width)]
        + [whole(w_out.shape), whole(w_up.shape), whole(w_down.shape), whole(vectors.shape)],
        out_specs=[tiled(tile, n) for n, _ in shapes] + [whole((8, width)), whole((8, deep))],
        out_shape=[jax.ShapeDtypeStruct((tokens, n), kind) for n, kind in shapes]
        + [jax.ShapeDtypeStruct((8, width), full), jax.ShapeDtypeStruct((8, deep), full)],
        compiler_params=pltpu.CompilerParams(vmem_limit_bytes=60 * 1024 * 1024),
        cost_estimate=pl.CostEstimate(flops=20_000_000_000, bytes_accessed=60_000_000, transcendentals=0),
        name="feed_back",
    )(branch, slope, top, mid, w_out, w_up, w_down, vectors)


DP = "dp"
STREAM = "stream"


def swap(value, axis, bit):
    count = lax.axis_size(axis)
    return lax.ppermute(value, axis, [(i, i ^ bit) for i in range(count)])


def bits_of(axis):
    count = lax.axis_size(axis)
    return [1 << n for n in range(count.bit_length() - 1)]


def rounds():
    core, *chips = bits_of(DP)
    groups = [(DP, [core])] + [(DP, chips[n : n + 2]) for n in range(0, len(chips), 2)]
    places = bits_of(STREAM)
    return groups + [(STREAM, places[n : n + 2]) for n in range(0, len(places), 2)]


def masks_of(bits):
    return [sum(bit for n, bit in enumerate(bits) if pick >> n & 1) for pick in range(1, 1 << len(bits))]


def add_all(kept, got):
    total = kept + got[0]
    return total + (got[1] + got[2]) if len(got) > 1 else total


class Scatter:
    def __init__(self, values):
        self.names = [(axis, bit) for axis in (DP, STREAM) for bit in bits_of(axis)[::-1]]
        self.values = [value.reshape((2,) * len(self.names) + value.shape[1:]) for value in values]
        self.left = rounds()

    def send(self):
        axis, bits = self.left.pop(0)
        place = lax.axis_index(axis)
        dims = {bit: self.names.index((axis, bit)) for bit in bits}

        def pick(value, mask):
            at = [0] * value.ndim
            size = list(value.shape)
            for bit, dim in dims.items():
                at[dim] = ((place ^ mask) // bit) % 2
                size[dim] = 1
            part = lax.dynamic_slice(value, at, size)
            return part.reshape([n for dim, n in enumerate(size) if dim not in dims.values()])

        self.kept = [pick(value, 0) for value in self.values]
        self.got = [
            swap(jnp.concatenate([pick(value, mask) for value in self.values], axis=-1), axis, mask)
            for mask in masks_of(bits)
        ]
        self.names = [name for name in self.names if name[0] != axis or name[1] not in bits]

    def add(self):
        if not self.got:
            return
        values, at = [], 0
        for kept in self.kept:
            got = [part[..., at : at + kept.shape[-1]].astype(jnp.float32) for part in self.got]
            at += kept.shape[-1]
            value = add_all(kept.astype(jnp.float32), got)
            values.append(value.astype(jnp.bfloat16) if self.left else value)
        self.values, self.got = values, []

    def next(self):
        self.add()
        if self.left:
            self.send()

    def finish(self):
        while self.left:
            self.next()
        self.add()
        return self.values


def advance(value, groups, extra=()):
    tied, got, held = lax.optimization_barrier((value, [group.got for group in groups], list(extra)))
    for group, parts in zip(groups, got):
        group.got = parts
        group.next()
    return tied, held


def together(*values):
    return lax.optimization_barrier(values)


def sum_all(value):
    for axis, bits in rounds():
        value = add_all(value, [swap(value, axis, mask) for mask in masks_of(bits)])
    return value


def turned(shift):
    count = lax.axis_size(STREAM)
    return [(i, (i + shift) % count) for i in range(count)]


def to_rows(value):
    count = lax.axis_size(STREAM)
    place = lax.axis_index(STREAM)
    block = value.shape[0] // count
    parts = []
    for shift in range(count):
        part = lax.dynamic_slice_in_dim(value, (place - shift) % count * block, block, 0)
        parts.append(lax.ppermute(part, STREAM, turned(-shift)) if shift else part)
    return parts


def slot_sends(value):
    count = lax.axis_size(STREAM)
    block = value.shape[1] // count
    parts = [value[:, shift * block : (shift + 1) * block] for shift in range(count)]
    return parts[:1] + [lax.ppermute(parts[shift], STREAM, turned(shift)) for shift in range(1, count)]


def from_sends(groups, dtype):
    count = lax.axis_size(STREAM)
    place = lax.axis_index(STREAM)
    rows = sum(parts[0].shape[0] for parts in groups)
    whole_value = jnp.zeros((rows * count,) + groups[0][0].shape[1:], dtype)
    at = 0
    for parts in groups:
        for shift, part in enumerate(parts):
            spot = (place - shift) % count * rows + at
            whole_value = lax.dynamic_update_slice_in_dim(whole_value, part.astype(dtype), spot, 0)
        at += parts[0].shape[0]
    return whole_value


def per_device(
    text_input,
    visual_features,
    receipt_text,
    receipt_visual,
    boxes,
    w_query,
    b_query,
    w_key,
    w_value,
    b_value,
    w_out,
    b_out,
    gain_attn,
    shift_attn,
    w_up,
    b_up,
    w_down,
    b_down,
    gain_ffn,
    shift_ffn,
    w_visual,
    b_visual,
    table_line,
    table_x,
    table_y,
    cotangent_text,
    cotangent_visual,
):
    floating = jnp.float32
    narrow = jnp.bfloat16
    width = text_input.shape[-1]
    rows, visual, channels = visual_features.shape
    text = receipt_text.shape[1]
    slots = text + visual
    world = lax.axis_size(DP) * lax.axis_size(STREAM)
    place = lax.axis_index(STREAM)
    first_row = place * rows

    text_parts = to_rows(text_input)
    text_parts, cotangent_text = lax.optimization_barrier((text_parts, cotangent_text))
    cotangent_parts = to_rows(cotangent_text)

    def pad(value, fill=0, size=SPAN):
        extra = size - value.shape[1]
        return jnp.pad(value, ((0, 0), (0, extra)) + ((0, 0),) * (value.ndim - 2), constant_values=fill)

    seg_text = lax.dynamic_slice_in_dim(receipt_text, first_row, rows, 0)
    seg_visual = lax.dynamic_slice_in_dim(receipt_visual, first_row, rows, 0)
    box = lax.dynamic_slice_in_dim(boxes, first_row, rows, 1)
    index = jnp.arange(SPAN, dtype=jnp.int32)
    position = jnp.where(index < text, index, index - text)
    facts = jnp.stack(
        [
            jnp.broadcast_to(position, (rows, SPAN)),
            pad(box[0]),
            pad(box[1]),
            pad(jnp.concatenate([seg_text, seg_visual], axis=1), RECEIPTS),
            jnp.broadcast_to(index, (rows, SPAN)),
        ],
        axis=1,
    )
    own = lax.dynamic_slice_in_dim(
        jnp.concatenate([facts[:, :, :text], facts[:, :, :text]], axis=2), place * text_input.shape[1], text, 2
    )
    facts = jnp.concatenate([own, facts[:, :, text:]], axis=2)
    rank = facts[:, 3] * SPAN + facts[:, 4]
    seg = facts[:, 3]
    target = jnp.sum((rank[:, None, :] < rank[:, :, None]).astype(jnp.int32), axis=2)
    moved = target[:, None, :] == index[None, :, None]
    facts = facts[:, :4]
    facts = jnp.sum(jnp.where(moved[:, None], facts[:, :, None, :], 0), axis=3)
    col = jnp.pad(jnp.swapaxes(facts, 1, 2), ((0, 0), (0, 0), (0, 124)))
    row = jnp.pad(facts, ((0, 0), (0, 4), (0, 640 - SPAN)), constant_values=RECEIPTS)
    starts = jnp.sum(
        (seg[:, None, :] < jnp.arange(RECEIPTS + 1, dtype=jnp.int32)[None, :, None]).astype(jnp.int32), axis=2
    )
    plan = make_plan(starts)
    plane = jnp.concatenate([table_x, table_y], axis=1).astype(floating)
    lines = jnp.pad(table_line.astype(floating), ((0, 0), (0, 96)), constant_values=NONE)

    bias, places = make_bias(plan, col, row, plane, lines)
    moving = moved.astype(narrow)

    def unsort(value):
        return jnp.einsum("rps,rpd->rsd", moving, value, preferred_element_type=floating)

    def rowwise(array):
        return array.reshape(rows, SPAN, -1)

    w_qkv = jnp.concatenate([w_query, w_key, w_value], axis=1)
    b_qkv = jnp.concatenate([b_query, jnp.zeros_like(b_query), b_value]).astype(floating)
    stream_in, entered, qkv = enter(
        moving, text_parts, pad(visual_features, 0, SPAN - text), w_visual, b_visual.astype(floating)[None],
        w_qkv, b_qkv[None],
    )
    qkv = rowwise(qkv)
    context, shares = attend(plan, qkv, row, bias)
    context, cotangent_parts = lax.optimization_barrier((context, cotangent_parts))
    context = context.reshape(-1, width)
    vectors = jnp.stack([b_out, gain_attn, shift_attn, b_down, gain_ffn, shift_ffn, b_out, b_out]).astype(floating)
    mid, hidden, active, slope, outcome, grad_top, grad_branch, ffn_sums = feed_forward(
        context, stream_in, moving, cotangent_parts + [pad(cotangent_visual, 0, SPAN - text)],
        w_out, w_up, w_down, vectors, b_up.astype(floating)[None],
    )

    def weight_grad(left, right):
        return jnp.einsum("ti,tj->ij", left, right, preferred_element_type=floating)

    def chunks(part):
        return part.astype(narrow).reshape(world, part.shape[0] // world, -1)

    grad_w_down = chunks(weight_grad(active, grad_branch))
    grad_w_down, grad_branch, outcome = together(grad_w_down, grad_branch, outcome)
    downs = Scatter([grad_w_down])
    downs.send()
    out_rows = unsort(rowwise(outcome)).astype(narrow)
    out_visual = out_rows[:, text:slots]
    (grad_branch, out_rows), _ = advance((grad_branch, out_rows), [downs])
    out_sends = slot_sends(out_rows[:, :text])
    grad_inner, grad_mid, grad_attended, grad_context, attn_sums, up_sums = feed_back(
        grad_branch, slope, grad_top, mid, w_out, w_up, w_down, vectors
    )
    grad_inner, out_sends, downs.got = lax.optimization_barrier((grad_inner, out_sends, downs.got))
    grad_w_up = chunks(weight_grad(hidden, grad_inner))
    grad_w_out = chunks(weight_grad(context, grad_attended))
    grad_context, grad_w_out, grad_w_up = together(grad_context, grad_w_out, grad_w_up)
    ups = Scatter([grad_w_up, grad_w_out])
    ups.send()
    grad_context, out_sends = advance(rowwise(grad_context), [downs], out_sends)
    out_text = from_sends([out_sends], narrow)

    entered_rows, grad_mid_rows = rowwise(entered), rowwise(grad_mid)

    def project(r, grad_qkv):
        grad_stream = grad_mid_rows[r] + jnp.einsum("te,de->td", grad_qkv, w_qkv, preferred_element_type=floating)
        (grad_low,) = together(grad_stream.astype(narrow))
        return jnp.einsum("ps,pd->sd", moving[r], grad_low, preferred_element_type=floating).astype(narrow)

    grad_qkv_0, step_0 = attend_back(plan, qkv, grad_context, shares, 0)
    grad_qkv_0, _ = advance(grad_qkv_0[0], [ups, downs])
    (down_sum,) = downs.finish()
    back_0 = project(0, grad_qkv_0)
    got_0 = slot_sends(back_0[None, :text])
    grad_w_qkv = weight_grad(entered_rows[0], grad_qkv_0)
    grad_b_qkv = jnp.sum(grad_qkv_0, axis=0, dtype=floating)
    grad_context, back_0, grad_w_qkv = together(grad_context, back_0, grad_w_qkv)
    grad_qkv_1, step_1 = attend_back(plan, qkv, grad_context, shares, 1)
    grad_qkv_1, got_0 = advance(grad_qkv_1[0], [ups], got_0)
    back_1 = project(1, grad_qkv_1)
    grad_w_qkv = grad_w_qkv + weight_grad(entered_rows[1], grad_qkv_1)
    grad_b_qkv = grad_b_qkv + jnp.sum(grad_qkv_1, axis=0, dtype=floating)
    grad_visual = jnp.stack([back_0[text:slots], back_1[text:slots]])
    grad_w_visual = jnp.einsum("rvc,rvd->cd", visual_features, grad_visual, preferred_element_type=floating)
    grad_b_visual = jnp.sum(grad_visual, axis=(0, 1), dtype=floating)
    grad_features = jnp.einsum("rvd,cd->rvc", grad_visual, w_visual, preferred_element_type=floating)
    lasts = Scatter([chunks(grad_w_qkv), grad_w_visual.astype(narrow).reshape(world, width // world, -1)])
    lasts.send()
    back_1, lasts.kept = lax.optimization_barrier((back_1, lasts.kept))
    got_1 = slot_sends(back_1[None, :text])
    step_0, _ = advance(step_0, [lasts])
    bins = make_bins(plan, places, step_0, 0)
    bins, got_1 = advance(bins, [ups, lasts], got_1)
    step_1, bins = lax.optimization_barrier((step_1, bins))
    more = make_bins(plan, places, step_1, 1)
    more, _ = advance(more, [lasts])
    bins = bins + more
    up_sum, out_sum = ups.finish()
    qkv_sum, visual_sum = lasts.finish()
    grad_text = from_sends([got_0, got_1], floating)
    query_sum, key_sum, value_sum = (qkv_sum[:, n * width : (n + 1) * width] for n in range(3))
    visual_sum = visual_sum.reshape(-1, width)
    step = width // world
    def lines_of(value):
        return [value[:, n : n + width] for n in range(0, value.shape[1], width)]

    small = sum_all(
        jnp.concatenate(
            [ffn_sums, attn_sums, bins]
            + lines_of(grad_b_qkv[None]) + [grad_b_visual[None]] + lines_of(up_sums[:1]),
            axis=0,
        )
    )
    device = lax.axis_index(DP) * lax.axis_size(STREAM) + place
    mine = lax.dynamic_slice_in_dim(small, device * step, step, 1)
    up_step = w_up.shape[1] // world
    bins = small[16 : 16 + HEADS]
    return (
        out_text,
        out_visual,
        grad_text,
        grad_features,
        query_sum,
        mine[32],
        key_sum,
        value_sum,
        mine[34],
        out_sum,
        mine[10],
        mine[8],
        mine[9],
        up_sum,
        lax.dynamic_slice_in_dim(small[36:].reshape(-1), device * up_step, up_step, 0),
        down_sum,
        mine[2],
        mine[0],
        mine[1],
        visual_sum,
        mine[35],
        bins[:, 128:160],
        bins[:, :64],
        bins[:, 64:128],
    )


def solution(mesh):
    placed = (
        P("dp", "stream", None),
        P(("dp", "stream"), None, None),
        P("dp", None),
        P("dp", None),
        P(None, "dp", None),
        P(),
        P(),
        P(),
        P(),
        P(),
        P(),
        P(),
        P(),
        P(),
        P(),
        P(),
        P(),
        P(),
        P(),
        P(),
        P(),
        P(),
        P(),
        P(),
        P(),
        P("dp", "stream", None),
        P(("dp", "stream"), None, None),
    )
    return jax.shard_map(
        per_device,
        mesh=mesh,
        in_specs=placed,
        out_specs=(
            P("dp", "stream", None),
            P(("dp", "stream"), None, None),
            P("dp", "stream", None),
            P(("dp", "stream"), None, None),
            P(("dp", "stream"), None),
            P(("dp", "stream")),
            P(("dp", "stream"), None),
            P(("dp", "stream"), None),
            P(("dp", "stream")),
            P(("dp", "stream"), None),
            P(("dp", "stream")),
            P(("dp", "stream")),
            P(("dp", "stream")),
            P(("dp", "stream"), None),
            P(("dp", "stream")),
            P(("dp", "stream"), None),
            P(("dp", "stream")),
            P(("dp", "stream")),
            P(("dp", "stream")),
            P(("dp", "stream"), None),
            P(("dp", "stream")),
            P(),
            P(),
            P(),
        ),
        check_vma=False,
    )
```

```python
import functools
import math

import jax, jax.numpy as jnp
from jax import lax
from jax.experimental import pallas as pl
from jax.experimental.pallas import tpu as pltpu
from jax.sharding import PartitionSpec as P

HEADS = 12
RECEIPTS = 8
VISUAL = 49
PLAN = 32
SPAN = 576
BINS = 160
NONE = -1e30
TALL = 192
WIDE = 256
FORWARD_PAIRS = 6
BACKWARD_PAIRS = 6


def thresholds(half, reach):
    exact = half // 2
    steps = half - exact
    return [
        int(math.floor(exact * (reach / exact) ** (power / steps) + 0.5))
        for power in range(1, steps)
    ]


def bucket(diff, count, reach):
    half = count // 2
    exact = half // 2
    dist = jnp.abs(diff)
    passed = jnp.where(diff > 0, half, 0)
    for limit in thresholds(half, reach):
        passed = passed + jnp.where(dist >= limit, 1, 0)
    return passed + jnp.minimum(dist, exact)


def dot(a, b, ca, cb):
    return lax.dot_general(a, b, (((ca,), (cb,)), ((), ())), preferred_element_type=jnp.float32)


def by_size(plan_ref, run, offset=0):
    step = pl.program_id(0)
    receipt = lax.rem(step, RECEIPTS)
    base = (step // RECEIPTS + offset) * PLAN + receipt
    first = plan_ref[base]
    last = plan_ref[base + 1]
    start = first // 16 * 16
    low = 0
    for tall in (64, 96, 128, 160, 192):
        wide = 128 if tall <= 128 else 256
        inside = last - start > low
        if tall < TALL:
            inside = jnp.logical_and(inside, last - start <= tall)
        low = tall

        @pl.when(inside)
        def _(tall=tall, wide=wide):
            at_k = pl.multiple_of(jnp.minimum(start, SPAN - tall), 16)
            at_q = pl.multiple_of(jnp.minimum(start, SPAN - wide), 16)
            run(receipt, first - at_k, last - at_k, at_k, at_q, tall, wide)


def blocks(refs, head, tile, tall):
    found = []
    for n, (which, lead) in enumerate((((0, ()), (1, ()), (2, (0,))), ((2, (1,)), (2, (2,)), (2, (3,))))[tile]):
        size = min(64, tall - 64 * n)
        if size > 0:
            found.append((refs[which], (0,) + lead + (head, pl.ds(0, size)), 64 * n, size))
    return found


def load(refs, head, tall, wide):
    return joined(
        [joined([ref[at] for ref, at, _, _ in blocks(refs, head, tile, tall)], 0) for tile in range(wide // 128)], 1
    )


def store(refs, head, value):
    tall, wide = value.shape
    for tile in range(wide // 128):
        for ref, at, row, size in blocks(refs, head, tile, tall):
            ref[at] = value[row : row + size, 128 * tile : 128 * tile + 128]


def joined(pieces, axis):
    return pieces[0] if len(pieces) == 1 else jnp.concatenate(pieces, axis=axis)


def bias_kernel(plan_ref, col_ref, row_ref, plane_ref, lines_ref, near_ref, mid_ref, far_ref, index_ref):
    refs = (near_ref, mid_ref, far_ref)
    height = 32

    def run(receipt, low, high, at_k, at_q, tall, wide):
        row = pltpu.roll(row_ref[0], lax.rem(640 - at_q, 640), 1)[:, :wide]
        shape = (height, 128)

        def fill(tile, n, at):
            _, lead = (((0, ()), (1, ()), (2, (0,))), ((2, (1,)), (2, (2,)), (2, (3,))))[tile][n]
            ref = refs[(((0, 1, 2), (2, 2, 2))[tile])[n]]
            lanes = slice(128 * tile, 128 * (tile + 1))
            here = pl.multiple_of(64 * n + at, height)
            used = jnp.logical_and(here < high, here + height > low)

            @pl.when(jnp.logical_not(used))
            def _():
                for h in range(HEADS):
                    ref[(0,) + lead + (h, pl.ds(at, height))] = jnp.full(shape, NONE, jnp.float32)

            @pl.when(used)
            def _():
                col = col_ref[0, pl.ds(pl.multiple_of(at_k + here, 16), height), :]

                def spread(r):
                    return (jnp.broadcast_to(col[:, r : r + 1], shape), jnp.broadcast_to(row[r : r + 1, lanes], shape))

                def gap(r):
                    key, query = spread(r)
                    return key - query

                key, query = spread(3)
                same = jnp.logical_and(key == receipt, query == receipt)
                line = jnp.where(same, bucket(gap(0), 32, 128), 32)
                across = bucket(gap(1), 64, 256)
                down = bucket(gap(2), 64, 256) + 64
                index_ref[0, pl.ds(here, height), lanes] = across + down * 256 + line * 65536
                def look(table_ref, h, index):
                    table = jnp.broadcast_to(table_ref[h : h + 1, :], (8, 128))
                    return jnp.take_along_axis(table, index, axis=1, mode="promise_in_bounds")
                for r in range(height // 8):
                    a8, d8, l8 = (v[8 * r : 8 * r + 8] for v in (across, down, line))

                    xs = [look(plane_ref, h, a8) for h in range(HEADS)]
                    ys = [look(plane_ref, h, d8) for h in range(HEADS)]
                    ls = [look(lines_ref, h, l8) for h in range(HEADS)]
                    for h in range(HEADS):
                        ref[(0,) + lead + (h, pl.ds(at + 8 * r, 8))] = xs[h] + ys[h] + ls[h]

        for tile in range(wide // 128):
            for n in range(pl.cdiv(tall, 64)):
                def step(m, carry, tile=tile, n=n):
                    fill(tile, n, pl.multiple_of(m * height, height))
                    return carry

                lax.fori_loop(0, 2, step, 0)

    by_size(plan_ref, run)


def split_pair(value, scale=1.0):
    lane = lax.broadcasted_iota(jnp.int32, value.shape, 1)
    full = value.astype(jnp.float32) * scale
    low = jnp.where(lane < 64, full, 0.0).astype(value.dtype)
    high = jnp.where(lane < 64, 0.0, full).astype(value.dtype)
    return jnp.concatenate([low, high], axis=0)


def grouped(size):
    return [range(n, n + size) for n in range(0, HEADS // 2, size)]


def parts(pair, at_k, at_q, tall, wide):
    width = HEADS * 64
    return (
        (0, pl.ds(at_q, wide), pl.ds(128 * pair, 128)),
        (0, pl.ds(at_k, tall), pl.ds(width + 128 * pair, 128)),
        (0, pl.ds(at_k, tall), pl.ds(2 * width + 128 * pair, 128)),
    )


def gather_into(ref, where, value):
    ref[where] = (ref[where].astype(jnp.float32) + value).astype(ref.dtype)


def forward_kernel(plan_ref, qkv_ref, row_ref, *refs):
    bias_refs, out_ref, shares_refs = refs[:3], refs[3], refs[4:]

    @pl.when(lax.rem(pl.program_id(0), RECEIPTS) == 0)
    def _():
        out_ref[...] = jnp.zeros_like(out_ref)

    def run(receipt, low, high, at_k, at_q, tall, wide):
        owner = pltpu.roll(row_ref[0], lax.rem(640 - at_q, 640), 1)[3:4, :wide]
        mine = jnp.where(owner == receipt, 1.0, 0.0)
        for group in grouped(FORWARD_PAIRS):
            spots = [parts(pair, at_k, at_q, tall, wide) for pair in group]
            scores = [
                dot(split_pair(qkv_ref[keys], 0.125), qkv_ref[queries], 1, 1) for queries, keys, _ in spots
            ]
            shares = []
            for pair, score in zip(group, scores):
                halves = []
                for h in range(2):
                    part = score[h * tall : (h + 1) * tall] + load(bias_refs, 2 * pair + h, tall, wide)
                    expo = jnp.exp(part - jnp.max(part, axis=0, keepdims=True))
                    share = expo * (mine / jnp.sum(expo, axis=0, keepdims=True))
                    halves.append(share.astype(jnp.bfloat16))
                    store(shares_refs, 2 * pair + h, halves[h])
                shares.append(jnp.concatenate(halves, axis=0))
            results = [dot(share, split_pair(qkv_ref[values]), 0, 0) for share, (_, _, values) in zip(shares, spots)]
            for result, (queries, _, _) in zip(results, spots):
                gather_into(out_ref, queries, result)

    by_size(plan_ref, run)


def backward_kernel(offset, plan_ref, qkv_ref, g_ref, index_ref, *refs):
    shares_refs, (dqkv_ref, bins_ref, terms_s) = refs[:3], refs[3:]

    @pl.when(pl.program_id(0) == 0)
    def _():
        bins_ref[...] = jnp.zeros_like(bins_ref)
        terms_s[...] = jnp.zeros_like(terms_s)


    @pl.when(lax.rem(pl.program_id(0), RECEIPTS) == 0)
    def _():
        dqkv_ref[...] = jnp.zeros_like(dqkv_ref)

    def run(receipt, low, high, at_k, at_q, tall, wide):
        for group in grouped(BACKWARD_PAIRS):
            spots = [parts(pair, at_k, at_q, tall, wide) for pair in group]
            grads = [g_ref[queries] for queries, _, _ in spots]
            parts_of = [
                dot(split_pair(qkv_ref[values]), grad, 1, 1) for grad, (_, _, values) in zip(grads, spots)
            ]
            shares, steps = [], []
            for pair, grad_probs in zip(group, parts_of):
                for h in range(2):
                    share = load(shares_refs, 2 * pair + h, tall, wide)
                    part = grad_probs[h * tall : (h + 1) * tall]
                    probs = share.astype(jnp.float32)
                    inner = jnp.sum(probs * part, axis=0, keepdims=True)
                    step = (probs * (part - inner)).astype(jnp.bfloat16)
                    wide_step = step.astype(jnp.float32)
                    for c in range(wide // 128):
                        lanes = slice(128 * c, 128 * c + 128)
                        terms_s[c, pl.ds(2 * pair + h, tall, stride=16), :] = wide_step[:, lanes]
                    shares.append(share)
                    steps.append(step)
            results = []
            for n, (queries, keys, values) in enumerate(spots):
                pair = slice(2 * n, 2 * n + 2)
                results.append((values, dot(jnp.concatenate(shares[pair], axis=1), split_pair(grads[n]), 1, 0)))
                query = split_pair(qkv_ref[queries], 0.125)
                results.append((keys, dot(jnp.concatenate(steps[pair], axis=1), query, 1, 0)))
                key = split_pair(qkv_ref[keys], 0.125)
                results.append((queries, dot(jnp.concatenate(steps[pair], axis=0), key, 0, 0)))
            for where, result in results:
                gather_into(dqkv_ref, where, result)

        group = 32
        level = lax.broadcasted_iota(jnp.int32, (BINS, 128), 0)

        def bin_step(n, total):
            hots, terms = [], []
            at = pl.multiple_of(n * group, group)
            for c in range(wide // 128):
                packed = index_ref[0, pl.ds(at, group), 128 * c : 128 * c + 128]
                x, y, line = packed & 255, (packed >> 8) & 255, (packed >> 16) + 128
                for i in range(group):
                    def spread(value, count):
                        return jnp.broadcast_to(value[i : i + 1, :], (count, 128))

                    index = jnp.concatenate([spread(x, 64), spread(y, 64), spread(line, 32)], axis=0)
                    hots.append(jnp.where(level == index, 1.0, 0.0).astype(jnp.bfloat16))
                    terms.append(terms_s[c, pl.ds(pl.multiple_of((at + i) * 16, 16), 16), :].astype(jnp.bfloat16))
            return total + dot(jnp.concatenate(terms, axis=1), jnp.concatenate(hots, axis=1), 1, 1)

        total = lax.fori_loop(low // group, pl.cdiv(high, group), bin_step, jnp.zeros((16, BINS), jnp.float32))
        bins_ref[:, :BINS] += total


    by_size(plan_ref, run, offset)


def of_row(shape, offset=0):
    return pl.BlockSpec((1,) + shape, lambda n, *_: (n // RECEIPTS + offset,) + (0,) * len(shape))


def of_step(shape, offset=0):
    return pl.BlockSpec((1,) + shape, lambda n, *_: (n + offset * RECEIPTS,) + (0,) * len(shape))


def of_plan(shape, offset, base, at):
    def place(n, plan_ref):
        row = n // RECEIPTS
        step = plan_ref[(row + offset) * PLAN + at + lax.rem(n, RECEIPTS)]
        return ((row + base) * RECEIPTS + step,) + (0,) * len(shape)

    return pl.BlockSpec((1,) + shape, place)


def tile_specs(offset=0, base=0):
    near, far = (HEADS, 64, 128), (4, HEADS, 64, 128)
    return [of_step(near, base), of_plan(near, offset, base, 16), of_plan(far, offset, base, 24)]


def tile_shapes(steps, kind):
    shapes = ((HEADS, 64, 128), (HEADS, 64, 128), (4, HEADS, 64, 128))
    return [jax.ShapeDtypeStruct((steps,) + shape, kind) for shape in shapes]


def fixed(shape):
    return pl.BlockSpec(shape, lambda n, *_: (0,) * len(shape))


def call(kernel, name, plan, args, in_specs, out_specs, out_shape, steps, cost, scratch=(), vmem=60):
    return pl.pallas_call(
        kernel,
        grid_spec=pltpu.PrefetchScalarGridSpec(
            num_scalar_prefetch=1, grid=(steps,), in_specs=in_specs, out_specs=out_specs, scratch_shapes=scratch
        ),
        out_shape=out_shape,
        compiler_params=pltpu.CompilerParams(vmem_limit_bytes=vmem * 1024 * 1024),
        cost_estimate=pl.CostEstimate(flops=cost, bytes_accessed=cost // 1000, transcendentals=0),
        name=name,
    )(plan, *args)


def make_bias(plan, col, row, plane, lines):
    steps = col.shape[0] * RECEIPTS
    *bias, index = call(
        bias_kernel, "make_bias", plan, (col, row, plane, lines),
        [of_row((SPAN, 128)), of_row((8, 640)), fixed((HEADS, 128)), fixed((HEADS, 128))],
        tile_specs() + [of_step((TALL, WIDE))],
        tile_shapes(steps, jnp.float32) + [jax.ShapeDtypeStruct((steps, TALL, WIDE), jnp.int32)],
        steps, 30_000_000_000,
    )
    return bias, index


def attend(plan, qkv, row, bias):
    rows, span, width = qkv.shape
    steps = rows * RECEIPTS
    out, *shares = call(
        forward_kernel, "attend", plan, (qkv, row, *bias),
        [of_row((span, width)), of_row((8, 640))] + tile_specs(),
        [of_row((span, width // 3))] + tile_specs(),
        [jax.ShapeDtypeStruct((rows, span, width // 3), qkv.dtype)] + tile_shapes(steps, jnp.bfloat16),
        steps, 20_000_000_000,
    )
    return out, shares


def attend_back(plan, qkv, g, index, shares, first):
    rows, span, width = qkv.shape
    bins = (16, width // 3)
    return call(
        functools.partial(backward_kernel, first), "attend_back", plan, (qkv, g, index, *shares),
        [of_row((span, width), first), of_row((span, width // 3), first), of_step((TALL, WIDE), first)]
        + tile_specs(first, first),
        [of_row((span, width)), fixed(bins)],
        [jax.ShapeDtypeStruct((1, span, width), qkv.dtype), jax.ShapeDtypeStruct(bins, jnp.float32)],
        RECEIPTS, 20_000_000_000, [pltpu.VMEM((2, TALL * 16, 128), jnp.float32)],
    )


def make_plan(starts):
    first, last = starts[:, :-1], starts[:, 1:]
    span = last - first // 16 * 16
    order = jnp.arange(RECEIPTS, dtype=jnp.int32)

    def latest(need):
        passed = need[:, None, :] & (order[None, :] <= order[:, None])[None]
        behind = jnp.max(jnp.where(passed, order, -1), axis=2)
        ahead = jnp.min(jnp.where(need, order, RECEIPTS - 1), axis=1, keepdims=True)
        return jnp.where(behind < 0, ahead, behind)

    bounds = jnp.pad(starts, ((0, 0), (0, 15 - RECEIPTS)))
    return jnp.concatenate([bounds, latest(span > 64), latest(span > 128)], axis=1).reshape(-1)


EPSILON = 1e-05


def gelu_parts(u):
    expo = jnp.exp(u * u * -0.5)
    share = 0.5 + 0.5 * lax.erf(u * (1.0 / math.sqrt(2.0)))
    return u * share, share + u * expo * (1.0 / math.sqrt(2.0 * math.pi))


def standard(values):
    centred = values - jnp.mean(values, axis=1, keepdims=True)
    scale = lax.rsqrt(jnp.mean(centred * centred, axis=1, keepdims=True) + EPSILON)
    return centred * scale, scale


def standard_back(normed, scale, grad):
    return (
        grad - jnp.mean(grad, axis=1, keepdims=True) - normed * jnp.mean(grad * normed, axis=1, keepdims=True)
    ) * scale


def total(value):
    return jnp.sum(value, axis=0, keepdims=True)


def sorted_sum(moving, parts):
    value, at = 0.0, 0
    for part in parts:
        count = part.shape[1]
        value = value + dot(moving[:, at : at + count], part[0], 1, 0)
        at += count
    return value


def enter_kernel(*refs):
    count = len(refs) - 11
    moving_ref, *part_refs = refs[: count + 1]
    features_ref, w_visual_ref, b_visual_ref, *w_refs, b_qkv_ref, stream_ref, low_ref, qkv_ref = refs[count + 1 :]
    moving = moving_ref[0]
    text = sum(ref.shape[1] for ref in part_refs)
    at_visual = moving[:, text:]
    features = dot(at_visual, features_ref[0], 1, 0).astype(jnp.bfloat16)
    lane = lax.broadcasted_iota(jnp.int32, at_visual.shape, 1)
    is_visual = jnp.sum(jnp.where(lane < VISUAL, at_visual.astype(jnp.float32), 0.0), axis=1, keepdims=True)
    visual = dot(features, w_visual_ref[...], 1, 0) + b_visual_ref[...]
    stream = sorted_sum(moving, part_refs) + visual * is_visual
    stream_ref[...] = stream
    low = stream.astype(jnp.bfloat16)
    low_ref[...] = low
    width = low.shape[1]
    for n, ref in enumerate(w_refs):
        lanes = slice(n * width, (n + 1) * width)
        qkv_ref[:, lanes] = (dot(low, ref[...], 1, 0) + b_qkv_ref[:, lanes]).astype(jnp.bfloat16)


def by_half(shape):
    return pl.BlockSpec((1,) + shape, lambda n: (n // 2, 0, 0))


def enter(moving, parts, features, w_visual, b_visual, weights, b_qkv):
    rows = moving.shape[0]
    width = w_visual.shape[1]
    tile = SPAN // 2
    tokens = rows * SPAN
    return pl.pallas_call(
        enter_kernel,
        grid=(2 * rows,),
        in_specs=[pl.BlockSpec((1, tile, SPAN), lambda n: (n // 2, n % 2, 0))]
        + [by_half(part.shape[1:]) for part in (*parts, features)]
        + [kept(value.shape) for value in (w_visual, b_visual, *weights, b_qkv)],
        out_specs=[tiled(tile, width), tiled(tile, width), tiled(tile, 3 * width)],
        out_shape=[
            jax.ShapeDtypeStruct((tokens, width), jnp.float32),
            jax.ShapeDtypeStruct((tokens, width), jnp.bfloat16),
            jax.ShapeDtypeStruct((tokens, 3 * width), jnp.bfloat16),
        ],
        compiler_params=pltpu.CompilerParams(vmem_limit_bytes=60 * 1024 * 1024),
        cost_estimate=pl.CostEstimate(flops=8_000_000_000, bytes_accessed=20_000_000, transcendentals=0),
        name="enter",
    )(moving, *parts, features, w_visual, b_visual, *weights, b_qkv)


def up_kernel(context_ref, stream_ref, w_out_ref, w_up_ref, w_down_ref, rows_ref, b_up_ref, moving_ref, *refs, chunk):
    part_refs = refs[:-8]
    mid_ref, hidden_ref, active_ref, slope_ref, out_ref, top_ref, branch_ref, sums_ref = refs[-8:]
    b_out, gain_1, shift_1, b_down, gain_2, shift_2 = (rows_ref[n : n + 1, :] for n in range(6))
    mid = stream_ref[...] + dot(context_ref[...], w_out_ref[...], 1, 0) + b_out
    mid_ref[...] = mid
    norm_one = standard(mid)[0] * gain_1 + shift_1
    hidden = norm_one.astype(jnp.bfloat16)
    hidden_ref[...] = hidden
    branch = norm_one + b_down
    for at in range(0, w_up_ref.shape[1], chunk):
        piece = slice(at, at + chunk)
        inner = dot(hidden, w_up_ref[:, piece], 1, 0) + b_up_ref[:, piece]
        active, slope = gelu_parts(inner)
        active = active.astype(jnp.bfloat16)
        active_ref[:, piece] = active
        slope_ref[:, piece] = slope.astype(jnp.bfloat16)
        branch = branch + dot(active, w_down_ref[piece, :], 1, 0)
    normed, scale = standard(branch)
    out_ref[...] = (normed * gain_2 + shift_2).astype(jnp.bfloat16)
    cot = sorted_sum(moving_ref[0], part_refs)
    top = standard_back(normed, scale, cot * gain_2)
    top_ref[...] = top
    low = top.astype(jnp.bfloat16)
    branch_ref[...] = low

    @pl.when(pl.program_id(0) == 0)
    def _():
        sums_ref[...] = jnp.zeros_like(sums_ref)

    sums_ref[0:1, :] += total(cot * normed)
    sums_ref[1:2, :] += total(cot)
    sums_ref[2:3, :] += total(low.astype(jnp.float32))


def down_kernel(
    branch_ref, slope_ref, top_ref, mid_ref, w_out_ref, w_up_ref, w_down_ref, rows_ref,
    inner_ref, mid_grad_ref, attended_ref, context_ref, sums_ref, ups_ref, *, chunk,
):
    @pl.when(pl.program_id(0) == 0)
    def _():
        sums_ref[...] = jnp.zeros_like(sums_ref)
        ups_ref[...] = jnp.zeros_like(ups_ref)

    gain_1 = rows_ref[1:2, :]
    branch = branch_ref[...]
    grad = top_ref[...]
    for at in range(0, w_up_ref.shape[1], chunk):
        piece = slice(at, at + chunk)
        inner = dot(branch, w_down_ref[piece, :], 1, 1) * slope_ref[:, piece].astype(jnp.float32)
        low = inner.astype(jnp.bfloat16)
        inner_ref[:, piece] = low
        ups_ref[0:1, piece] += total(low.astype(jnp.float32))
        grad = grad + dot(low, w_up_ref[:, piece], 1, 1)
    normed, scale = standard(mid_ref[...])
    back = standard_back(normed, scale, grad * gain_1)
    mid_grad_ref[...] = back
    low = back.astype(jnp.bfloat16)
    attended_ref[...] = low
    context_ref[...] = dot(low, w_out_ref[...], 1, 1).astype(jnp.bfloat16)
    sums_ref[0:1, :] += total(grad * normed)
    sums_ref[1:2, :] += total(grad)
    sums_ref[2:3, :] += total(low.astype(jnp.float32))


def tiled(tile, width):
    return pl.BlockSpec((tile, width), lambda n: (n, 0))


def whole(shape):
    return pl.BlockSpec(shape, lambda n: (0, 0))


def kept(shape):
    return pl.BlockSpec(shape, lambda n: (0, 0), pipeline_mode=pl.Buffered(1))


def feed_forward(context, stream_in, moving, cots, w_out, w_up, w_down, vectors, b_up, chunk=768):
    tokens, width = context.shape
    tile = SPAN // 2
    deep = w_up.shape[1]
    low, full = jnp.bfloat16, jnp.float32
    shapes = [(width, full), (width, low), (deep, low), (deep, low), (width, low), (width, full), (width, low)]
    return pl.pallas_call(
        functools.partial(up_kernel, chunk=chunk),
        grid=(tokens // tile,),
        in_specs=[tiled(tile, width)] * 2
        + [kept(w_out.shape), kept(w_up.shape), kept(w_down.shape), whole(vectors.shape), whole(b_up.shape)]
        + [pl.BlockSpec((1, tile, SPAN), lambda n: (n // 2, n % 2, 0))]
        + [by_half(part.shape[1:]) for part in cots],
        out_specs=[tiled(tile, n) for n, _ in shapes] + [whole((8, width))],
        out_shape=[jax.ShapeDtypeStruct((tokens, n), kind) for n, kind in shapes]
        + [jax.ShapeDtypeStruct((8, width), full)],
        compiler_params=pltpu.CompilerParams(vmem_limit_bytes=60 * 1024 * 1024),
        cost_estimate=pl.CostEstimate(flops=20_000_000_000, bytes_accessed=60_000_000, transcendentals=0),
        name="feed_forward",
    )(context, stream_in, w_out, w_up, w_down, vectors, b_up, moving, *cots)


def feed_back(branch, slope, top, mid, w_out, w_up, w_down, vectors, tile=SPAN // 2, chunk=768):
    tokens, width = branch.shape
    deep = w_up.shape[1]
    low, full = jnp.bfloat16, jnp.float32
    shapes = [(deep, low), (width, full), (width, low), (width, low)]
    return pl.pallas_call(
        functools.partial(down_kernel, chunk=chunk),
        grid=(tokens // tile,),
        in_specs=[tiled(tile, width), tiled(tile, deep), tiled(tile, width), tiled(tile, width)]
        + [kept(w_out.shape), kept(w_up.shape), kept(w_down.shape), whole(vectors.shape)],
        out_specs=[tiled(tile, n) for n, _ in shapes] + [whole((8, width)), whole((8, deep))],
        out_shape=[jax.ShapeDtypeStruct((tokens, n), kind) for n, kind in shapes]
        + [jax.ShapeDtypeStruct((8, width), full), jax.ShapeDtypeStruct((8, deep), full)],
        compiler_params=pltpu.CompilerParams(vmem_limit_bytes=60 * 1024 * 1024),
        cost_estimate=pl.CostEstimate(flops=20_000_000_000, bytes_accessed=60_000_000, transcendentals=0),
        name="feed_back",
    )(branch, slope, top, mid, w_out, w_up, w_down, vectors)


def leave_kernel(grad_ref, mid_ref, moving_ref, *refs):
    w_refs, out_ref = refs[:-1], refs[-1]
    width = mid_ref.shape[2]
    stream = mid_ref[0]
    for n, ref in enumerate(w_refs):
        stream = stream + dot(grad_ref[0, :, n * width : (n + 1) * width], ref[...], 1, 1)
    out_ref[...] = dot(moving_ref[0], stream.astype(jnp.bfloat16), 0, 0).astype(jnp.bfloat16)


def leave(grad, mid, moving, weights, row):
    _, span, width = mid.shape
    return pl.pallas_call(
        leave_kernel,
        grid=(1,),
        in_specs=[
            pl.BlockSpec((1, span, 3 * width), lambda n: (0, 0, 0)),
            pl.BlockSpec((1, span, width), lambda n: (row, 0, 0)),
            pl.BlockSpec((1, span, span), lambda n: (row, 0, 0)),
        ]
        + [kept(value.shape) for value in weights],
        out_specs=whole((span, width)),
        out_shape=jax.ShapeDtypeStruct((span, width), jnp.bfloat16),
        compiler_params=pltpu.CompilerParams(vmem_limit_bytes=60 * 1024 * 1024),
        cost_estimate=pl.CostEstimate(flops=3_000_000_000, bytes_accessed=9_000_000, transcendentals=0),
        name="leave",
    )(grad, mid, moving, *weights)


DP = "dp"
STREAM = "stream"


def swap(value, axis, bit):
    count = lax.axis_size(axis)
    return lax.ppermute(value, axis, [(i, i ^ bit) for i in range(count)])


def bits_of(axis):
    count = lax.axis_size(axis)
    return [1 << n for n in range(count.bit_length() - 1)]


def rounds():
    core, *chips = bits_of(DP)
    groups = [(DP, [core])] + [(DP, chips[n : n + 2]) for n in range(0, len(chips), 2)]
    places = bits_of(STREAM)
    return groups + [(STREAM, places[n : n + 2]) for n in range(0, len(places), 2)]


def masks_of(bits):
    return [sum(bit for n, bit in enumerate(bits) if pick >> n & 1) for pick in range(1, 1 << len(bits))]


def add_all(kept, got):
    total = kept + got[0]
    return total + (got[1] + got[2]) if len(got) > 1 else total


class Scatter:
    def __init__(self, values):
        self.names = [(axis, bit) for axis in (DP, STREAM) for bit in bits_of(axis)[::-1]]
        self.values = [value.reshape((2,) * len(self.names) + value.shape[1:]) for value in values]
        self.left = rounds()

    def send(self):
        axis, bits = self.left.pop(0)
        place = lax.axis_index(axis)
        count = lax.axis_size(axis)
        self.whole = 1 << len(bits) == count
        if self.whole:
            given = [value.reshape((count,) + value.shape[len(bits) :]) for value in self.values]
            self.kept = []
            self.got = [lax.all_to_all(joined(given, -1), axis, 0, 0, tiled=True)]
            self.sizes = [value.shape[-1] for value in self.values]
            self.names = [name for name in self.names if name[0] != axis]
            return
        dims = {bit: self.names.index((axis, bit)) for bit in bits}

        def pick(value, mask):
            at = [0] * value.ndim
            size = list(value.shape)
            for bit, dim in dims.items():
                at[dim] = ((place ^ mask) // bit) % 2
                size[dim] = 1
            part = lax.dynamic_slice(value, at, size)
            return part.reshape([n for dim, n in enumerate(size) if dim not in dims.values()])

        self.kept = [pick(value, 0) for value in self.values]
        self.got = [
            swap(joined([pick(value, mask) for value in self.values], -1), axis, mask)
            for mask in masks_of(bits)
        ]
        self.names = [name for name in self.names if name[0] != axis or name[1] not in bits]

    def add(self):
        if not self.got:
            return
        values, at = [], 0
        if self.whole:
            for size in self.sizes:
                values.append(jnp.sum(self.got[0][..., at : at + size].astype(jnp.float32), axis=0))
                at += size
        for kept in self.kept:
            got = [part[..., at : at + kept.shape[-1]].astype(jnp.float32) for part in self.got]
            at += kept.shape[-1]
            value = add_all(kept.astype(jnp.float32), got)
            values.append(value.astype(jnp.bfloat16) if self.left else value)
        self.values, self.got = values, []

    def next(self):
        self.add()
        if self.left:
            self.send()

    def finish(self):
        while self.left:
            self.next()
        self.add()
        return self.values


def advance(value, groups, extra=()):
    tied, got, held = lax.optimization_barrier((value, [group.got for group in groups], list(extra)))
    for group, parts in zip(groups, got):
        group.got = parts
        group.next()
    return tied, held


def together(*values):
    return lax.optimization_barrier(values)


def sum_over(value, groups):
    for axis, bits in groups:
        value = add_all(value, [swap(value, axis, mask) for mask in masks_of(bits)])
    return value


def turned(shift):
    count = lax.axis_size(STREAM)
    return [(i, (i + shift) % count) for i in range(count)]


def to_rows(value):
    count = lax.axis_size(STREAM)
    place = lax.axis_index(STREAM)
    block = value.shape[0] // count
    parts = []
    for shift in range(count):
        part = lax.dynamic_slice_in_dim(value, (place - shift) % count * block, block, 0)
        parts.append(lax.ppermute(part, STREAM, turned(-shift)) if shift else part)
    return parts


def rows_back(value):
    count = lax.axis_size(STREAM)
    place = lax.axis_index(STREAM)
    rows, slots, width = value.shape
    parts = jnp.swapaxes(value.reshape(rows, count, slots // count, width), 0, 1)
    parts = jnp.concatenate([parts, parts], axis=0)
    parts = lax.dynamic_slice_in_dim(parts, (count - place) % count, count, 0)
    return lax.all_to_all(parts, STREAM, 0, 0, tiled=True)


def per_device(
    text_input,
    visual_features,
    receipt_text,
    receipt_visual,
    boxes,
    w_query,
    b_query,
    w_key,
    w_value,
    b_value,
    w_out,
    b_out,
    gain_attn,
    shift_attn,
    w_up,
    b_up,
    w_down,
    b_down,
    gain_ffn,
    shift_ffn,
    w_visual,
    b_visual,
    table_line,
    table_x,
    table_y,
    cotangent_text,
    cotangent_visual,
):
    floating = jnp.float32
    narrow = jnp.bfloat16
    width = text_input.shape[-1]
    rows, visual, channels = visual_features.shape
    text = receipt_text.shape[1]
    slots = text + visual
    world = lax.axis_size(DP) * lax.axis_size(STREAM)
    place = lax.axis_index(STREAM)
    first_row = place * rows

    text_parts = to_rows(text_input)
    text_parts, cotangent_text = lax.optimization_barrier((text_parts, cotangent_text))
    cotangent_parts = to_rows(cotangent_text)

    def pad(value, fill=0, size=SPAN):
        extra = size - value.shape[1]
        return jnp.pad(value, ((0, 0), (0, extra)) + ((0, 0),) * (value.ndim - 2), constant_values=fill)

    seg_text = lax.dynamic_slice_in_dim(receipt_text, first_row, rows, 0)
    seg_visual = lax.dynamic_slice_in_dim(receipt_visual, first_row, rows, 0)
    box = lax.dynamic_slice_in_dim(boxes, first_row, rows, 1)
    index = jnp.arange(SPAN, dtype=jnp.int32)
    position = jnp.where(index < text, index, index - text)
    facts = jnp.stack(
        [
            jnp.broadcast_to(position, (rows, SPAN)),
            pad(box[0]),
            pad(box[1]),
            pad(jnp.concatenate([seg_text, seg_visual], axis=1), RECEIPTS),
            jnp.broadcast_to(index, (rows, SPAN)),
        ],
        axis=1,
    )
    own = lax.dynamic_slice_in_dim(
        jnp.concatenate([facts[:, :, :text], facts[:, :, :text]], axis=2), place * text_input.shape[1], text, 2
    )
    facts = jnp.concatenate([own, facts[:, :, text:]], axis=2)
    rank = facts[:, 3] * SPAN + facts[:, 4]
    seg = facts[:, 3]
    target = jnp.sum((rank[:, None, :] < rank[:, :, None]).astype(jnp.int32), axis=2)
    moved = target[:, None, :] == index[None, :, None]
    facts = facts[:, :4]
    facts = jnp.sum(jnp.where(moved[:, None], facts[:, :, None, :], 0), axis=3)
    col = jnp.pad(jnp.swapaxes(facts, 1, 2), ((0, 0), (0, 0), (0, 124)))
    row = jnp.pad(facts, ((0, 0), (0, 4), (0, 640 - SPAN)), constant_values=RECEIPTS)
    starts = jnp.sum(
        (seg[:, None, :] < jnp.arange(RECEIPTS + 1, dtype=jnp.int32)[None, :, None]).astype(jnp.int32), axis=2
    )
    plan = make_plan(starts)
    plane = jnp.concatenate([table_x, table_y], axis=1).astype(floating)
    lines = jnp.pad(table_line.astype(floating), ((0, 0), (0, 96)), constant_values=NONE)

    bias, places = make_bias(plan, col, row, plane, lines)
    moving = moved.astype(narrow)

    def unsort(value):
        return jnp.einsum("rps,rpd->rsd", moving, value, preferred_element_type=floating)

    def rowwise(array):
        return array.reshape(rows, SPAN, -1)

    weights = (w_query, w_key, w_value)
    b_qkv = jnp.concatenate([b_query, jnp.zeros_like(b_query), b_value]).astype(floating)
    stream_in, entered, qkv = enter(
        moving, text_parts, pad(visual_features, 0, SPAN - text), w_visual, b_visual.astype(floating)[None],
        weights, b_qkv[None],
    )
    qkv = rowwise(qkv)
    context, shares = attend(plan, qkv, row, bias)
    context, cotangent_parts = lax.optimization_barrier((context, cotangent_parts))
    context = context.reshape(-1, width)
    vectors = jnp.stack([b_out, gain_attn, shift_attn, b_down, gain_ffn, shift_ffn, b_out, b_out]).astype(floating)
    mid, hidden, active, slope, outcome, grad_top, grad_branch, ffn_sums = feed_forward(
        context, stream_in, moving, cotangent_parts + [pad(cotangent_visual, 0, SPAN - text)],
        w_out, w_up, w_down, vectors, b_up.astype(floating)[None],
    )

    def lines_of(value):
        return [value[:, n : n + width] for n in range(0, value.shape[1], width)]

    def weight_grad(left, right):
        return jnp.einsum("ti,tj->ij", left, right, preferred_element_type=floating)

    def chunks(part):
        return part.astype(narrow).reshape(world, part.shape[0] // world, -1)

    grad_w_down = chunks(weight_grad(active, grad_branch))
    grad_w_down, grad_branch, outcome = together(grad_w_down, grad_branch, outcome)
    downs = Scatter([grad_w_down])
    downs.send()
    out_rows = unsort(rowwise(outcome)).astype(narrow)
    out_visual = out_rows[:, text:slots]
    (grad_branch, out_rows), _ = advance((grad_branch, out_rows), [downs])
    out_text = rows_back(out_rows[:, :text])
    grad_inner, grad_mid, grad_attended, grad_context, attn_sums, up_sums = feed_back(
        grad_branch, slope, grad_top, mid, w_out, w_up, w_down, vectors
    )
    grad_inner, downs.got = lax.optimization_barrier((grad_inner, downs.got))
    grad_w_up = chunks(weight_grad(hidden, grad_inner))
    grad_w_out = chunks(weight_grad(context, grad_attended))
    grad_context, grad_w_out, grad_w_up = together(grad_context, grad_w_out, grad_w_up)
    ups = Scatter([grad_w_up, grad_w_out])
    ups.send()
    (grad_context, out_text), _ = advance((rowwise(grad_context), out_text), [downs])
    out_text = out_text.reshape((-1,) + out_text.shape[2:])

    entered_rows, grad_mid_rows = rowwise(entered), rowwise(grad_mid)

    grad_qkv_0, bins_0 = attend_back(plan, qkv, grad_context, places, shares, 0)
    grad_qkv_0, _ = advance(grad_qkv_0, [ups])
    grad_qkv_0, downs.got = lax.optimization_barrier((grad_qkv_0, downs.got))
    back_0 = leave(grad_qkv_0, grad_mid_rows, moving, weights, 0)
    got_0 = rows_back(back_0[None, :text])
    grad_w_qkv = weight_grad(entered_rows[0], grad_qkv_0[0])
    grad_b_qkv = jnp.sum(grad_qkv_0[0], axis=0, dtype=floating)
    grad_context, back_0, grad_w_qkv = together(grad_context, back_0, grad_w_qkv)
    grad_qkv_1, bins_1 = attend_back(plan, qkv, grad_context, places, shares, 1)
    (grad_qkv_1, got_0), _ = advance((grad_qkv_1, got_0), [ups])
    grad_w_qkv = chunks(grad_w_qkv + weight_grad(entered_rows[1], grad_qkv_1[0]))
    grad_b_qkv = grad_b_qkv + jnp.sum(grad_qkv_1[0], axis=0, dtype=floating)
    lasts = Scatter([grad_w_qkv])
    lasts.send()
    grad_qkv_1, lasts.kept = lax.optimization_barrier((grad_qkv_1, lasts.kept))
    back_1 = leave(grad_qkv_1, grad_mid_rows, moving, weights, 1)
    back_1, ups.got = lax.optimization_barrier((back_1, ups.got))
    grad_visual = jnp.stack([back_0[text:slots], back_1[text:slots]])
    grad_w_visual = jnp.einsum("rvc,rvd->cd", visual_features, grad_visual, preferred_element_type=floating)
    grad_b_visual = jnp.sum(grad_visual, axis=(0, 1), dtype=floating)
    grad_features = jnp.einsum("rvd,cd->rvc", grad_visual, w_visual, preferred_element_type=floating)
    grad_w_visual = chunks(grad_w_visual)
    third = width // 3
    extra = Scatter([jnp.concatenate([grad_w_visual[:, :, n : n + third] for n in range(0, width, third)], axis=1)])
    extra.send()
    lasts.got, extra.got = lax.optimization_barrier((lasts.got, extra.got))
    lasts.add()
    extra.add()
    lasts.values += extra.values
    lasts.send()
    held = (back_1, grad_features, lasts.kept, ups.got, downs.got)
    back_1, grad_features, lasts.kept, ups.got, downs.got = lax.optimization_barrier(held)
    got_1 = rows_back(back_1[None, :text])
    vectors = (ffn_sums, attn_sums, bins_0, bins_1, grad_b_qkv, grad_b_visual, up_sums)
    vectors, lasts.kept, ups.got, downs.got = lax.optimization_barrier((vectors, lasts.kept, ups.got, downs.got))
    ffn_sums, attn_sums, bins_0, bins_1, grad_b_qkv, grad_b_visual, up_sums = vectors
    small = jnp.concatenate(
        [ffn_sums, attn_sums, bins_0 + bins_1]
        + lines_of(grad_b_qkv[None]) + [grad_b_visual[None]] + lines_of(up_sums[:1]),
        axis=0,
    )
    out_text = jnp.where(place >= 0, out_text, 0.0)
    opening, *later = rounds()
    small = sum_over(small, [opening, later.pop()])
    (small, got_0, got_1, out_text), _ = advance((small, got_0, got_1, out_text), [lasts])
    small = sum_over(small, later)
    (down_sum,) = downs.finish()
    up_sum, out_sum = ups.finish()
    qkv_sum, visual_sum = lasts.finish()
    grad_text = jnp.stack([got_0[:, 0].astype(floating), got_1[:, 0].astype(floating)], axis=1)
    grad_text = grad_text.reshape((-1,) + grad_text.shape[2:])
    query_sum, key_sum, value_sum = (qkv_sum[:, n * width : (n + 1) * width] for n in range(3))
    visual_sum = visual_sum.reshape(3, -1, third)
    visual_sum = jnp.concatenate([visual_sum[n] for n in range(3)], axis=1)
    step = width // world
    device = lax.axis_index(DP) * lax.axis_size(STREAM) + place
    mine = lax.dynamic_slice_in_dim(small, device * step, step, 1)
    up_step = w_up.shape[1] // world
    bins = small[16 : 16 + HEADS]
    return (
        out_text,
        out_visual,
        grad_text,
        grad_features,
        query_sum,
        mine[32],
        key_sum,
        value_sum,
        mine[34],
        out_sum,
        mine[10],
        mine[8],
        mine[9],
        up_sum,
        lax.dynamic_slice_in_dim(small[36:].reshape(-1), device * up_step, up_step, 0),
        down_sum,
        mine[2],
        mine[0],
        mine[1],
        visual_sum,
        mine[35],
        bins[:, 128:160],
        bins[:, :64],
        bins[:, 64:128],
    )


def solution(mesh):
    placed = (
        P("dp", "stream", None),
        P(("dp", "stream"), None, None),
        P("dp", None),
        P("dp", None),
        P(None, "dp", None),
        P(),
        P(),
        P(),
        P(),
        P(),
        P(),
        P(),
        P(),
        P(),
        P(),
        P(),
        P(),
        P(),
        P(),
        P(),
        P(),
        P(),
        P(),
        P(),
        P(),
        P("dp", "stream", None),
        P(("dp", "stream"), None, None),
    )
    return jax.shard_map(
        per_device,
        mesh=mesh,
        in_specs=placed,
        out_specs=(
            P("dp", "stream", None),
            P(("dp", "stream"), None, None),
            P("dp", "stream", None),
            P(("dp", "stream"), None, None),
            P(("dp", "stream"), None),
            P(("dp", "stream")),
            P(("dp", "stream"), None),
            P(("dp", "stream"), None),
            P(("dp", "stream")),
            P(("dp", "stream"), None),
            P(("dp", "stream")),
            P(("dp", "stream")),
            P(("dp", "stream")),
            P(("dp", "stream"), None),
            P(("dp", "stream")),
            P(("dp", "stream"), None),
            P(("dp", "stream")),
            P(("dp", "stream")),
            P(("dp", "stream")),
            P(("dp", "stream"), None),
            P(("dp", "stream")),
            P(),
            P(),
            P(),
        ),
        check_vma=False,
    )
```

```python
import functools
import math

import jax, jax.numpy as jnp
from jax import lax
from jax.experimental import pallas as pl
from jax.experimental.pallas import tpu as pltpu
from jax.sharding import PartitionSpec as P

HEADS = 12
RECEIPTS = 8
VISUAL = 49
PLAN = 32
SPAN = 576
BINS = 160
NONE = -1e30
TALL = 192
WIDE = 256
FORWARD_PAIRS = 6
BACKWARD_PAIRS = 6


def thresholds(half, reach):
    exact = half // 2
    steps = half - exact
    return [
        int(math.floor(exact * (reach / exact) ** (power / steps) + 0.5))
        for power in range(1, steps)
    ]


def bucket(diff, count, reach):
    half = count // 2
    exact = half // 2
    dist = jnp.abs(diff)
    passed = jnp.where(diff > 0, half, 0)
    for limit in thresholds(half, reach):
        passed = passed + jnp.where(dist >= limit, 1, 0)
    return passed + jnp.minimum(dist, exact)


def dot(a, b, ca, cb):
    return lax.dot_general(a, b, (((ca,), (cb,)), ((), ())), preferred_element_type=jnp.float32)


def by_size(plan_ref, run, offset=0):
    step = pl.program_id(0)
    receipt = lax.rem(step, RECEIPTS)
    base = (step // RECEIPTS + offset) * PLAN + receipt
    first = plan_ref[base]
    last = plan_ref[base + 1]
    start = first // 16 * 16
    low = 0
    for tall in (64, 96, 128, 160, 192):
        wide = 128 if tall <= 128 else 256
        inside = last - start > low
        if tall < TALL:
            inside = jnp.logical_and(inside, last - start <= tall)
        low = tall

        @pl.when(inside)
        def _(tall=tall, wide=wide):
            at_k = pl.multiple_of(jnp.minimum(start, SPAN - tall), 16)
            at_q = pl.multiple_of(jnp.minimum(start, SPAN - wide), 16)
            run(receipt, first - at_k, last - at_k, at_k, at_q, tall, wide)


def blocks(refs, head, tile, tall):
    found = []
    for n, (which, lead) in enumerate((((0, ()), (1, ()), (2, (0,))), ((2, (1,)), (2, (2,)), (2, (3,))))[tile]):
        size = min(64, tall - 64 * n)
        if size > 0:
            found.append((refs[which], (0,) + lead + (head, pl.ds(0, size)), 64 * n, size))
    return found


def load(refs, head, tall, wide):
    return joined(
        [joined([ref[at] for ref, at, _, _ in blocks(refs, head, tile, tall)], 0) for tile in range(wide // 128)], 1
    )


def store(refs, head, value):
    tall, wide = value.shape
    for tile in range(wide // 128):
        for ref, at, row, size in blocks(refs, head, tile, tall):
            ref[at] = value[row : row + size, 128 * tile : 128 * tile + 128]


def joined(pieces, axis):
    return pieces[0] if len(pieces) == 1 else jnp.concatenate(pieces, axis=axis)


def bias_kernel(plan_ref, col_ref, row_ref, plane_ref, lines_ref, near_ref, mid_ref, far_ref, index_ref):
    refs = (near_ref, mid_ref, far_ref)
    height = 32

    def run(receipt, low, high, at_k, at_q, tall, wide):
        row = pltpu.roll(row_ref[0], lax.rem(640 - at_q, 640), 1)[:, :wide]
        shape = (height, 128)

        def fill(tile, n, at):
            _, lead = (((0, ()), (1, ()), (2, (0,))), ((2, (1,)), (2, (2,)), (2, (3,))))[tile][n]
            ref = refs[(((0, 1, 2), (2, 2, 2))[tile])[n]]
            lanes = slice(128 * tile, 128 * (tile + 1))
            here = pl.multiple_of(64 * n + at, height)
            used = jnp.logical_and(here < high, here + height > low)

            @pl.when(jnp.logical_not(used))
            def _():
                for h in range(HEADS):
                    ref[(0,) + lead + (h, pl.ds(at, height))] = jnp.full(shape, NONE, jnp.float32)

            @pl.when(used)
            def _():
                col = col_ref[0, pl.ds(pl.multiple_of(at_k + here, 16), height), :]

                def spread(r):
                    return (jnp.broadcast_to(col[:, r : r + 1], shape), jnp.broadcast_to(row[r : r + 1, lanes], shape))

                def gap(r):
                    key, query = spread(r)
                    return key - query

                key, query = spread(3)
                same = jnp.logical_and(key == receipt, query == receipt)
                line = jnp.where(same, bucket(gap(0), 32, 128), 32)
                across = bucket(gap(1), 64, 256)
                down = bucket(gap(2), 64, 256) + 64
                index_ref[0, pl.ds(here, height), lanes] = across + down * 256 + line * 65536
                def look(table_ref, h, index):
                    table = jnp.broadcast_to(table_ref[h : h + 1, :], (8, 128))
                    return jnp.take_along_axis(table, index, axis=1, mode="promise_in_bounds")
                for r in range(height // 8):
                    a8, d8, l8 = (v[8 * r : 8 * r + 8] for v in (across, down, line))

                    xs = [look(plane_ref, h, a8) for h in range(HEADS)]
                    ys = [look(plane_ref, h, d8) for h in range(HEADS)]
                    ls = [look(lines_ref, h, l8) for h in range(HEADS)]
                    for h in range(HEADS):
                        ref[(0,) + lead + (h, pl.ds(at + 8 * r, 8))] = xs[h] + ys[h] + ls[h]

        for tile in range(wide // 128):
            for n in range(pl.cdiv(tall, 64)):
                def step(m, carry, tile=tile, n=n):
                    fill(tile, n, pl.multiple_of(m * height, height))
                    return carry

                lax.fori_loop(0, 2, step, 0)

    by_size(plan_ref, run)


def split_pair(value, scale=1.0):
    lane = lax.broadcasted_iota(jnp.int32, value.shape, 1)
    full = value.astype(jnp.float32) * scale
    low = jnp.where(lane < 64, full, 0.0).astype(value.dtype)
    high = jnp.where(lane < 64, 0.0, full).astype(value.dtype)
    return jnp.concatenate([low, high], axis=0)


def grouped(size):
    return [range(n, n + size) for n in range(0, HEADS // 2, size)]


def parts(pair, at_k, at_q, tall, wide):
    width = HEADS * 64
    return (
        (0, pl.ds(at_q, wide), pl.ds(128 * pair, 128)),
        (0, pl.ds(at_k, tall), pl.ds(width + 128 * pair, 128)),
        (0, pl.ds(at_k, tall), pl.ds(2 * width + 128 * pair, 128)),
    )


def gather_into(ref, where, value):
    ref[where] = (ref[where].astype(jnp.float32) + value).astype(ref.dtype)


def forward_kernel(plan_ref, qkv_ref, row_ref, *refs):
    bias_refs, out_ref, shares_refs = refs[:3], refs[3], refs[4:]

    @pl.when(lax.rem(pl.program_id(0), RECEIPTS) == 0)
    def _():
        out_ref[...] = jnp.zeros_like(out_ref)

    def run(receipt, low, high, at_k, at_q, tall, wide):
        owner = pltpu.roll(row_ref[0], lax.rem(640 - at_q, 640), 1)[3:4, :wide]
        mine = jnp.where(owner == receipt, 1.0, 0.0)
        for group in grouped(FORWARD_PAIRS):
            spots = [parts(pair, at_k, at_q, tall, wide) for pair in group]
            scores = [
                dot(split_pair(qkv_ref[keys], 0.125), qkv_ref[queries], 1, 1) for queries, keys, _ in spots
            ]
            shares = []
            for pair, score in zip(group, scores):
                halves = []
                for h in range(2):
                    part = score[h * tall : (h + 1) * tall] + load(bias_refs, 2 * pair + h, tall, wide)
                    expo = jnp.exp(part - jnp.max(part, axis=0, keepdims=True))
                    share = expo * (mine / jnp.sum(expo, axis=0, keepdims=True))
                    halves.append(share.astype(jnp.bfloat16))
                    store(shares_refs, 2 * pair + h, halves[h])
                shares.append(jnp.concatenate(halves, axis=0))
            results = [dot(share, split_pair(qkv_ref[values]), 0, 0) for share, (_, _, values) in zip(shares, spots)]
            for result, (queries, _, _) in zip(results, spots):
                gather_into(out_ref, queries, result)

    by_size(plan_ref, run)


def backward_kernel(offset, plan_ref, qkv_ref, g_ref, index_ref, *refs):
    shares_refs, (dqkv_ref, bins_ref, terms_s) = refs[:3], refs[-3:]

    @pl.when(pl.program_id(0) == 0)
    def _():
        bins_ref[...] = jnp.zeros_like(bins_ref)
        terms_s[...] = jnp.zeros_like(terms_s)


    @pl.when(lax.rem(pl.program_id(0), RECEIPTS) == 0)
    def _():
        dqkv_ref[...] = jnp.zeros_like(dqkv_ref)

    def run(receipt, low, high, at_k, at_q, tall, wide):
        for group in grouped(BACKWARD_PAIRS):
            spots = [parts(pair, at_k, at_q, tall, wide) for pair in group]
            grads = [g_ref[queries] for queries, _, _ in spots]
            parts_of = [
                dot(split_pair(qkv_ref[values]), grad, 1, 1) for grad, (_, _, values) in zip(grads, spots)
            ]
            shares, steps = [], []
            for pair, grad_probs in zip(group, parts_of):
                for h in range(2):
                    share = load(shares_refs, 2 * pair + h, tall, wide)
                    part = grad_probs[h * tall : (h + 1) * tall]
                    probs = share.astype(jnp.float32)
                    inner = jnp.sum(probs * part, axis=0, keepdims=True)
                    step = (probs * (part - inner)).astype(jnp.bfloat16)
                    wide_step = step.astype(jnp.float32)
                    for c in range(wide // 128):
                        lanes = slice(128 * c, 128 * c + 128)
                        terms_s[c, pl.ds(2 * pair + h, tall, stride=16), :] = wide_step[:, lanes]
                    shares.append(share)
                    steps.append(step)
            results = []
            for n, (queries, keys, values) in enumerate(spots):
                pair = slice(2 * n, 2 * n + 2)
                results.append((values, dot(jnp.concatenate(shares[pair], axis=1), split_pair(grads[n]), 1, 0)))
                query = split_pair(qkv_ref[queries], 0.125)
                results.append((keys, dot(jnp.concatenate(steps[pair], axis=1), query, 1, 0)))
                key = split_pair(qkv_ref[keys], 0.125)
                results.append((queries, dot(jnp.concatenate(steps[pair], axis=0), key, 0, 0)))
            for where, result in results:
                gather_into(dqkv_ref, where, result)

        group = 32
        level = lax.broadcasted_iota(jnp.int32, (BINS, 128), 0)

        def bin_step(n, total):
            hots, terms = [], []
            at = pl.multiple_of(n * group, group)
            for c in range(wide // 128):
                packed = index_ref[0, pl.ds(at, group), 128 * c : 128 * c + 128]
                x, y, line = packed & 255, (packed >> 8) & 255, (packed >> 16) + 128
                for i in range(group):
                    def spread(value, count):
                        return jnp.broadcast_to(value[i : i + 1, :], (count, 128))

                    index = jnp.concatenate([spread(x, 64), spread(y, 64), spread(line, 32)], axis=0)
                    hots.append(jnp.where(level == index, 1.0, 0.0).astype(jnp.bfloat16))
                    terms.append(terms_s[c, pl.ds(pl.multiple_of((at + i) * 16, 16), 16), :].astype(jnp.bfloat16))
            return total + dot(jnp.concatenate(terms, axis=1), jnp.concatenate(hots, axis=1), 1, 1)

        total = lax.fori_loop(low // group, pl.cdiv(high, group), bin_step, jnp.zeros((16, BINS), jnp.float32))
        bins_ref[:, :BINS] += total


    by_size(plan_ref, run, offset)


def of_row(shape, offset=0):
    return pl.BlockSpec((1,) + shape, lambda n, *_: (n // RECEIPTS + offset,) + (0,) * len(shape))


def of_step(shape, offset=0):
    return pl.BlockSpec((1,) + shape, lambda n, *_: (n + offset * RECEIPTS,) + (0,) * len(shape))


def of_plan(shape, offset, base, at):
    def place(n, plan_ref):
        row = n // RECEIPTS
        step = plan_ref[(row + offset) * PLAN + at + lax.rem(n, RECEIPTS)]
        return ((row + base) * RECEIPTS + step,) + (0,) * len(shape)

    return pl.BlockSpec((1,) + shape, place)


def tile_specs(offset=0, base=0):
    near, far = (HEADS, 64, 128), (4, HEADS, 64, 128)
    return [of_step(near, base), of_plan(near, offset, base, 16), of_plan(far, offset, base, 24)]


def tile_shapes(steps, kind):
    shapes = ((HEADS, 64, 128), (HEADS, 64, 128), (4, HEADS, 64, 128))
    return [jax.ShapeDtypeStruct((steps,) + shape, kind) for shape in shapes]


def fixed(shape):
    return pl.BlockSpec(shape, lambda n, *_: (0,) * len(shape))


def call(kernel, name, plan, args, in_specs, out_specs, out_shape, steps, cost, scratch=(), vmem=60, alias=None):
    return pl.pallas_call(
        kernel,
        grid_spec=pltpu.PrefetchScalarGridSpec(
            num_scalar_prefetch=1, grid=(steps,), in_specs=in_specs, out_specs=out_specs, scratch_shapes=scratch
        ),
        out_shape=out_shape,
        compiler_params=pltpu.CompilerParams(vmem_limit_bytes=vmem * 1024 * 1024),
        cost_estimate=pl.CostEstimate(flops=cost, bytes_accessed=cost // 1000, transcendentals=0),
        input_output_aliases=alias or {},
        name=name,
    )(plan, *args)


def make_bias(plan, col, row, plane, lines):
    steps = col.shape[0] * RECEIPTS
    *bias, index = call(
        bias_kernel, "make_bias", plan, (col, row, plane, lines),
        [of_row((SPAN, 128)), of_row((8, 640)), fixed((HEADS, 128)), fixed((HEADS, 128))],
        tile_specs() + [of_step((TALL, WIDE))],
        tile_shapes(steps, jnp.float32) + [jax.ShapeDtypeStruct((steps, TALL, WIDE), jnp.int32)],
        steps, 30_000_000_000,
    )
    return bias, index


def attend(plan, qkv, row, bias):
    rows, span, width = qkv.shape
    steps = rows * RECEIPTS
    out, *shares = call(
        forward_kernel, "attend", plan, (qkv, row, *bias),
        [of_row((span, width)), of_row((8, 640))] + tile_specs(),
        [of_row((span, width // 3))] + tile_specs(),
        [jax.ShapeDtypeStruct((rows, span, width // 3), qkv.dtype)] + tile_shapes(steps, jnp.bfloat16),
        steps, 20_000_000_000,
    )
    return out, shares


def attend_back(plan, qkv, g, index, shares, first, before=None):
    rows, span, width = qkv.shape
    bins = (16, width // 3)
    specs = [of_row((span, width), first), of_row((span, width // 3), first), of_step((TALL, WIDE), first)]
    args = (qkv, g, index, *shares)
    specs += tile_specs(first, first)
    alias = {}
    if before is not None:
        args += (before,)
        specs.append(pl.BlockSpec(memory_space=pl.ANY))
        alias = {len(args): 0}
    return call(
        functools.partial(backward_kernel, first), "attend_back", plan, args, specs,
        [of_row((span, width), first), fixed(bins)],
        [jax.ShapeDtypeStruct((rows, span, width), qkv.dtype), jax.ShapeDtypeStruct(bins, jnp.float32)],
        RECEIPTS, 20_000_000_000, [pltpu.VMEM((2, TALL * 16, 128), jnp.float32)], alias=alias,
    )


def make_plan(starts):
    first, last = starts[:, :-1], starts[:, 1:]
    span = last - first // 16 * 16
    order = jnp.arange(RECEIPTS, dtype=jnp.int32)

    def latest(need):
        passed = need[:, None, :] & (order[None, :] <= order[:, None])[None]
        behind = jnp.max(jnp.where(passed, order, -1), axis=2)
        ahead = jnp.min(jnp.where(need, order, RECEIPTS - 1), axis=1, keepdims=True)
        return jnp.where(behind < 0, ahead, behind)

    bounds = jnp.pad(starts, ((0, 0), (0, 15 - RECEIPTS)))
    return jnp.concatenate([bounds, latest(span > 64), latest(span > 128)], axis=1).reshape(-1)


EPSILON = 1e-05


def gelu_parts(u):
    expo = jnp.exp(u * u * -0.5)
    share = 0.5 + 0.5 * lax.erf(u * (1.0 / math.sqrt(2.0)))
    return u * share, share + u * expo * (1.0 / math.sqrt(2.0 * math.pi))


def standard(values):
    centred = values - jnp.mean(values, axis=1, keepdims=True)
    scale = lax.rsqrt(jnp.mean(centred * centred, axis=1, keepdims=True) + EPSILON)
    return centred * scale, scale


def standard_back(normed, scale, grad):
    return (
        grad - jnp.mean(grad, axis=1, keepdims=True) - normed * jnp.mean(grad * normed, axis=1, keepdims=True)
    ) * scale


def total(value):
    return jnp.sum(value, axis=0, keepdims=True)


def sorted_sum(moving, parts):
    value, at = 0.0, 0
    for part in parts:
        count = part.shape[1]
        value = value + dot(moving[:, at : at + count], part[0], 1, 0)
        at += count
    return value


def enter_kernel(*refs):
    count = len(refs) - 11
    moving_ref, *part_refs = refs[: count + 1]
    features_ref, w_visual_ref, b_visual_ref, *w_refs, b_qkv_ref, stream_ref, low_ref, qkv_ref = refs[count + 1 :]
    moving = moving_ref[0]
    text = sum(ref.shape[1] for ref in part_refs)
    at_visual = moving[:, text:]
    features = dot(at_visual, features_ref[0], 1, 0).astype(jnp.bfloat16)
    lane = lax.broadcasted_iota(jnp.int32, at_visual.shape, 1)
    is_visual = jnp.sum(jnp.where(lane < VISUAL, at_visual.astype(jnp.float32), 0.0), axis=1, keepdims=True)
    visual = dot(features, w_visual_ref[...], 1, 0) + b_visual_ref[...]
    stream = sorted_sum(moving, part_refs) + visual * is_visual
    stream_ref[...] = stream
    low = stream.astype(jnp.bfloat16)
    low_ref[...] = low
    width = low.shape[1]
    for n, ref in enumerate(w_refs):
        lanes = slice(n * width, (n + 1) * width)
        qkv_ref[:, lanes] = (dot(low, ref[...], 1, 0) + b_qkv_ref[:, lanes]).astype(jnp.bfloat16)


def by_half(shape):
    return pl.BlockSpec((1,) + shape, lambda n: (n // 2, 0, 0))


def enter(moving, parts, features, w_visual, b_visual, weights, b_qkv):
    rows = moving.shape[0]
    width = w_visual.shape[1]
    tile = SPAN // 2
    tokens = rows * SPAN
    return pl.pallas_call(
        enter_kernel,
        grid=(2 * rows,),
        in_specs=[pl.BlockSpec((1, tile, SPAN), lambda n: (n // 2, n % 2, 0))]
        + [by_half(part.shape[1:]) for part in (*parts, features)]
        + [kept(value.shape) for value in (w_visual, b_visual, *weights, b_qkv)],
        out_specs=[tiled(tile, width), tiled(tile, width), tiled(tile, 3 * width)],
        out_shape=[
            jax.ShapeDtypeStruct((tokens, width), jnp.float32),
            jax.ShapeDtypeStruct((tokens, width), jnp.bfloat16),
            jax.ShapeDtypeStruct((tokens, 3 * width), jnp.bfloat16),
        ],
        compiler_params=pltpu.CompilerParams(vmem_limit_bytes=60 * 1024 * 1024),
        cost_estimate=pl.CostEstimate(flops=8_000_000_000, bytes_accessed=20_000_000, transcendentals=0),
        name="enter",
    )(moving, *parts, features, w_visual, b_visual, *weights, b_qkv)


def up_kernel(context_ref, stream_ref, w_out_ref, w_up_ref, w_down_ref, rows_ref, b_up_ref, moving_ref, *refs, chunk):
    part_refs = refs[:-8]
    mid_ref, hidden_ref, active_ref, slope_ref, out_ref, top_ref, branch_ref, sums_ref = refs[-8:]
    b_out, gain_1, shift_1, b_down, gain_2, shift_2 = (rows_ref[n : n + 1, :] for n in range(6))
    mid = stream_ref[...] + dot(context_ref[...], w_out_ref[...], 1, 0) + b_out
    mid_ref[...] = mid
    norm_one = standard(mid)[0] * gain_1 + shift_1
    hidden = norm_one.astype(jnp.bfloat16)
    hidden_ref[...] = hidden
    branch = norm_one + b_down
    for at in range(0, w_up_ref.shape[1], chunk):
        piece = slice(at, at + chunk)
        inner = dot(hidden, w_up_ref[:, piece], 1, 0) + b_up_ref[:, piece]
        active, slope = gelu_parts(inner)
        active = active.astype(jnp.bfloat16)
        active_ref[:, piece] = active
        slope_ref[:, piece] = slope.astype(jnp.bfloat16)
        branch = branch + dot(active, w_down_ref[piece, :], 1, 0)
    normed, scale = standard(branch)
    out_ref[...] = (normed * gain_2 + shift_2).astype(jnp.bfloat16)
    cot = sorted_sum(moving_ref[0], part_refs)
    top = standard_back(normed, scale, cot * gain_2)
    top_ref[...] = top
    low = top.astype(jnp.bfloat16)
    branch_ref[...] = low

    @pl.when(pl.program_id(0) == 0)
    def _():
        sums_ref[...] = jnp.zeros_like(sums_ref)

    sums_ref[0:1, :] += total(cot * normed)
    sums_ref[1:2, :] += total(cot)
    sums_ref[2:3, :] += total(low.astype(jnp.float32))


def down_kernel(
    branch_ref, slope_ref, top_ref, mid_ref, w_out_ref, w_up_ref, w_down_ref, rows_ref,
    inner_ref, mid_grad_ref, attended_ref, context_ref, sums_ref, ups_ref, *, chunk,
):
    @pl.when(pl.program_id(0) == 0)
    def _():
        sums_ref[...] = jnp.zeros_like(sums_ref)
        ups_ref[...] = jnp.zeros_like(ups_ref)

    gain_1 = rows_ref[1:2, :]
    branch = branch_ref[...]
    grad = top_ref[...]
    for at in range(0, w_up_ref.shape[1], chunk):
        piece = slice(at, at + chunk)
        inner = dot(branch, w_down_ref[piece, :], 1, 1) * slope_ref[:, piece].astype(jnp.float32)
        low = inner.astype(jnp.bfloat16)
        inner_ref[:, piece] = low
        ups_ref[0:1, piece] += total(low.astype(jnp.float32))
        grad = grad + dot(low, w_up_ref[:, piece], 1, 1)
    normed, scale = standard(mid_ref[...])
    back = standard_back(normed, scale, grad * gain_1)
    mid_grad_ref[...] = back
    low = back.astype(jnp.bfloat16)
    attended_ref[...] = low
    context_ref[...] = dot(low, w_out_ref[...], 1, 1).astype(jnp.bfloat16)
    sums_ref[0:1, :] += total(grad * normed)
    sums_ref[1:2, :] += total(grad)
    sums_ref[2:3, :] += total(low.astype(jnp.float32))


def tiled(tile, width):
    return pl.BlockSpec((tile, width), lambda n: (n, 0))


def whole(shape):
    return pl.BlockSpec(shape, lambda n: (0, 0))


def kept(shape):
    return pl.BlockSpec(shape, lambda n: (0, 0), pipeline_mode=pl.Buffered(1))


def feed_forward(context, stream_in, moving, cots, w_out, w_up, w_down, vectors, b_up, chunk=768):
    tokens, width = context.shape
    tile = SPAN // 2
    deep = w_up.shape[1]
    low, full = jnp.bfloat16, jnp.float32
    shapes = [(width, full), (width, low), (deep, low), (deep, low), (width, low), (width, full), (width, low)]
    return pl.pallas_call(
        functools.partial(up_kernel, chunk=chunk),
        grid=(tokens // tile,),
        in_specs=[tiled(tile, width)] * 2
        + [kept(w_out.shape), kept(w_up.shape), kept(w_down.shape), whole(vectors.shape), whole(b_up.shape)]
        + [pl.BlockSpec((1, tile, SPAN), lambda n: (n // 2, n % 2, 0))]
        + [by_half(part.shape[1:]) for part in cots],
        out_specs=[tiled(tile, n) for n, _ in shapes] + [whole((8, width))],
        out_shape=[jax.ShapeDtypeStruct((tokens, n), kind) for n, kind in shapes]
        + [jax.ShapeDtypeStruct((8, width), full)],
        compiler_params=pltpu.CompilerParams(vmem_limit_bytes=60 * 1024 * 1024),
        cost_estimate=pl.CostEstimate(flops=20_000_000_000, bytes_accessed=60_000_000, transcendentals=0),
        name="feed_forward",
    )(context, stream_in, w_out, w_up, w_down, vectors, b_up, moving, *cots)


def feed_back(branch, slope, top, mid, w_out, w_up, w_down, vectors, tile=SPAN // 2, chunk=768):
    tokens, width = branch.shape
    deep = w_up.shape[1]
    low, full = jnp.bfloat16, jnp.float32
    shapes = [(deep, low), (width, full), (width, low), (width, low)]
    return pl.pallas_call(
        functools.partial(down_kernel, chunk=chunk),
        grid=(tokens // tile,),
        in_specs=[tiled(tile, width), tiled(tile, deep), tiled(tile, width), tiled(tile, width)]
        + [kept(w_out.shape), kept(w_up.shape), kept(w_down.shape), whole(vectors.shape)],
        out_specs=[tiled(tile, n) for n, _ in shapes] + [whole((8, width)), whole((8, deep))],
        out_shape=[jax.ShapeDtypeStruct((tokens, n), kind) for n, kind in shapes]
        + [jax.ShapeDtypeStruct((8, width), full), jax.ShapeDtypeStruct((8, deep), full)],
        compiler_params=pltpu.CompilerParams(vmem_limit_bytes=60 * 1024 * 1024),
        cost_estimate=pl.CostEstimate(flops=20_000_000_000, bytes_accessed=60_000_000, transcendentals=0),
        name="feed_back",
    )(branch, slope, top, mid, w_out, w_up, w_down, vectors)


def leave_kernel(grad_ref, mid_ref, moving_ref, *refs):
    w_refs, out_ref = refs[:-1], refs[-1]
    width = mid_ref.shape[2]
    stream = mid_ref[0]
    for n, ref in enumerate(w_refs):
        stream = stream + dot(grad_ref[0, :, n * width : (n + 1) * width], ref[...], 1, 1)
    out_ref[...] = dot(moving_ref[0], stream.astype(jnp.bfloat16), 0, 0).astype(jnp.bfloat16)


def leave(grad, mid, moving, weights, row):
    _, span, width = mid.shape
    return pl.pallas_call(
        leave_kernel,
        grid=(1,),
        in_specs=[
            pl.BlockSpec((1, span, 3 * width), lambda n: (row, 0, 0)),
            pl.BlockSpec((1, span, width), lambda n: (row, 0, 0)),
            pl.BlockSpec((1, span, span), lambda n: (row, 0, 0)),
        ]
        + [kept(value.shape) for value in weights],
        out_specs=whole((span, width)),
        out_shape=jax.ShapeDtypeStruct((span, width), jnp.bfloat16),
        compiler_params=pltpu.CompilerParams(vmem_limit_bytes=60 * 1024 * 1024),
        cost_estimate=pl.CostEstimate(flops=3_000_000_000, bytes_accessed=9_000_000, transcendentals=0),
        name="leave",
    )(grad, mid, moving, *weights)


DP = "dp"
STREAM = "stream"


def swap(value, axis, bit):
    count = lax.axis_size(axis)
    return lax.ppermute(value, axis, [(i, i ^ bit) for i in range(count)])


def bits_of(axis):
    count = lax.axis_size(axis)
    return [1 << n for n in range(count.bit_length() - 1)]


def rounds():
    core, *chips = bits_of(DP)
    groups = [(DP, [core])] + [(DP, chips[n : n + 2]) for n in range(0, len(chips), 2)]
    places = bits_of(STREAM)
    return groups + [(STREAM, places[n : n + 2]) for n in range(0, len(places), 2)]


def masks_of(bits):
    return [sum(bit for n, bit in enumerate(bits) if pick >> n & 1) for pick in range(1, 1 << len(bits))]


def add_all(kept, got):
    total = kept + got[0]
    return total + (got[1] + got[2]) if len(got) > 1 else total


class Scatter:
    def __init__(self, values):
        self.names = [(axis, bit) for axis in (DP, STREAM) for bit in bits_of(axis)[::-1]]
        self.values = [value.reshape((2,) * len(self.names) + value.shape[1:]) for value in values]
        self.left = rounds()

    def send(self):
        axis, bits = self.left.pop(0)
        place = lax.axis_index(axis)
        count = lax.axis_size(axis)
        self.whole = 1 << len(bits) == count
        if self.whole:
            given = [value.reshape((count,) + value.shape[len(bits) :]) for value in self.values]
            self.kept = []
            self.got = [lax.all_to_all(joined(given, -1), axis, 0, 0, tiled=True)]
            self.sizes = [value.shape[-1] for value in self.values]
            self.names = [name for name in self.names if name[0] != axis]
            return
        dims = {bit: self.names.index((axis, bit)) for bit in bits}

        def pick(value, mask):
            at = [0] * value.ndim
            size = list(value.shape)
            for bit, dim in dims.items():
                at[dim] = ((place ^ mask) // bit) % 2
                size[dim] = 1
            part = lax.dynamic_slice(value, at, size)
            return part.reshape([n for dim, n in enumerate(size) if dim not in dims.values()])

        self.kept = [pick(value, 0) for value in self.values]
        self.got = [
            swap(joined([pick(value, mask) for value in self.values], -1), axis, mask)
            for mask in masks_of(bits)
        ]
        self.names = [name for name in self.names if name[0] != axis or name[1] not in bits]

    def add(self):
        if not self.got:
            return
        values, at = [], 0
        if self.whole:
            for size in self.sizes:
                values.append(jnp.sum(self.got[0][..., at : at + size].astype(jnp.float32), axis=0))
                at += size
        for kept in self.kept:
            got = [part[..., at : at + kept.shape[-1]].astype(jnp.float32) for part in self.got]
            at += kept.shape[-1]
            value = add_all(kept.astype(jnp.float32), got)
            values.append(value.astype(jnp.bfloat16) if self.left else value)
        self.values, self.got = values, []

    def next(self):
        self.add()
        if self.left:
            self.send()

    def finish(self):
        while self.left:
            self.next()
        self.add()
        return self.values


def advance(value, groups, extra=()):
    tied, got, held = lax.optimization_barrier((value, [group.got for group in groups], list(extra)))
    for group, parts in zip(groups, got):
        group.got = parts
        group.next()
    return tied, held


def together(*values):
    return lax.optimization_barrier(values)


def sum_over(value, groups):
    for axis, bits in groups:
        value = add_all(value, [swap(value, axis, mask) for mask in masks_of(bits)])
    return value


def turned(shift):
    count = lax.axis_size(STREAM)
    return [(i, (i + shift) % count) for i in range(count)]


def row_slices(value):
    count = lax.axis_size(STREAM)
    place = lax.axis_index(STREAM)
    block = value.shape[0] // count
    return [
        lax.dynamic_slice_in_dim(value, (place - shift) % count * block, block, 0) for shift in range(count)
    ]


def to_rows(parts):
    return parts[:1] + [lax.ppermute(part, STREAM, turned(-shift)) for shift, part in enumerate(parts) if shift]


def rows_back(value):
    count = lax.axis_size(STREAM)
    place = lax.axis_index(STREAM)
    rows, slots, width = value.shape
    parts = jnp.swapaxes(value.reshape(rows, count, slots // count, width), 0, 1)
    parts = jnp.concatenate([parts, parts], axis=0)
    parts = lax.dynamic_slice_in_dim(parts, (count - place) % count, count, 0)
    return lax.all_to_all(parts, STREAM, 0, 0, tiled=True)


def per_device(
    text_input,
    visual_features,
    receipt_text,
    receipt_visual,
    boxes,
    w_query,
    b_query,
    w_key,
    w_value,
    b_value,
    w_out,
    b_out,
    gain_attn,
    shift_attn,
    w_up,
    b_up,
    w_down,
    b_down,
    gain_ffn,
    shift_ffn,
    w_visual,
    b_visual,
    table_line,
    table_x,
    table_y,
    cotangent_text,
    cotangent_visual,
):
    floating = jnp.float32
    narrow = jnp.bfloat16
    width = text_input.shape[-1]
    rows, visual, channels = visual_features.shape
    text = receipt_text.shape[1]
    slots = text + visual
    world = lax.axis_size(DP) * lax.axis_size(STREAM)
    place = lax.axis_index(STREAM)
    first_row = place * rows

    text_parts = to_rows(row_slices(text_input))
    text_parts, cotangent_parts = lax.optimization_barrier((text_parts, row_slices(cotangent_text)))
    cotangent_parts = to_rows(cotangent_parts)

    def pad(value, fill=0, size=SPAN):
        extra = size - value.shape[1]
        return jnp.pad(value, ((0, 0), (0, extra)) + ((0, 0),) * (value.ndim - 2), constant_values=fill)

    seg_text = lax.dynamic_slice_in_dim(receipt_text, first_row, rows, 0)
    seg_visual = lax.dynamic_slice_in_dim(receipt_visual, first_row, rows, 0)
    box = lax.dynamic_slice_in_dim(boxes, first_row, rows, 1)
    index = jnp.arange(SPAN, dtype=jnp.int32)
    position = jnp.where(index < text, index, index - text)
    facts = jnp.stack(
        [
            jnp.broadcast_to(position, (rows, SPAN)),
            pad(box[0]),
            pad(box[1]),
            pad(jnp.concatenate([seg_text, seg_visual], axis=1), RECEIPTS),
            jnp.broadcast_to(index, (rows, SPAN)),
        ],
        axis=1,
    )
    own = lax.dynamic_slice_in_dim(
        jnp.concatenate([facts[:, :, :text], facts[:, :, :text]], axis=2), place * text_input.shape[1], text, 2
    )
    facts = jnp.concatenate([own, facts[:, :, text:]], axis=2)
    rank = facts[:, 3] * SPAN + facts[:, 4]
    seg = facts[:, 3]
    target = jnp.sum((rank[:, None, :] < rank[:, :, None]).astype(jnp.int32), axis=2)
    moved = target[:, None, :] == index[None, :, None]
    facts = facts[:, :4]
    facts = jnp.sum(jnp.where(moved[:, None], facts[:, :, None, :], 0), axis=3)
    col = jnp.pad(jnp.swapaxes(facts, 1, 2), ((0, 0), (0, 0), (0, 124)))
    row = jnp.pad(facts, ((0, 0), (0, 4), (0, 640 - SPAN)), constant_values=RECEIPTS)
    starts = jnp.sum(
        (seg[:, None, :] < jnp.arange(RECEIPTS + 1, dtype=jnp.int32)[None, :, None]).astype(jnp.int32), axis=2
    )
    plan = make_plan(starts)
    plane = jnp.concatenate([table_x, table_y], axis=1).astype(floating)
    lines = jnp.pad(table_line.astype(floating), ((0, 0), (0, 96)), constant_values=NONE)

    bias, places = make_bias(plan, col, row, plane, lines)
    moving = moved.astype(narrow)

    def unsort(value):
        return jnp.einsum("rps,rpd->rsd", moving, value, preferred_element_type=floating)

    def rowwise(array):
        return array.reshape(rows, SPAN, -1)

    weights = (w_query, w_key, w_value)
    b_qkv = jnp.concatenate([b_query, jnp.zeros_like(b_query), b_value]).astype(floating)
    stream_in, entered, qkv = enter(
        moving, text_parts, pad(visual_features, 0, SPAN - text), w_visual, b_visual.astype(floating)[None],
        weights, b_qkv[None],
    )
    qkv = rowwise(qkv)
    context, shares = attend(plan, qkv, row, bias)
    context, cotangent_parts = lax.optimization_barrier((context, cotangent_parts))
    context = context.reshape(-1, width)
    vectors = jnp.stack([b_out, gain_attn, shift_attn, b_down, gain_ffn, shift_ffn, b_out, b_out]).astype(floating)
    mid, hidden, active, slope, outcome, grad_top, grad_branch, ffn_sums = feed_forward(
        context, stream_in, moving, cotangent_parts + [pad(cotangent_visual, 0, SPAN - text)],
        w_out, w_up, w_down, vectors, b_up.astype(floating)[None],
    )

    def lines_of(value):
        return [value[:, n : n + width] for n in range(0, value.shape[1], width)]

    def weight_grad(left, right):
        return jnp.einsum("ti,tj->ij", left, right, preferred_element_type=floating)

    def chunks(part):
        return part.astype(narrow).reshape(world, part.shape[0] // world, -1)

    grad_w_down = chunks(weight_grad(active, grad_branch))
    grad_w_down, grad_branch, outcome = together(grad_w_down, grad_branch, outcome)
    downs = Scatter([grad_w_down])
    downs.send()
    out_rows = unsort(rowwise(outcome)).astype(narrow)
    out_visual = out_rows[:, text:slots]
    (grad_branch, out_rows), _ = advance((grad_branch, out_rows), [downs])
    out_text = rows_back(out_rows[:, :text])
    grad_inner, grad_mid, grad_attended, grad_context, attn_sums, up_sums = feed_back(
        grad_branch, slope, grad_top, mid, w_out, w_up, w_down, vectors
    )
    grad_inner, downs.got = lax.optimization_barrier((grad_inner, downs.got))
    grad_w_up = chunks(weight_grad(hidden, grad_inner))
    grad_w_out = chunks(weight_grad(context, grad_attended))
    grad_context, grad_w_out, grad_w_up = together(grad_context, grad_w_out, grad_w_up)
    ups = Scatter([grad_w_up, grad_w_out])
    ups.send()
    (grad_context, out_text), _ = advance((rowwise(grad_context), out_text), [downs])
    out_text = out_text.reshape((-1,) + out_text.shape[2:])

    grad_mid_rows = rowwise(grad_mid)

    grad_qkv_0, bins_0 = attend_back(plan, qkv, grad_context, places, shares, 0)
    grad_qkv_0, _ = advance(grad_qkv_0, [ups])
    grad_qkv_0, downs.got = lax.optimization_barrier((grad_qkv_0, downs.got))
    back_0 = leave(grad_qkv_0, grad_mid_rows, moving, weights, 0)
    got_0 = rows_back(back_0[None, :text])
    grad_context, back_0, grad_qkv_0 = together(grad_context, back_0, grad_qkv_0)
    grad_qkv, bins_1 = attend_back(plan, qkv, grad_context, places, shares, 1, grad_qkv_0)
    (grad_qkv, got_0), _ = advance((grad_qkv, got_0), [ups])
    flat_qkv = grad_qkv.reshape(-1, grad_qkv.shape[-1])
    grad_w_qkv = chunks(weight_grad(entered, flat_qkv))
    lasts = Scatter([grad_w_qkv])
    lasts.send()
    grad_qkv, lasts.kept = lax.optimization_barrier((grad_qkv, lasts.kept))
    back_1 = leave(grad_qkv, grad_mid_rows, moving, weights, 1)
    back_1, ups.got = lax.optimization_barrier((back_1, ups.got))
    grad_visual = jnp.stack([back_0[text:slots], back_1[text:slots]])
    grad_w_visual = jnp.einsum("rvc,rvd->cd", visual_features, grad_visual, preferred_element_type=floating)
    grad_w_visual = chunks(grad_w_visual)
    third = width // 3
    extra = Scatter([jnp.concatenate([grad_w_visual[:, :, n : n + third] for n in range(0, width, third)], axis=1)])
    extra.send()
    lasts.got, extra.got = lax.optimization_barrier((lasts.got, extra.got))
    lasts.add()
    extra.add()
    lasts.values += extra.values
    lasts.send()
    held = (back_1, grad_qkv, grad_visual, out_text, lasts.kept, ups.got, downs.got)
    held = lax.optimization_barrier(held)
    back_1, grad_qkv, grad_visual, out_text, lasts.kept, ups.got, downs.got = held
    got_1 = rows_back(back_1[None, :text])
    grad_b_qkv = jnp.sum(grad_qkv, axis=(0, 1), dtype=floating)
    grad_b_visual = jnp.sum(grad_visual, axis=(0, 1), dtype=floating)
    grad_features = jnp.einsum("rvd,cd->rvc", grad_visual, w_visual, preferred_element_type=floating)
    vectors = (ffn_sums, attn_sums, bins_0, bins_1, grad_b_qkv, grad_b_visual, up_sums)
    vectors, lasts.kept, ups.got, downs.got = lax.optimization_barrier((vectors, lasts.kept, ups.got, downs.got))
    ffn_sums, attn_sums, bins_0, bins_1, grad_b_qkv, grad_b_visual, up_sums = vectors
    small = jnp.concatenate(
        [ffn_sums, attn_sums, bins_0 + bins_1]
        + lines_of(grad_b_qkv[None]) + [grad_b_visual[None]] + lines_of(up_sums[:1]),
        axis=0,
    )
    out_text = jnp.where(place >= 0, out_text, 0.0)
    opening, *later = rounds()
    small = sum_over(small, [opening, later.pop()])
    (small, got_0, got_1, out_text), _ = advance((small, got_0, got_1, out_text), [lasts])
    small = sum_over(small, later)
    (down_sum,) = downs.finish()
    up_sum, out_sum = ups.finish()
    qkv_sum, visual_sum = lasts.finish()
    grad_text = jnp.stack([got_0[:, 0].astype(floating), got_1[:, 0].astype(floating)], axis=1)
    grad_text = grad_text.reshape((-1,) + grad_text.shape[2:])
    query_sum, key_sum, value_sum = (qkv_sum[:, n * width : (n + 1) * width] for n in range(3))
    visual_sum = visual_sum.reshape(3, -1, third)
    visual_sum = jnp.concatenate([visual_sum[n] for n in range(3)], axis=1)
    step = width // world
    device = lax.axis_index(DP) * lax.axis_size(STREAM) + place
    mine = lax.dynamic_slice_in_dim(small, device * step, step, 1)
    up_step = w_up.shape[1] // world
    bins = small[16 : 16 + HEADS]
    return (
        out_text,
        out_visual,
        grad_text,
        grad_features,
        query_sum,
        mine[32],
        key_sum,
        value_sum,
        mine[34],
        out_sum,
        mine[10],
        mine[8],
        mine[9],
        up_sum,
        lax.dynamic_slice_in_dim(small[36:].reshape(-1), device * up_step, up_step, 0),
        down_sum,
        mine[2],
        mine[0],
        mine[1],
        visual_sum,
        mine[35],
        bins[:, 128:160],
        bins[:, :64],
        bins[:, 64:128],
    )


def solution(mesh):
    placed = (
        P("dp", "stream", None),
        P(("dp", "stream"), None, None),
        P("dp", None),
        P("dp", None),
        P(None, "dp", None),
        P(),
        P(),
        P(),
        P(),
        P(),
        P(),
        P(),
        P(),
        P(),
        P(),
        P(),
        P(),
        P(),
        P(),
        P(),
        P(),
        P(),
        P(),
        P(),
        P(),
        P("dp", "stream", None),
        P(("dp", "stream"), None, None),
    )
    return jax.shard_map(
        per_device,
        mesh=mesh,
        in_specs=placed,
        out_specs=(
            P("dp", "stream", None),
            P(("dp", "stream"), None, None),
            P("dp", "stream", None),
            P(("dp", "stream"), None, None),
            P(("dp", "stream"), None),
            P(("dp", "stream")),
            P(("dp", "stream"), None),
            P(("dp", "stream"), None),
            P(("dp", "stream")),
            P(("dp", "stream"), None),
            P(("dp", "stream")),
            P(("dp", "stream")),
            P(("dp", "stream")),
            P(("dp", "stream"), None),
            P(("dp", "stream")),
            P(("dp", "stream"), None),
            P(("dp", "stream")),
            P(("dp", "stream")),
            P(("dp", "stream")),
            P(("dp", "stream"), None),
            P(("dp", "stream")),
            P(),
            P(),
            P(),
        ),
        check_vma=False,
    )
```

```python
import functools
import math

import jax, jax.numpy as jnp
from jax import lax
from jax.experimental import pallas as pl
from jax.experimental.pallas import tpu as pltpu
from jax.sharding import PartitionSpec as P

HEADS = 12
RECEIPTS = 8
VISUAL = 49
PLAN = 32
SPAN = 576
BINS = 160
NONE = -1e30
TALL = 192
WIDE = 256
FORWARD_PAIRS = 6
BACKWARD_PAIRS = 6


def thresholds(half, reach):
    exact = half // 2
    steps = half - exact
    return [
        int(math.floor(exact * (reach / exact) ** (power / steps) + 0.5))
        for power in range(1, steps)
    ]


def bucket(diff, count, reach):
    half = count // 2
    exact = half // 2
    dist = jnp.abs(diff)
    passed = jnp.where(diff > 0, half, 0)
    for limit in thresholds(half, reach):
        passed = passed + jnp.where(dist >= limit, 1, 0)
    return passed + jnp.minimum(dist, exact)


def dot(a, b, ca, cb):
    return lax.dot_general(a, b, (((ca,), (cb,)), ((), ())), preferred_element_type=jnp.float32)


def by_size(plan_ref, run, offset=0):
    step = pl.program_id(0)
    receipt = lax.rem(step, RECEIPTS)
    base = (step // RECEIPTS + offset) * PLAN + receipt
    first = plan_ref[base]
    last = plan_ref[base + 1]
    start = first // 16 * 16
    low = 0
    for tall in (64, 96, 128, 160, 192):
        wide = 128 if tall <= 128 else 256
        inside = last - start > low
        if tall < TALL:
            inside = jnp.logical_and(inside, last - start <= tall)
        low = tall

        @pl.when(inside)
        def _(tall=tall, wide=wide):
            at_k = pl.multiple_of(jnp.minimum(start, SPAN - tall), 16)
            at_q = pl.multiple_of(jnp.minimum(start, SPAN - wide), 16)
            run(receipt, first - at_k, last - at_k, at_k, at_q, tall, wide)


def blocks(refs, head, tile, tall):
    found = []
    for n, (which, lead) in enumerate((((0, ()), (1, ()), (2, (0,))), ((2, (1,)), (2, (2,)), (2, (3,))))[tile]):
        size = min(64, tall - 64 * n)
        if size > 0:
            found.append((refs[which], (0,) + lead + (head, pl.ds(0, size)), 64 * n, size))
    return found


def load(refs, head, tall, wide):
    return joined(
        [joined([ref[at] for ref, at, _, _ in blocks(refs, head, tile, tall)], 0) for tile in range(wide // 128)], 1
    )


def store(refs, head, value):
    tall, wide = value.shape
    for tile in range(wide // 128):
        for ref, at, row, size in blocks(refs, head, tile, tall):
            ref[at] = value[row : row + size, 128 * tile : 128 * tile + 128]


def joined(pieces, axis):
    return pieces[0] if len(pieces) == 1 else jnp.concatenate(pieces, axis=axis)


def bias_kernel(plan_ref, col_ref, row_ref, plane_ref, lines_ref, near_ref, mid_ref, far_ref, index_ref):
    refs = (near_ref, mid_ref, far_ref)
    height = 64

    def run(receipt, low, high, at_k, at_q, tall, wide):
        row = pltpu.roll(row_ref[0], lax.rem(640 - at_q, 640), 1)[:, :wide]
        shape = (height, 128)

        def fill(tile, n, at):
            _, lead = (((0, ()), (1, ()), (2, (0,))), ((2, (1,)), (2, (2,)), (2, (3,))))[tile][n]
            ref = refs[(((0, 1, 2), (2, 2, 2))[tile])[n]]
            lanes = slice(128 * tile, 128 * (tile + 1))
            here = 64 * n + at
            used = jnp.logical_and(here < high, here + height > low)

            @pl.when(jnp.logical_not(used))
            def _():
                for h in range(HEADS):
                    ref[(0,) + lead + (h, pl.ds(at, height))] = jnp.full(shape, NONE, jnp.float32)

            @pl.when(used)
            def _():
                col = col_ref[0, pl.ds(pl.multiple_of(at_k + here, 16), height), :]

                def spread(r):
                    return (jnp.broadcast_to(col[:, r : r + 1], shape), jnp.broadcast_to(row[r : r + 1, lanes], shape))

                def gap(r):
                    key, query = spread(r)
                    return key - query

                key, query = spread(3)
                same = jnp.logical_and(key == receipt, query == receipt)
                line = jnp.where(same, bucket(gap(0), 32, 128), 32)
                across = bucket(gap(1), 64, 256)
                down = bucket(gap(2), 64, 256) + 64
                index_ref[0, pl.ds(here, height), lanes] = across + down * 256 + line * 65536
                def look(table_ref, h, index):
                    table = jnp.broadcast_to(table_ref[h : h + 1, :], (8, 128))
                    return jnp.take_along_axis(table, index, axis=1, mode="promise_in_bounds")
                for r in range(height // 8):
                    a8, d8, l8 = (v[8 * r : 8 * r + 8] for v in (across, down, line))

                    xs = [look(plane_ref, h, a8) for h in range(HEADS)]
                    ys = [look(plane_ref, h, d8) for h in range(HEADS)]
                    ls = [look(lines_ref, h, l8) for h in range(HEADS)]
                    for h in range(HEADS):
                        ref[(0,) + lead + (h, pl.ds(at + 8 * r, 8))] = xs[h] + ys[h] + ls[h]

        for tile in range(wide // 128):
            for n in range(pl.cdiv(tall, 64)):
                fill(tile, n, 0)

    by_size(plan_ref, run)


def split_pair(value, scale=1.0):
    lane = lax.broadcasted_iota(jnp.int32, value.shape, 1)
    full = value.astype(jnp.float32) * scale
    low = jnp.where(lane < 64, full, 0.0).astype(value.dtype)
    high = jnp.where(lane < 64, 0.0, full).astype(value.dtype)
    return jnp.concatenate([low, high], axis=0)


def grouped(size):
    return [range(n, n + size) for n in range(0, HEADS // 2, size)]


def parts(pair, at_k, at_q, tall, wide):
    width = HEADS * 64
    return (
        (0, pl.ds(at_q, wide), pl.ds(128 * pair, 128)),
        (0, pl.ds(at_k, tall), pl.ds(width + 128 * pair, 128)),
        (0, pl.ds(at_k, tall), pl.ds(2 * width + 128 * pair, 128)),
    )


def gather_into(ref, where, value):
    ref[where] = (ref[where].astype(jnp.float32) + value).astype(ref.dtype)


def forward_kernel(plan_ref, qkv_ref, row_ref, *refs):
    bias_refs, out_ref, shares_refs = refs[:3], refs[3], refs[4:]

    @pl.when(lax.rem(pl.program_id(0), RECEIPTS) == 0)
    def _():
        out_ref[...] = jnp.zeros_like(out_ref)

    def run(receipt, low, high, at_k, at_q, tall, wide):
        owner = pltpu.roll(row_ref[0], lax.rem(640 - at_q, 640), 1)[3:4, :wide]
        mine = jnp.where(owner == receipt, 1.0, 0.0)
        for group in grouped(FORWARD_PAIRS):
            spots = [parts(pair, at_k, at_q, tall, wide) for pair in group]
            scores = [
                dot(split_pair(qkv_ref[keys], 0.125), qkv_ref[queries], 1, 1) for queries, keys, _ in spots
            ]
            shares = []
            for pair, score in zip(group, scores):
                halves = []
                for h in range(2):
                    part = score[h * tall : (h + 1) * tall] + load(bias_refs, 2 * pair + h, tall, wide)
                    expo = jnp.exp(part - jnp.max(part, axis=0, keepdims=True))
                    share = expo * (mine / jnp.sum(expo, axis=0, keepdims=True))
                    halves.append(share.astype(jnp.bfloat16))
                    store(shares_refs, 2 * pair + h, halves[h])
                shares.append(jnp.concatenate(halves, axis=0))
            results = [dot(share, split_pair(qkv_ref[values]), 0, 0) for share, (_, _, values) in zip(shares, spots)]
            for result, (queries, _, _) in zip(results, spots):
                gather_into(out_ref, queries, result)

    by_size(plan_ref, run)


def backward_kernel(offset, plan_ref, qkv_ref, g_ref, index_ref, *refs):
    shares_refs, (dqkv_ref, bins_ref, terms_s) = refs[:3], refs[-3:]

    @pl.when(pl.program_id(0) == 0)
    def _():
        bins_ref[...] = jnp.zeros_like(bins_ref)
        terms_s[...] = jnp.zeros_like(terms_s)


    @pl.when(lax.rem(pl.program_id(0), RECEIPTS) == 0)
    def _():
        dqkv_ref[...] = jnp.zeros_like(dqkv_ref)

    def run(receipt, low, high, at_k, at_q, tall, wide):
        for group in grouped(BACKWARD_PAIRS):
            spots = [parts(pair, at_k, at_q, tall, wide) for pair in group]
            grads = [g_ref[queries] for queries, _, _ in spots]
            parts_of = [
                dot(split_pair(qkv_ref[values]), grad, 1, 1) for grad, (_, _, values) in zip(grads, spots)
            ]
            shares, steps = [], []
            for pair, grad_probs in zip(group, parts_of):
                for h in range(2):
                    share = load(shares_refs, 2 * pair + h, tall, wide)
                    part = grad_probs[h * tall : (h + 1) * tall]
                    probs = share.astype(jnp.float32)
                    inner = jnp.sum(probs * part, axis=0, keepdims=True)
                    step = (probs * (part - inner)).astype(jnp.bfloat16)
                    wide_step = step.astype(jnp.float32)
                    for c in range(wide // 128):
                        lanes = slice(128 * c, 128 * c + 128)
                        terms_s[c, pl.ds(2 * pair + h, tall, stride=16), :] = wide_step[:, lanes]
                    shares.append(share)
                    steps.append(step)
            results = []
            for n, (queries, keys, values) in enumerate(spots):
                pair = slice(2 * n, 2 * n + 2)
                results.append((values, dot(jnp.concatenate(shares[pair], axis=1), split_pair(grads[n]), 1, 0)))
                query = split_pair(qkv_ref[queries], 0.125)
                results.append((keys, dot(jnp.concatenate(steps[pair], axis=1), query, 1, 0)))
                key = split_pair(qkv_ref[keys], 0.125)
                results.append((queries, dot(jnp.concatenate(steps[pair], axis=0), key, 0, 0)))
            for where, result in results:
                gather_into(dqkv_ref, where, result)

        group = 32
        level = lax.broadcasted_iota(jnp.int32, (BINS, 128), 0)

        def bin_step(n, total):
            hots, terms = [], []
            at = pl.multiple_of(n * group, group)
            for c in range(wide // 128):
                packed = index_ref[0, pl.ds(at, group), 128 * c : 128 * c + 128]
                x, y, line = packed & 255, (packed >> 8) & 255, (packed >> 16) + 128
                for i in range(group):
                    def spread(value, count):
                        return jnp.broadcast_to(value[i : i + 1, :], (count, 128))

                    index = jnp.concatenate([spread(x, 64), spread(y, 64), spread(line, 32)], axis=0)
                    hots.append(jnp.where(level == index, 1.0, 0.0).astype(jnp.bfloat16))
                    terms.append(terms_s[c, pl.ds(pl.multiple_of((at + i) * 16, 16), 16), :].astype(jnp.bfloat16))
            return total + dot(jnp.concatenate(terms, axis=1), jnp.concatenate(hots, axis=1), 1, 1)

        total = lax.fori_loop(low // group, pl.cdiv(high, group), bin_step, jnp.zeros((16, BINS), jnp.float32))
        bins_ref[:, :BINS] += total


    by_size(plan_ref, run, offset)


def of_row(shape, offset=0):
    return pl.BlockSpec((1,) + shape, lambda n, *_: (n // RECEIPTS + offset,) + (0,) * len(shape))


def of_step(shape, offset=0):
    return pl.BlockSpec((1,) + shape, lambda n, *_: (n + offset * RECEIPTS,) + (0,) * len(shape))


def of_plan(shape, offset, base, at):
    def place(n, plan_ref):
        row = n // RECEIPTS
        step = plan_ref[(row + offset) * PLAN + at + lax.rem(n, RECEIPTS)]
        return ((row + base) * RECEIPTS + step,) + (0,) * len(shape)

    return pl.BlockSpec((1,) + shape, place)


def tile_specs(offset=0, base=0):
    near, far = (HEADS, 64, 128), (4, HEADS, 64, 128)
    return [of_step(near, base), of_plan(near, offset, base, 16), of_plan(far, offset, base, 24)]


def tile_shapes(steps, kind):
    shapes = ((HEADS, 64, 128), (HEADS, 64, 128), (4, HEADS, 64, 128))
    return [jax.ShapeDtypeStruct((steps,) + shape, kind) for shape in shapes]


def fixed(shape):
    return pl.BlockSpec(shape, lambda n, *_: (0,) * len(shape))


def call(kernel, name, plan, args, in_specs, out_specs, out_shape, steps, cost, scratch=(), vmem=60, alias=None):
    return pl.pallas_call(
        kernel,
        grid_spec=pltpu.PrefetchScalarGridSpec(
            num_scalar_prefetch=1, grid=(steps,), in_specs=in_specs, out_specs=out_specs, scratch_shapes=scratch
        ),
        out_shape=out_shape,
        compiler_params=pltpu.CompilerParams(vmem_limit_bytes=vmem * 1024 * 1024),
        cost_estimate=pl.CostEstimate(flops=cost, bytes_accessed=cost // 1000, transcendentals=0),
        input_output_aliases=alias or {},
        name=name,
    )(plan, *args)


def make_bias(plan, col, row, plane, lines):
    steps = col.shape[0] * RECEIPTS
    *bias, index = call(
        bias_kernel, "make_bias", plan, (col, row, plane, lines),
        [of_row((640, 128)), of_row((8, 640)), fixed((HEADS, 128)), fixed((HEADS, 128))],
        tile_specs() + [of_step((TALL, WIDE))],
        tile_shapes(steps, jnp.float32) + [jax.ShapeDtypeStruct((steps, TALL, WIDE), jnp.int32)],
        steps, 30_000_000_000,
    )
    return bias, index


def attend(plan, qkv, row, bias):
    rows, span, width = qkv.shape
    steps = rows * RECEIPTS
    out, *shares = call(
        forward_kernel, "attend", plan, (qkv, row, *bias),
        [of_row((span, width)), of_row((8, 640))] + tile_specs(),
        [of_row((span, width // 3))] + tile_specs(),
        [jax.ShapeDtypeStruct((rows, span, width // 3), qkv.dtype)] + tile_shapes(steps, jnp.bfloat16),
        steps, 20_000_000_000,
    )
    return out, shares


def attend_back(plan, qkv, g, index, shares, first, before=None):
    rows, span, width = qkv.shape
    bins = (16, width // 3)
    specs = [of_row((span, width), first), of_row((span, width // 3), first), of_step((TALL, WIDE), first)]
    args = (qkv, g, index, *shares)
    specs += tile_specs(first, first)
    alias = {}
    if before is not None:
        args += (before,)
        specs.append(pl.BlockSpec(memory_space=pl.ANY))
        alias = {len(args): 0}
    return call(
        functools.partial(backward_kernel, first), "attend_back", plan, args, specs,
        [of_row((span, width), first), fixed(bins)],
        [jax.ShapeDtypeStruct((rows, span, width), qkv.dtype), jax.ShapeDtypeStruct(bins, jnp.float32)],
        RECEIPTS, 20_000_000_000, [pltpu.VMEM((2, TALL * 16, 128), jnp.float32)], alias=alias,
    )


def make_plan(starts):
    first, last = starts[:, :-1], starts[:, 1:]
    span = last - first // 16 * 16
    order = jnp.arange(RECEIPTS, dtype=jnp.int32)

    def latest(need):
        passed = need[:, None, :] & (order[None, :] <= order[:, None])[None]
        behind = jnp.max(jnp.where(passed, order, -1), axis=2)
        ahead = jnp.min(jnp.where(need, order, RECEIPTS - 1), axis=1, keepdims=True)
        return jnp.where(behind < 0, ahead, behind)

    bounds = jnp.pad(starts, ((0, 0), (0, 15 - RECEIPTS)))
    return jnp.concatenate([bounds, latest(span > 64), latest(span > 128)], axis=1).reshape(-1)


EPSILON = 1e-05


def gelu_parts(u):
    expo = jnp.exp(u * u * -0.5)
    share = 0.5 + 0.5 * lax.erf(u * (1.0 / math.sqrt(2.0)))
    return u * share, share + u * expo * (1.0 / math.sqrt(2.0 * math.pi))


def standard(values):
    centred = values - jnp.mean(values, axis=1, keepdims=True)
    scale = lax.rsqrt(jnp.mean(centred * centred, axis=1, keepdims=True) + EPSILON)
    return centred * scale, scale


def standard_back(normed, scale, grad):
    return (
        grad - jnp.mean(grad, axis=1, keepdims=True) - normed * jnp.mean(grad * normed, axis=1, keepdims=True)
    ) * scale


def total(value):
    return jnp.sum(value, axis=0, keepdims=True)


def sorted_sum(moving, parts):
    value, at = 0.0, 0
    for part in parts:
        count = part.shape[1]
        value = value + dot(moving[:, at : at + count], part[0], 1, 0)
        at += count
    return value


def enter_kernel(*refs):
    count = len(refs) - 11
    moving_ref, *part_refs = refs[: count + 1]
    features_ref, w_visual_ref, b_visual_ref, *w_refs, b_qkv_ref, stream_ref, low_ref, qkv_ref = refs[count + 1 :]
    moving = moving_ref[0]
    text = sum(ref.shape[1] for ref in part_refs)
    at_visual = moving[:, text:]
    features = dot(at_visual, features_ref[0], 1, 0).astype(jnp.bfloat16)
    lane = lax.broadcasted_iota(jnp.int32, at_visual.shape, 1)
    is_visual = jnp.sum(jnp.where(lane < VISUAL, at_visual.astype(jnp.float32), 0.0), axis=1, keepdims=True)
    visual = dot(features, w_visual_ref[...], 1, 0) + b_visual_ref[...]
    stream = sorted_sum(moving, part_refs) + visual * is_visual
    stream_ref[...] = stream
    low = stream.astype(jnp.bfloat16)
    low_ref[...] = low
    width = low.shape[1]
    for n, ref in enumerate(w_refs):
        lanes = slice(n * width, (n + 1) * width)
        qkv_ref[:, lanes] = (dot(low, ref[...], 1, 0) + b_qkv_ref[:, lanes]).astype(jnp.bfloat16)


def by_half(shape):
    return pl.BlockSpec((1,) + shape, lambda n: (n // 2, 0, 0))


def enter(moving, parts, features, w_visual, b_visual, weights, b_qkv):
    rows = moving.shape[0]
    width = w_visual.shape[1]
    tile = SPAN // 2
    tokens = rows * SPAN
    return pl.pallas_call(
        enter_kernel,
        grid=(2 * rows,),
        in_specs=[pl.BlockSpec((1, tile, SPAN), lambda n: (n // 2, n % 2, 0))]
        + [by_half(part.shape[1:]) for part in (*parts, features)]
        + [kept(value.shape) for value in (w_visual, b_visual, *weights, b_qkv)],
        out_specs=[tiled(tile, width), tiled(tile, width), tiled(tile, 3 * width)],
        out_shape=[
            jax.ShapeDtypeStruct((tokens, width), jnp.float32),
            jax.ShapeDtypeStruct((tokens, width), jnp.bfloat16),
            jax.ShapeDtypeStruct((tokens, 3 * width), jnp.bfloat16),
        ],
        compiler_params=pltpu.CompilerParams(vmem_limit_bytes=60 * 1024 * 1024),
        cost_estimate=pl.CostEstimate(flops=8_000_000_000, bytes_accessed=20_000_000, transcendentals=0),
        name="enter",
    )(moving, *parts, features, w_visual, b_visual, *weights, b_qkv)


def up_kernel(context_ref, stream_ref, w_out_ref, w_up_ref, w_down_ref, rows_ref, b_up_ref, moving_ref, *refs, chunk):
    part_refs = refs[:-8]
    mid_ref, hidden_ref, active_ref, slope_ref, out_ref, top_ref, branch_ref, sums_ref = refs[-8:]
    b_out, gain_1, shift_1, b_down, gain_2, shift_2 = (rows_ref[n : n + 1, :] for n in range(6))
    mid = stream_ref[...] + dot(context_ref[...], w_out_ref[...], 1, 0) + b_out
    mid_ref[...] = mid
    norm_one = standard(mid)[0] * gain_1 + shift_1
    hidden = norm_one.astype(jnp.bfloat16)
    hidden_ref[...] = hidden
    branch = norm_one + b_down
    for at in range(0, w_up_ref.shape[1], chunk):
        piece = slice(at, at + chunk)
        inner = dot(hidden, w_up_ref[:, piece], 1, 0) + b_up_ref[:, piece]
        active, slope = gelu_parts(inner)
        active = active.astype(jnp.bfloat16)
        active_ref[:, piece] = active
        slope_ref[:, piece] = slope.astype(jnp.bfloat16)
        branch = branch + dot(active, w_down_ref[piece, :], 1, 0)
    normed, scale = standard(branch)
    out_ref[...] = (normed * gain_2 + shift_2).astype(jnp.bfloat16)
    cot = sorted_sum(moving_ref[0], part_refs)
    top = standard_back(normed, scale, cot * gain_2)
    top_ref[...] = top
    low = top.astype(jnp.bfloat16)
    branch_ref[...] = low

    @pl.when(pl.program_id(0) == 0)
    def _():
        sums_ref[...] = jnp.zeros_like(sums_ref)

    sums_ref[0:1, :] += total(cot * normed)
    sums_ref[1:2, :] += total(cot)
    sums_ref[2:3, :] += total(low.astype(jnp.float32))


def down_kernel(
    branch_ref, slope_ref, top_ref, mid_ref, w_out_ref, w_up_ref, w_down_ref, rows_ref,
    inner_ref, mid_grad_ref, attended_ref, context_ref, sums_ref, ups_ref, *, chunk,
):
    @pl.when(pl.program_id(0) == 0)
    def _():
        sums_ref[...] = jnp.zeros_like(sums_ref)
        ups_ref[...] = jnp.zeros_like(ups_ref)

    gain_1 = rows_ref[1:2, :]
    branch = branch_ref[...]
    grad = top_ref[...]
    for at in range(0, w_up_ref.shape[1], chunk):
        piece = slice(at, at + chunk)
        inner = dot(branch, w_down_ref[piece, :], 1, 1) * slope_ref[:, piece].astype(jnp.float32)
        low = inner.astype(jnp.bfloat16)
        inner_ref[:, piece] = low
        ups_ref[0:1, piece] += total(low.astype(jnp.float32))
        grad = grad + dot(low, w_up_ref[:, piece], 1, 1)
    normed, scale = standard(mid_ref[...])
    back = standard_back(normed, scale, grad * gain_1)
    mid_grad_ref[...] = back
    low = back.astype(jnp.bfloat16)
    attended_ref[...] = low
    context_ref[...] = dot(low, w_out_ref[...], 1, 1).astype(jnp.bfloat16)
    sums_ref[0:1, :] += total(grad * normed)
    sums_ref[1:2, :] += total(grad)
    sums_ref[2:3, :] += total(low.astype(jnp.float32))


def tiled(tile, width):
    return pl.BlockSpec((tile, width), lambda n: (n, 0))


def whole(shape):
    return pl.BlockSpec(shape, lambda n: (0, 0))


def kept(shape):
    return pl.BlockSpec(shape, lambda n: (0, 0), pipeline_mode=pl.Buffered(1))


def feed_forward(context, stream_in, moving, cots, w_out, w_up, w_down, vectors, b_up, chunk=768):
    tokens, width = context.shape
    tile = SPAN // 2
    deep = w_up.shape[1]
    low, full = jnp.bfloat16, jnp.float32
    shapes = [(width, full), (width, low), (deep, low), (deep, low), (width, low), (width, full), (width, low)]
    return pl.pallas_call(
        functools.partial(up_kernel, chunk=chunk),
        grid=(tokens // tile,),
        in_specs=[tiled(tile, width)] * 2
        + [kept(w_out.shape), kept(w_up.shape), kept(w_down.shape), whole(vectors.shape), whole(b_up.shape)]
        + [pl.BlockSpec((1, tile, SPAN), lambda n: (n // 2, n % 2, 0))]
        + [by_half(part.shape[1:]) for part in cots],
        out_specs=[tiled(tile, n) for n, _ in shapes] + [whole((8, width))],
        out_shape=[jax.ShapeDtypeStruct((tokens, n), kind) for n, kind in shapes]
        + [jax.ShapeDtypeStruct((8, width), full)],
        compiler_params=pltpu.CompilerParams(vmem_limit_bytes=60 * 1024 * 1024),
        cost_estimate=pl.CostEstimate(flops=20_000_000_000, bytes_accessed=60_000_000, transcendentals=0),
        name="feed_forward",
    )(context, stream_in, w_out, w_up, w_down, vectors, b_up, moving, *cots)


def feed_back(branch, slope, top, mid, w_out, w_up, w_down, vectors, tile=SPAN // 2, chunk=768):
    tokens, width = branch.shape
    deep = w_up.shape[1]
    low, full = jnp.bfloat16, jnp.float32
    shapes = [(deep, low), (width, full), (width, low), (width, low)]
    return pl.pallas_call(
        functools.partial(down_kernel, chunk=chunk),
        grid=(tokens // tile,),
        in_specs=[tiled(tile, width), tiled(tile, deep), tiled(tile, width), tiled(tile, width)]
        + [kept(w_out.shape), kept(w_up.shape), kept(w_down.shape), whole(vectors.shape)],
        out_specs=[tiled(tile, n) for n, _ in shapes] + [whole((8, width)), whole((8, deep))],
        out_shape=[jax.ShapeDtypeStruct((tokens, n), kind) for n, kind in shapes]
        + [jax.ShapeDtypeStruct((8, width), full), jax.ShapeDtypeStruct((8, deep), full)],
        compiler_params=pltpu.CompilerParams(vmem_limit_bytes=60 * 1024 * 1024),
        cost_estimate=pl.CostEstimate(flops=20_000_000_000, bytes_accessed=60_000_000, transcendentals=0),
        name="feed_back",
    )(branch, slope, top, mid, w_out, w_up, w_down, vectors)


def leave_kernel(grad_ref, mid_ref, moving_ref, *refs):
    w_refs, out_ref = refs[:-1], refs[-1]
    width = mid_ref.shape[2]
    stream = mid_ref[0]
    for n, ref in enumerate(w_refs):
        stream = stream + dot(grad_ref[0, :, n * width : (n + 1) * width], ref[...], 1, 1)
    out_ref[...] = dot(moving_ref[0], stream.astype(jnp.bfloat16), 0, 0).astype(jnp.bfloat16)


def leave(grad, mid, moving, weights, row):
    _, span, width = mid.shape
    return pl.pallas_call(
        leave_kernel,
        grid=(1,),
        in_specs=[
            pl.BlockSpec((1, span, 3 * width), lambda n: (row, 0, 0)),
            pl.BlockSpec((1, span, width), lambda n: (row, 0, 0)),
            pl.BlockSpec((1, span, span), lambda n: (row, 0, 0)),
        ]
        + [kept(value.shape) for value in weights],
        out_specs=whole((span, width)),
        out_shape=jax.ShapeDtypeStruct((span, width), jnp.bfloat16),
        compiler_params=pltpu.CompilerParams(vmem_limit_bytes=60 * 1024 * 1024),
        cost_estimate=pl.CostEstimate(flops=3_000_000_000, bytes_accessed=9_000_000, transcendentals=0),
        name="leave",
    )(grad, mid, moving, *weights)


DP = "dp"
STREAM = "stream"


def swap(value, axis, bit):
    count = lax.axis_size(axis)
    return lax.ppermute(value, axis, [(i, i ^ bit) for i in range(count)])


def bits_of(axis):
    count = lax.axis_size(axis)
    return [1 << n for n in range(count.bit_length() - 1)]


def rounds():
    core, *chips = bits_of(DP)
    groups = [(DP, [core])] + [(DP, chips[n : n + 2]) for n in range(0, len(chips), 2)]
    places = bits_of(STREAM)
    return groups + [(STREAM, places[n : n + 2]) for n in range(0, len(places), 2)]


def masks_of(bits):
    return [sum(bit for n, bit in enumerate(bits) if pick >> n & 1) for pick in range(1, 1 << len(bits))]


def add_all(kept, got):
    total = kept + got[0]
    return total + (got[1] + got[2]) if len(got) > 1 else total


class Scatter:
    def __init__(self, values):
        self.names = [(axis, bit) for axis in (DP, STREAM) for bit in bits_of(axis)[::-1]]
        self.values = [value.reshape((2,) * len(self.names) + value.shape[1:]) for value in values]
        self.left = rounds()

    def send(self):
        axis, bits = self.left.pop(0)
        place = lax.axis_index(axis)
        count = lax.axis_size(axis)
        self.whole = 1 << len(bits) == count
        if self.whole:
            given = [value.reshape((count,) + value.shape[len(bits) :]) for value in self.values]
            self.kept = []
            self.got = [lax.all_to_all(joined(given, -1), axis, 0, 0, tiled=True)]
            self.sizes = [value.shape[-1] for value in self.values]
            self.names = [name for name in self.names if name[0] != axis]
            return
        dims = {bit: self.names.index((axis, bit)) for bit in bits}

        def pick(value, mask):
            at = [0] * value.ndim
            size = list(value.shape)
            for bit, dim in dims.items():
                at[dim] = ((place ^ mask) // bit) % 2
                size[dim] = 1
            part = lax.dynamic_slice(value, at, size)
            return part.reshape([n for dim, n in enumerate(size) if dim not in dims.values()])

        self.kept = [pick(value, 0) for value in self.values]
        self.got = [
            swap(joined([pick(value, mask) for value in self.values], -1), axis, mask)
            for mask in masks_of(bits)
        ]
        self.names = [name for name in self.names if name[0] != axis or name[1] not in bits]

    def add(self):
        if not self.got:
            return
        values, at = [], 0
        if self.whole:
            for size in self.sizes:
                values.append(jnp.sum(self.got[0][..., at : at + size].astype(jnp.float32), axis=0))
                at += size
        for kept in self.kept:
            got = [part[..., at : at + kept.shape[-1]].astype(jnp.float32) for part in self.got]
            at += kept.shape[-1]
            value = add_all(kept.astype(jnp.float32), got)
            values.append(value.astype(jnp.bfloat16) if self.left else value)
        self.values, self.got = values, []

    def next(self):
        self.add()
        if self.left:
            self.send()

    def finish(self):
        while self.left:
            self.next()
        self.add()
        return self.values


def advance(value, groups, extra=()):
    tied, got, held = lax.optimization_barrier((value, [group.got for group in groups], list(extra)))
    for group, parts in zip(groups, got):
        group.got = parts
        group.next()
    return tied, held


def together(*values):
    return lax.optimization_barrier(values)


def sum_over(value, groups):
    for axis, bits in groups:
        value = add_all(value, [swap(value, axis, mask) for mask in masks_of(bits)])
    return value


def turned(shift):
    count = lax.axis_size(STREAM)
    return [(i, (i + shift) % count) for i in range(count)]


def row_slices(value):
    count = lax.axis_size(STREAM)
    place = lax.axis_index(STREAM)
    block = value.shape[0] // count
    return [
        lax.dynamic_slice_in_dim(value, (place - shift) % count * block, block, 0) for shift in range(count)
    ]


def to_rows(parts):
    return parts[:1] + [lax.ppermute(part, STREAM, turned(-shift)) for shift, part in enumerate(parts) if shift]


def rows_back(value):
    count = lax.axis_size(STREAM)
    place = lax.axis_index(STREAM)
    rows, slots, width = value.shape
    parts = jnp.swapaxes(value.reshape(rows, count, slots // count, width), 0, 1)
    parts = jnp.concatenate([parts, parts], axis=0)
    parts = lax.dynamic_slice_in_dim(parts, (count - place) % count, count, 0)
    return lax.all_to_all(parts, STREAM, 0, 0, tiled=True)


def per_device(
    text_input,
    visual_features,
    receipt_text,
    receipt_visual,
    boxes,
    w_query,
    b_query,
    w_key,
    w_value,
    b_value,
    w_out,
    b_out,
    gain_attn,
    shift_attn,
    w_up,
    b_up,
    w_down,
    b_down,
    gain_ffn,
    shift_ffn,
    w_visual,
    b_visual,
    table_line,
    table_x,
    table_y,
    cotangent_text,
    cotangent_visual,
):
    floating = jnp.float32
    narrow = jnp.bfloat16
    width = text_input.shape[-1]
    rows, visual, channels = visual_features.shape
    text = receipt_text.shape[1]
    slots = text + visual
    world = lax.axis_size(DP) * lax.axis_size(STREAM)
    place = lax.axis_index(STREAM)
    first_row = place * rows

    text_parts = to_rows(row_slices(text_input))
    text_parts, cotangent_parts = lax.optimization_barrier((text_parts, row_slices(cotangent_text)))
    cotangent_parts = to_rows(cotangent_parts)

    def pad(value, fill=0, size=SPAN):
        extra = size - value.shape[1]
        return jnp.pad(value, ((0, 0), (0, extra)) + ((0, 0),) * (value.ndim - 2), constant_values=fill)

    seg_text = lax.dynamic_slice_in_dim(receipt_text, first_row, rows, 0)
    seg_visual = lax.dynamic_slice_in_dim(receipt_visual, first_row, rows, 0)
    box = lax.dynamic_slice_in_dim(boxes, first_row, rows, 1)
    index = jnp.arange(SPAN, dtype=jnp.int32)
    position = jnp.where(index < text, index, index - text)
    facts = jnp.stack(
        [
            jnp.broadcast_to(position, (rows, SPAN)),
            pad(box[0]),
            pad(box[1]),
            pad(jnp.concatenate([seg_text, seg_visual], axis=1), RECEIPTS),
            jnp.broadcast_to(index, (rows, SPAN)),
        ],
        axis=1,
    )
    own = lax.dynamic_slice_in_dim(
        jnp.concatenate([facts[:, :, :text], facts[:, :, :text]], axis=2), place * text_input.shape[1], text, 2
    )
    facts = jnp.concatenate([own, facts[:, :, text:]], axis=2)
    rank = facts[:, 3] * SPAN + facts[:, 4]
    seg = facts[:, 3]
    target = jnp.sum((rank[:, None, :] < rank[:, :, None]).astype(jnp.int32), axis=2)
    moved = target[:, None, :] == index[None, :, None]
    facts = facts[:, :4]
    facts = jnp.sum(jnp.where(moved[:, None], facts[:, :, None, :], 0), axis=3)
    col = jnp.pad(jnp.swapaxes(facts, 1, 2), ((0, 0), (0, 640 - SPAN), (0, 124)), constant_values=RECEIPTS)
    row = jnp.pad(facts, ((0, 0), (0, 4), (0, 640 - SPAN)), constant_values=RECEIPTS)
    starts = jnp.sum(
        (seg[:, None, :] < jnp.arange(RECEIPTS + 1, dtype=jnp.int32)[None, :, None]).astype(jnp.int32), axis=2
    )
    plan = make_plan(starts)
    plane = jnp.concatenate([table_x, table_y], axis=1).astype(floating)
    lines = jnp.pad(table_line.astype(floating), ((0, 0), (0, 96)), constant_values=NONE)

    bias, places = make_bias(plan, col, row, plane, lines)
    moving = moved.astype(narrow)

    def unsort(value):
        return jnp.einsum("rps,rpd->rsd", moving, value, preferred_element_type=floating)

    def rowwise(array):
        return array.reshape(rows, SPAN, -1)

    weights = (w_query, w_key, w_value)
    b_qkv = jnp.concatenate([b_query, jnp.zeros_like(b_query), b_value]).astype(floating)
    stream_in, entered, qkv = enter(
        moving, text_parts, pad(visual_features, 0, SPAN - text), w_visual, b_visual.astype(floating)[None],
        weights, b_qkv[None],
    )
    qkv = rowwise(qkv)
    context, shares = attend(plan, qkv, row, bias)
    context, cotangent_parts = lax.optimization_barrier((context, cotangent_parts))
    context = context.reshape(-1, width)
    vectors = jnp.stack([b_out, gain_attn, shift_attn, b_down, gain_ffn, shift_ffn, b_out, b_out]).astype(floating)
    mid, hidden, active, slope, outcome, grad_top, grad_branch, ffn_sums = feed_forward(
        context, stream_in, moving, cotangent_parts + [pad(cotangent_visual, 0, SPAN - text)],
        w_out, w_up, w_down, vectors, b_up.astype(floating)[None],
    )

    def lines_of(value):
        return [value[:, n : n + width] for n in range(0, value.shape[1], width)]

    def weight_grad(left, right):
        return jnp.einsum("ti,tj->ij", left, right, preferred_element_type=floating)

    def chunks(part):
        return part.astype(narrow).reshape(world, part.shape[0] // world, -1)

    grad_w_down = chunks(weight_grad(active, grad_branch))
    grad_w_down, grad_branch, outcome = together(grad_w_down, grad_branch, outcome)
    downs = Scatter([grad_w_down])
    downs.send()
    out_rows = unsort(rowwise(outcome)).astype(narrow)
    out_visual = out_rows[:, text:slots]
    (grad_branch, out_rows), _ = advance((grad_branch, out_rows), [downs])
    out_text = rows_back(out_rows[:, :text])
    grad_inner, grad_mid, grad_attended, grad_context, attn_sums, up_sums = feed_back(
        grad_branch, slope, grad_top, mid, w_out, w_up, w_down, vectors
    )
    grad_inner, downs.got = lax.optimization_barrier((grad_inner, downs.got))
    grad_w_up = chunks(weight_grad(hidden, grad_inner))
    grad_w_out = chunks(weight_grad(context, grad_attended))
    grad_context, grad_w_out, grad_w_up = together(grad_context, grad_w_out, grad_w_up)
    ups = Scatter([grad_w_up, grad_w_out])
    ups.send()
    grad_context, out_text = together(rowwise(grad_context), out_text)
    out_text = out_text.reshape((-1,) + out_text.shape[2:])

    grad_mid_rows = rowwise(grad_mid)

    grad_qkv_0, bins_0 = attend_back(plan, qkv, grad_context, places, shares, 0)
    grad_qkv_0, _ = advance(grad_qkv_0, [ups])
    grad_qkv_0, downs.got = lax.optimization_barrier((grad_qkv_0, downs.got))
    back_0 = leave(grad_qkv_0, grad_mid_rows, moving, weights, 0)
    got_0 = rows_back(back_0[None, :text])
    grad_context, back_0, grad_qkv_0 = together(grad_context, back_0, grad_qkv_0)
    grad_qkv, bins_1 = attend_back(plan, qkv, grad_context, places, shares, 1, grad_qkv_0)
    (grad_qkv, got_0), _ = advance((grad_qkv, got_0), [ups])
    flat_qkv = grad_qkv.reshape(-1, grad_qkv.shape[-1])
    grad_w_qkv = chunks(weight_grad(entered, flat_qkv))
    lasts = Scatter([grad_w_qkv])
    lasts.send()
    grad_qkv, lasts.kept = lax.optimization_barrier((grad_qkv, lasts.kept))
    back_1 = leave(grad_qkv, grad_mid_rows, moving, weights, 1)
    back_1, ups.got = lax.optimization_barrier((back_1, ups.got))
    grad_visual = jnp.stack([back_0[text:slots], back_1[text:slots]])
    grad_w_visual = jnp.einsum("rvc,rvd->cd", visual_features, grad_visual, preferred_element_type=floating)
    grad_w_visual = chunks(grad_w_visual)
    third = width // 3
    extra = Scatter([jnp.concatenate([grad_w_visual[:, :, n : n + third] for n in range(0, width, third)], axis=1)])
    extra.send()
    lasts.got, extra.got = lax.optimization_barrier((lasts.got, extra.got))
    lasts.add()
    extra.add()
    lasts.values += extra.values
    lasts.send()
    held = (back_1, grad_qkv, grad_visual, out_text, lasts.kept, ups.got, downs.got)
    held = lax.optimization_barrier(held)
    back_1, grad_qkv, grad_visual, out_text, lasts.kept, ups.got, downs.got = held
    got_1 = rows_back(back_1[None, :text])
    got_1, downs.got = lax.optimization_barrier((got_1, downs.got))
    downs.next()
    grad_b_qkv = jnp.sum(grad_qkv, axis=(0, 1), dtype=floating)
    grad_b_visual = jnp.sum(grad_visual, axis=(0, 1), dtype=floating)
    grad_features = jnp.einsum("rvd,cd->rvc", grad_visual, w_visual, preferred_element_type=floating)
    vectors = (ffn_sums, attn_sums, bins_0, bins_1, grad_b_qkv, grad_b_visual, up_sums)
    vectors, lasts.kept, ups.got, downs.got = lax.optimization_barrier((vectors, lasts.kept, ups.got, downs.got))
    ffn_sums, attn_sums, bins_0, bins_1, grad_b_qkv, grad_b_visual, up_sums = vectors
    small = jnp.concatenate(
        [ffn_sums, attn_sums, bins_0 + bins_1]
        + lines_of(grad_b_qkv[None]) + [grad_b_visual[None]] + lines_of(up_sums[:1]),
        axis=0,
    )
    out_text = jnp.where(place >= 0, out_text, 0.0)
    opening, *later = rounds()
    small = sum_over(small, [opening, later.pop()])
    (small, got_0, got_1, out_text), _ = advance((small, got_0, got_1, out_text), [lasts])
    small = sum_over(small, later)
    (down_sum,) = downs.finish()
    up_sum, out_sum = ups.finish()
    qkv_sum, visual_sum = lasts.finish()
    grad_text = jnp.stack([got_0[:, 0].astype(floating), got_1[:, 0].astype(floating)], axis=1)
    grad_text = grad_text.reshape((-1,) + grad_text.shape[2:])
    query_sum, key_sum, value_sum = (qkv_sum[:, n * width : (n + 1) * width] for n in range(3))
    visual_sum = visual_sum.reshape(3, -1, third)
    visual_sum = jnp.concatenate([visual_sum[n] for n in range(3)], axis=1)
    step = width // world
    device = lax.axis_index(DP) * lax.axis_size(STREAM) + place
    mine = lax.dynamic_slice_in_dim(small, device * step, step, 1)
    up_step = w_up.shape[1] // world
    bins = small[16 : 16 + HEADS]
    return (
        out_text,
        out_visual,
        grad_text,
        grad_features,
        query_sum,
        mine[32],
        key_sum,
        value_sum,
        mine[34],
        out_sum,
        mine[10],
        mine[8],
        mine[9],
        up_sum,
        lax.dynamic_slice_in_dim(small[36:].reshape(-1), device * up_step, up_step, 0),
        down_sum,
        mine[2],
        mine[0],
        mine[1],
        visual_sum,
        mine[35],
        bins[:, 128:160],
        bins[:, :64],
        bins[:, 64:128],
    )


def solution(mesh):
    placed = (
        P("dp", "stream", None),
        P(("dp", "stream"), None, None),
        P("dp", None),
        P("dp", None),
        P(None, "dp", None),
        P(),
        P(),
        P(),
        P(),
        P(),
        P(),
        P(),
        P(),
        P(),
        P(),
        P(),
        P(),
        P(),
        P(),
        P(),
        P(),
        P(),
        P(),
        P(),
        P(),
        P("dp", "stream", None),
        P(("dp", "stream"), None, None),
    )
    return jax.shard_map(
        per_device,
        mesh=mesh,
        in_specs=placed,
        out_specs=(
            P("dp", "stream", None),
            P(("dp", "stream"), None, None),
            P("dp", "stream", None),
            P(("dp", "stream"), None, None),
            P(("dp", "stream"), None),
            P(("dp", "stream")),
            P(("dp", "stream"), None),
            P(("dp", "stream"), None),
            P(("dp", "stream")),
            P(("dp", "stream"), None),
            P(("dp", "stream")),
            P(("dp", "stream")),
            P(("dp", "stream")),
            P(("dp", "stream"), None),
            P(("dp", "stream")),
            P(("dp", "stream"), None),
            P(("dp", "stream")),
            P(("dp", "stream")),
            P(("dp", "stream")),
            P(("dp", "stream"), None),
            P(("dp", "stream")),
            P(),
            P(),
            P(),
        ),
        check_vma=False,
    )
```
